32 devices in a mesh: dp: 8 (over z, x), tensor: 4 (over y, core).
Axes of the slice: x: 2, y: 2, z: 4, core: 2. Of those that a mesh axis runs over, the one named last changes fastest.
Arguments:
- clips: bfloat16 [16, 512, 1280], P('dp', 'tensor'), may hold values from -6 to 6
- lengths: int32 [16], P('dp'), may hold values from 1 to 512, 6144 in all
- norm1_gain: bfloat16 [1280], P('dp'), may hold values from 0.25 to 1.75
- norm1_bias: bfloat16 [1280], P('dp'), may hold values from -2 to 2
- w_query: bfloat16 [1280, 1280], P('dp', 'tensor'), may hold values from -0.25 to 0.25
- bias_query: bfloat16 [1280], P('tensor'), may hold values from -3 to 3
- w_key: bfloat16 [1280, 1280], P('dp', 'tensor'), may hold values from -0.15625 to 0.15625
- w_value: bfloat16 [1280, 1280], P('dp', 'tensor'), may hold values from -0.15625 to 0.15625
- bias_value: bfloat16 [1280], P('tensor'), may hold values from -3 to 3
- w_out: bfloat16 [1280, 1280], P('tensor', 'dp'), may hold values from -1.25 to 1.25
- bias_out: bfloat16 [1280], P('dp'), may hold values from -3 to 3
- norm2_gain: bfloat16 [1280], P('dp'), may hold values from 0.25 to 1.75
- norm2_bias: bfloat16 [1280], P('dp'), may hold values from -2 to 2
- w_up: bfloat16 [1280, 5120], P('dp', 'tensor'), may hold values from -0.15625 to 0.15625
- bias_up: bfloat16 [5120], P('tensor'), may hold values from -3 to 3
- w_down: bfloat16 [5120, 1280], P('tensor', 'dp'), may hold values from -0.078125 to 0.078125
- bias_down: bfloat16 [1280], P('dp'), may hold values from -3 to 3
- cotangent: bfloat16 [16, 512, 1280], P('dp', 'tensor'), may hold values from -6 to 6
Outputs:
- output: bfloat16 [16, 512, 1280], P('dp', 'tensor')
- clip_grad: float32 [16, 512, 1280], P('dp', 'tensor')
- norm1_gain_grad: float32 [1280], P('dp')
- norm1_bias_grad: float32 [1280], P('dp')
- w_query_grad: float32 [1280, 1280], P('dp', 'tensor')
- bias_query_grad: float32 [1280], P('tensor')
- w_key_grad: float32 [1280, 1280], P('dp', 'tensor')
- w_value_grad: float32 [1280, 1280], P('dp', 'tensor')
- bias_value_grad: float32 [1280], P('tensor')
- w_out_grad: float32 [1280, 1280], P('tensor', 'dp')
- bias_out_grad: float32 [1280], P('dp')
- norm2_gain_grad: float32 [1280], P('dp')
- norm2_bias_grad: float32 [1280], P('dp')
- w_up_grad: float32 [1280, 5120], P('dp', 'tensor')
- bias_up_grad: float32 [5120], P('tensor')
- w_down_grad: float32 [5120, 1280], P('tensor', 'dp')
- bias_down_grad: float32 [1280], P('dp')
The draws below stay inside these ranges and needn't reach their ends.
Inputs may be any that keep to these rules, and one draw needn't show every extreme that they name: `lengths`: positions of a clip at or beyond its length are padding, whose keys are masked.
All inputs are finite; a program needn't handle non-finite values. No bound on the sum of `lengths` on one device may be relied on, other than what follows from the above.
Results may differ from the reference program's by a relative error of at most 0.014.
Values may be sent and summed in bfloat16 or wider, within the bound.
No kernel may reach another device: no remote copies, remote signals or barrier semaphores. Data moves between devices by JAX's collectives and lax.ppermute only.
A program may use at most 192 MiB of HBM per device.

```python
import math
import jax
import jax.numpy as jnp
import numpy as np
from jax import lax

D = 1280
HEADS = 16
HEAD_DIM = 80
FF = 5120
CLIP_LEN = 512
CLIPS = 16


def spiked(array, stream_key, source, target, parts, factor):
    def block_of(position):
        return (jnp.arange(array.shape[position]) // (array.shape[position] // parts)).reshape((-1,) + (1,) * (array.ndim - 1 - position))

    near = jax.random.permutation(stream_key, parts)[block_of(target)]
    second = (block_of(target) + parts // 2) % parts
    return jnp.where((block_of(source) == near) | (block_of(source) == second), factor * array, array)


def level_of(stream_key, extent, pieces, smallest, top_value):
    def one(dim, shards_of):
        steps = jax.random.uniform(jax.random.fold_in(jax.random.fold_in(stream_key, 6), dim), (shards_of,), jnp.float32, smallest / len(pieces), top_value / len(pieces))
        return jnp.repeat(jnp.exp(steps), extent[dim] // shards_of).reshape((-1,) + (1,) * (len(extent) - dim - 1))

    factor_of = one(*pieces[0])
    for cut in pieces[1:]:
        factor_of = factor_of * one(*cut)
    return factor_of


def profile(count, total, reach, skew):
    weights = [(1 << 20) // math.isqrt(rank ** skew) + 1 for rank in range(2, count + 1)]
    spare, counts = total - reach - (count - 1), [1] * (count - 1)
    while spare > 0:
        movable = [i for i in range(count - 1) if counts[i] < reach]
        pool, left = sum([weights[i] for i in movable]), spare
        for i in movable:
            addition = min(reach - counts[i], max(1, left * weights[i] // pool), spare)
            counts[i] = counts[i] + addition
            spare = spare - addition
    return np.array([reach] + counts)


def uneven(own_key, amount, total, bound, slope):
    if amount == 2:
        one = jax.random.randint(own_key, (), max(1, total - bound), min(bound, total - 1) + 1)
        return jnp.stack([one, total - one])
    sizes = jnp.asarray(profile(amount, total, bound, slope), jnp.int32)
    twos = (amount - 1) // 2
    giver, receiver = sizes[1:1 + 2 * twos:2], sizes[2:2 + 2 * twos:2]
    room = jnp.minimum(giver - 1, bound - receiver)
    shifted = jax.random.randint(jax.random.fold_in(own_key, 1), (twos,), 0, 1 << 20) % (room + 1)
    sizes = sizes.at[1:1 + 2 * twos:2].set(giver - shifted).at[2:2 + 2 * twos:2].set(receiver + shifted)
    return sizes[jax.random.permutation(jax.random.fold_in(own_key, 2), amount)]


def scatter_about(rng, shape, width, most, pieces=(), dtype=jnp.bfloat16):
    array = jax.random.normal(rng, shape, jnp.float32) * width
    if len(pieces) > 0:
        array = level_of(rng, shape, pieces, -0.22, 0.18) * array
    return jnp.clip(array, min=-most, max=most).astype(dtype)


def noise_with(own_key, extent, width, limit, split, heavy, held_as=jnp.bfloat16):
    entries = width * jax.random.normal(own_key, extent, jnp.float32)
    if split:
        entries = entries * level_of(own_key, extent, split, -0.22, 0.18)
    return jnp.clip(spiked(entries, jax.random.fold_in(own_key, 3), *heavy), -limit, limit).astype(held_as)


def setup_inputs(seed: int = 0) -> dict:
    key_of = jax.random.split(jax.random.key(seed), 19)
    clips = noise_with(key_of[0], (CLIPS, CLIP_LEN, D), 1.0, 6.0, ((0, 8), (1, 4)), (0, 2, 8, 2.0))
    lengths = uneven(key_of[1], CLIPS, CLIPS * CLIP_LEN * 3 // 4, CLIP_LEN, 2).astype(jnp.int32)
    norm1_gain = jnp.clip(1.0 + 0.15 * jax.random.normal(key_of[2], (D,), jnp.float32), 0.25, 1.75).astype(jnp.bfloat16)
    norm1_bias = scatter_about(key_of[3], (D,), 0.3, 2.0, ((0, 8),))
    w_query = scatter_about(key_of[4], (D, D), (D // 2) ** -0.5, 0.25, ((0, 8), (1, 4)))
    bias_query = scatter_about(key_of[5], (D,), 0.5, 3.0, ((0, 4),))
    w_key = scatter_about(key_of[6], (D, D), D ** -0.5, 0.15625, ((0, 8), (1, 4)))
    w_value = scatter_about(key_of[7], (D, D), D ** -0.5, 0.15625, ((0, 8), (1, 4)))
    bias_value = scatter_about(key_of[8], (D,), 0.5, 3.0, ((0, 4),))
    w_out = scatter_about(key_of[9], (D, D), (D * 8 // CLIP_LEN) ** -0.5, 1.25, ((0, 4), (1, 8)))
    bias_out = scatter_about(key_of[10], (D,), 0.5, 3.0, ((0, 8),))
    norm2_gain = jnp.clip(1.0 + 0.15 * jax.random.normal(key_of[11], (D,), jnp.float32), 0.25, 1.75).astype(jnp.bfloat16)
    norm2_bias = scatter_about(key_of[12], (D,), 0.3, 2.0, ((0, 8),))
    w_up = scatter_about(key_of[13], (D, FF), D ** -0.5, 0.15625, ((0, 8), (1, 4)))
    bias_up = scatter_about(key_of[14], (FF,), 0.5, 3.0, ((0, 4),))
    w_down = scatter_about(key_of[15], (FF, D), FF ** -0.5, 0.078125, ((0, 4), (1, 8)))
    bias_down = scatter_about(key_of[16], (D,), 0.5, 3.0, ((0, 8),))
    cotangent = noise_with(key_of[17], (CLIPS, CLIP_LEN, D), 1.0, 6.0, ((0, 8), (1, 4)), (0, 2, 8, 2.0))
    return dict(clips=clips, lengths=lengths, norm1_gain=norm1_gain, norm1_bias=norm1_bias, w_query=w_query, bias_query=bias_query, w_key=w_key, w_value=w_value, bias_value=bias_value, w_out=w_out, bias_out=bias_out, norm2_gain=norm2_gain, norm2_bias=norm2_bias, w_up=w_up, bias_up=bias_up, w_down=w_down, bias_down=bias_down, cotangent=cotangent)


@jax.custom_vjp
def low(v):
    return lax.optimization_barrier(v.astype(jnp.bfloat16)).astype(jnp.float32)

@jax.custom_vjp
def low_back(v):
    return v

def low_keep(v):
    return (low(v), None)

def low_pass(kept, grad):
    return (grad,)

def back_keep(v):
    return (v, None)

def back_low(kept, grad):
    return (low(grad),)
low.defvjp(low_keep, low_pass)
low_back.defvjp(back_keep, back_low)
norm_eps = 1e-05

def layer_norm(values, gain, shift):
    center = values - lax.optimization_barrier(jnp.mean(values, axis=-1, keepdims=True))
    spread = lax.optimization_barrier(jnp.mean(center * center, axis=-1, keepdims=True))
    return center * lax.rsqrt(spread + norm_eps) * gain + shift

def product(left, right):
    return jnp.dot(left, right, precision=lax.Precision.HIGHEST)

def clip_forward(params, rows, length):
    gain_one, shift_one, w_query, bias_query, w_key, w_value, bias_value, w_out, bias_out, gain_two, shift_two, w_up, bias_up, w_down, bias_down = params
    normed_one = low(layer_norm(rows, gain_one, shift_one))
    shape = (CLIP_LEN, HEADS, HEAD_DIM)
    query = low_back(low(product(normed_one, w_query) + bias_query)).reshape(shape)
    keys = low_back(low(product(normed_one, w_key))).reshape(shape)
    values = low_back(low(product(normed_one, w_value) + bias_value)).reshape(shape)
    scores = jnp.einsum('ihd,jhd->hij', query, keys, precision=lax.Precision.HIGHEST) * HEAD_DIM ** (-0.5)
    visible = lax.iota(jnp.int32, CLIP_LEN) < length
    scores = low_back(jnp.where(visible[None, None, :], scores, -1000000000.0))
    probs = low(jax.nn.softmax(scores, axis=-1))
    mixed = jnp.einsum('hij,jhd->ihd', probs, values, precision=lax.Precision.HIGHEST).reshape(CLIP_LEN, D)
    mixed = low_back(low(mixed))
    inner = rows + low_back(product(mixed, w_out) + bias_out)
    normed_two = low(layer_norm(inner, gain_two, shift_two))
    hidden_pre = low_back(product(normed_two, w_up) + bias_up)
    hidden = low(jax.nn.gelu(hidden_pre, approximate=False))
    return inner + low_back(product(hidden, w_down) + bias_down)

def reference(clips, lengths, norm1_gain, norm1_bias, w_query, bias_query, w_key, w_value, bias_value, w_out, bias_out, norm2_gain, norm2_bias, w_up, bias_up, w_down, bias_down, cotangent):
    params = tuple((item.astype(jnp.float32) for item in (norm1_gain, norm1_bias, w_query, bias_query, w_key, w_value, bias_value, w_out, bias_out, norm2_gain, norm2_bias, w_up, bias_up, w_down, bias_down)))

    def one_clip(carry, item):
        rows, length, grad_top = item

        def forward(rows_in, params_in):
            return clip_forward(params_in, rows_in, length)
        result, pull = jax.vjp(forward, rows.astype(jnp.float32), params)
        grad_rows, grad_params = pull(grad_top.astype(jnp.float32))
        carry = jax.tree.map(jnp.add, carry, grad_params)
        return (carry, (result.astype(jnp.bfloat16), grad_rows))
    zeros = tuple((jnp.zeros_like(item) for item in params))
    grads, (output, clip_grad) = lax.scan(one_clip, zeros, (clips, lengths, cotangent))
    return (output, clip_grad, grads[0], grads[1], grads[2], grads[3], grads[4], grads[5], grads[6], grads[7], grads[8], grads[9], grads[10], grads[11], grads[12], grads[13], grads[14])
```

```python
import jax
import jax.numpy as jnp
from jax import lax
from jax.sharding import PartitionSpec as P

HEAD_DIM = 80
norm_eps = 1e-05
VEC_ROWS = 16


def low(values):
    return values.astype(jnp.bfloat16)


def wide(values):
    return values.astype(jnp.float32)


def mm(left, right):
    return jnp.dot(left, right, preferred_element_type=jnp.float32)


def mm_left(left, right):
    return lax.dot_general(left, right, (((0,), (0,)), ((), ())), preferred_element_type=jnp.float32)


def mm_right(left, right):
    return lax.dot_general(left, right, (((1,), (1,)), ((), ())), preferred_element_type=jnp.float32)


def norm_parts(values):
    center = values - jnp.mean(values, axis=-1, keepdims=True)
    spread = jnp.mean(center * center, axis=-1, keepdims=True)
    inverse = lax.rsqrt(spread + norm_eps)
    return center * inverse, inverse


def norm_back(grad, xhat, inverse, gain):
    scaled = grad * gain
    first = jnp.mean(scaled, axis=-1, keepdims=True)
    second = jnp.mean(scaled * xhat, axis=-1, keepdims=True)
    return (scaled - first - xhat * second) * inverse


def gelu_pair(pre):
    half = 0.5 * (1.0 + lax.erf(pre * (0.5 ** 0.5)))
    slope = half + pre * jnp.exp(-0.5 * pre * pre) * 0.3989422804014327
    return pre * half, slope


def tensor_swap(values, mask):
    size = lax.axis_size("tensor")
    return lax.ppermute(values, "tensor", [(i, i ^ mask) for i in range(size)])


def data_swap(values, mask):
    size = lax.axis_size("dp")
    return lax.ppermute(values, "dp", [(i, i ^ mask) for i in range(size)])


def masks_of(size):
    masks = []
    while size > 1:
        size //= 2
        masks.append(size)
    return masks


def gather_blocks(shard):
    size = lax.axis_size("dp")
    held = shard[None]
    order = [0]
    for mask in masks_of(size):
        held = jnp.concatenate([held, data_swap(held, mask)], axis=0)
        order = order + [item ^ mask for item in order]
    place = [0] * size
    for position, item in enumerate(order):
        place[item] = position
    me = lax.axis_index("dp")
    table = jnp.asarray(place, jnp.int32)
    return jnp.concatenate([lax.dynamic_slice_in_dim(held, table[me ^ item], 1, axis=0) for item in range(size)], axis=0)


def scatter_blocks(blocks):
    size = lax.axis_size("dp")
    me = lax.axis_index("dp")
    held = blocks
    for mask in reversed(masks_of(size)):
        pairs = held.reshape((held.shape[0] // 2, 2) + held.shape[1:])
        bit = (me // mask) % 2
        keep = lax.dynamic_index_in_dim(pairs, bit, axis=1, keepdims=False)
        send = lax.dynamic_index_in_dim(pairs, 1 - bit, axis=1, keepdims=False)
        held = low(wide(keep) + wide(data_swap(send, mask)))
    return held[0]


def heads_of(joined, width, index):
    tokens = joined.shape[0]
    part = joined[:, index * width : (index + 1) * width]
    return part.reshape(tokens, width // HEAD_DIM, HEAD_DIM)


def attend(query, keys, values, visible):
    scale = HEAD_DIM ** (-0.5)
    scores = jnp.einsum("ihd,jhd->hij", query, keys, preferred_element_type=jnp.float32) * scale
    scores = jnp.where(visible[None, None, :], scores, -1000000000.0)
    top = jnp.max(scores, axis=-1, keepdims=True)
    expo = jnp.exp(scores - top)
    total = jnp.sum(expo, axis=-1, keepdims=True)
    probs = low(expo / total)
    mixed = jnp.einsum("hij,jhd->ihd", probs, values, preferred_element_type=jnp.float32)
    return low(mixed.reshape(mixed.shape[0], -1)), top + jnp.log(total)


def attend_back(query, keys, values, visible, log_total, grad_mixed):
    scale = HEAD_DIM ** (-0.5)
    tokens = query.shape[0]
    scores = jnp.einsum("ihd,jhd->hij", query, keys, preferred_element_type=jnp.float32) * scale
    scores = jnp.where(visible[None, None, :], scores, -1000000000.0)
    probs = jnp.exp(scores - log_total)
    grad_heads = grad_mixed.reshape(query.shape)
    grad_probs = jnp.einsum("ihd,jhd->hij", grad_heads, values, preferred_element_type=jnp.float32)
    delta = jnp.sum(grad_probs * probs, axis=-1, keepdims=True)
    grad_scores = low(probs * (grad_probs - delta))
    grad_query = jnp.einsum("hij,jhd->ihd", grad_scores, keys, preferred_element_type=jnp.float32) * scale
    grad_keys = jnp.einsum("hij,ihd->jhd", grad_scores, query, preferred_element_type=jnp.float32) * scale
    grad_values = jnp.einsum("hij,ihd->jhd", low(probs), grad_heads, preferred_element_type=jnp.float32)
    parts = [item.reshape(tokens, -1) for item in (grad_query, grad_keys, grad_values)]
    return low(jnp.concatenate(parts, axis=1))


def pick(pair, index):
    return lax.dynamic_index_in_dim(pair, index, axis=0, keepdims=False)


def order_pair(mine, other, core):
    return jnp.where(core == 0, jnp.stack([mine, other]), jnp.stack([other, mine]))


def shards(
    clips,
    lengths,
    norm1_gain,
    norm1_bias,
    w_query,
    bias_query,
    w_key,
    w_value,
    bias_value,
    w_out,
    bias_out,
    norm2_gain,
    norm2_bias,
    w_up,
    bias_up,
    w_down,
    bias_down,
    cotangent,
):
    rows = clips.shape[1]
    model = clips.shape[2]
    depth, width = w_query.shape
    hidden_width = w_up.shape[1]
    half_hidden = hidden_width // 2
    data_size = lax.axis_size("dp")
    place = lax.axis_index("tensor")
    core = place % 2

    vectors = jnp.stack([norm1_gain, norm1_bias, bias_out, norm2_gain, norm2_bias, bias_down])
    vectors = jnp.pad(vectors, ((0, VEC_ROWS - 6), (0, model - depth)))
    attn_shard = jnp.concatenate([w_query, w_key, w_value, w_out.T], axis=1)
    attn_shard = jnp.concatenate([attn_shard, vectors], axis=0)
    down_t = w_down.T
    ff_shards = [
        jnp.concatenate([w_up[:, k * half_hidden : (k + 1) * half_hidden], down_t[:, k * half_hidden : (k + 1) * half_hidden]], axis=1)
        for k in range(2)
    ]

    local_bias = jnp.zeros((VEC_ROWS, model), jnp.bfloat16)
    local_bias = local_bias.at[0, :hidden_width].set(bias_up)
    local_bias = local_bias.at[1, : 2 * width].set(jnp.concatenate([bias_query, bias_value]))
    sent = jnp.concatenate([pick(clips, 1 - core), pick(cotangent, 1 - core), local_bias], axis=0)
    got = tensor_swap(sent, 1)
    half_rows = jnp.concatenate([pick(clips, core), got[:rows], pick(cotangent, core), got[rows : 2 * rows]], axis=0)
    sib_bias = got[2 * rows :]
    other_half = tensor_swap(half_rows, 2)
    low_rows = jnp.concatenate([half_rows[: 2 * rows], other_half[: 2 * rows]], axis=0)
    cot = jnp.concatenate([half_rows[2 * rows :], other_half[2 * rows :]], axis=0)
    cot_wide = wide(cot)
    x = wide(low_rows)
    length = pick(lengths, core)
    block = place ^ lax.iota(jnp.int32, 4)
    position = (block[:, None] * rows + lax.iota(jnp.int32, rows)[None, :]).reshape(-1)
    visible = position < length

    attn_all = gather_blocks(attn_shard)
    attn_own = attn_all[:, :depth].reshape(model, model)
    vectors_full = wide(attn_all[:, depth : depth + 6, :depth].transpose(1, 0, 2).reshape(6, model))
    gain_one, shift_one, out_bias, gain_two, shift_two, down_bias = [vectors_full[k] for k in range(6)]
    attn_sib = tensor_swap(attn_own, 1)
    attn_w = (attn_own, attn_sib)
    ff_own = [gather_blocks(item).reshape(model, model) for item in ff_shards]
    ff_sib = [tensor_swap(item, 1) for item in ff_own]

    xhat_one, inverse_one = norm_parts(x)
    normed_one = low(xhat_one * gain_one + shift_one)
    biases = (local_bias, sib_bias)
    saved = []
    partial_out = None
    for k in range(2):
        bias_row = wide(biases[k][1])
        bias_joined = jnp.concatenate([bias_row[:width], jnp.zeros((width,), jnp.float32), bias_row[width : 2 * width]])
        joined = low(mm(normed_one, attn_w[k][:, : 3 * width]) + bias_joined)
        query, keys, values = [heads_of(joined, width, i) for i in range(3)]
        mixed, log_total = attend(query, keys, values, visible)
        saved.append((query, keys, values, mixed, log_total))
        term = mm_right(mixed, attn_w[k][:, 3 * width :])
        partial_out = term if partial_out is None else partial_out + term

    def both_halves(partial):
        first = tensor_swap(low(partial[2 * rows :]), 2)
        second = tensor_swap(low(partial[: 2 * rows]), 2)
        return partial + wide(jnp.concatenate([first, second], axis=0))

    def own_half(partial):
        return partial[: 2 * rows] + wide(tensor_swap(low(partial[2 * rows :]), 2))

    inner = x + (both_halves(partial_out) + out_bias)
    xhat_two, inverse_two = norm_parts(inner)
    normed_two = low(xhat_two * gain_two + shift_two)

    branch_two = None
    grad_two = None
    ff_grads = []
    bias_up_terms = [[], []]
    for k in range(2):
        sums = []
        for side, weights in enumerate((ff_own[k], ff_sib[k])):
            up, down = weights[:, :half_hidden], weights[:, half_hidden:]
            bias = wide(biases[side][0, k * half_hidden : (k + 1) * half_hidden])
            pre = mm(normed_two, up) + bias
            act, slope = gelu_pair(pre)
            hidden = low(act)
            term = mm_right(hidden, down)
            branch_two = term if branch_two is None else branch_two + term
            grad_pre = low(mm(cot, down) * slope)
            term = mm_right(grad_pre, up)
            grad_two = term if grad_two is None else grad_two + term
            bias_up_terms[side].append(jnp.sum(wide(grad_pre), axis=0))
            sums.append(jnp.concatenate([mm_left(normed_two, grad_pre), mm_left(cot, hidden)], axis=1))
        ff_grads.append(low(sums[0] + wide(tensor_swap(low(sums[1]), 1))))

    out_half = inner[: 2 * rows] + (own_half(branch_two) + down_bias)
    out_low = low(out_half)
    output = order_pair(out_low[:rows], tensor_swap(out_low[rows:], 1), core)

    ff_shard_grads = [wide(scatter_blocks(item.reshape(data_size, depth, model))) for item in ff_grads]

    grad_normed_two = both_halves(grad_two)
    grad_inner = cot_wide + norm_back(grad_normed_two, xhat_two, inverse_two, gain_two)
    grad_branch = low(grad_inner)
    own = slice(0, 2 * rows)
    v_gain_two = jnp.sum(grad_normed_two[own] * xhat_two[own], axis=0)
    v_shift_two = jnp.sum(grad_normed_two[own], axis=0)
    v_bias_out = jnp.sum(wide(grad_branch[own]), axis=0)
    v_bias_down = jnp.sum(cot_wide[own], axis=0)

    grad_one = None
    attn_grads = []
    bias_terms = []
    for k in range(2):
        query, keys, values, mixed, log_total = saved[k]
        grad_mixed = low(mm(grad_branch, attn_w[k][:, 3 * width :]))
        grad_qkv = attend_back(query, keys, values, visible, log_total, grad_mixed)
        term = mm_right(grad_qkv, attn_w[k][:, : 3 * width])
        grad_one = term if grad_one is None else grad_one + term
        sums = jnp.sum(wide(grad_qkv), axis=0)
        bias_terms.append(jnp.concatenate([sums[:width], sums[2 * width :]] + bias_up_terms[k]))
        attn_grads.append(jnp.concatenate([mm_left(normed_one, grad_qkv), mm_left(grad_branch, mixed)], axis=1))
    attn_grad = low(attn_grads[0] + wide(tensor_swap(low(attn_grads[1]), 1)))
    attn_shard_grad = wide(scatter_blocks(attn_grad.reshape(data_size, depth, model)))

    grad_normed_one = own_half(grad_one)
    v_gain_one = jnp.sum(grad_normed_one * xhat_one[own], axis=0)
    v_shift_one = jnp.sum(grad_normed_one, axis=0)
    clip_half = grad_inner[own] + norm_back(grad_normed_one, xhat_one[own], inverse_one[own], gain_one)
    clip_grad = order_pair(clip_half[:rows], tensor_swap(clip_half[rows:], 1), core)

    bias_total = bias_terms[0] + tensor_swap(bias_terms[1], 1)
    bias_total = lax.psum(bias_total, "dp")
    vector_total = jnp.stack([v_gain_one, v_shift_one, v_bias_out, v_gain_two, v_shift_two, v_bias_down])
    vector_total = lax.psum(vector_total, ("dp", "tensor"))
    vector_own = lax.dynamic_slice_in_dim(vector_total, lax.axis_index("dp") * depth, depth, axis=1)

    w_out_grad = attn_shard_grad[:, 3 * width :].T
    w_up_grad = jnp.concatenate([item[:, :half_hidden] for item in ff_shard_grads], axis=1)
    w_down_grad = jnp.concatenate([item[:, half_hidden:] for item in ff_shard_grads], axis=1).T
    return (
        output,
        clip_grad,
        vector_own[0],
        vector_own[1],
        attn_shard_grad[:, :width],
        bias_total[:width],
        attn_shard_grad[:, width : 2 * width],
        attn_shard_grad[:, 2 * width : 3 * width],
        bias_total[width : 2 * width],
        w_out_grad,
        vector_own[2],
        vector_own[3],
        vector_own[4],
        w_up_grad,
        bias_total[2 * width :],
        w_down_grad,
        vector_own[5],
    )


def solution(mesh):
    rows_spec = P("dp", "tensor", None)
    data, tensor = P("dp"), P("tensor")
    wide_spec, tall_spec = P("dp", "tensor"), P("tensor", "dp")
    placed = (
        rows_spec,
        data,
        data,
        data,
        wide_spec,
        tensor,
        wide_spec,
        wide_spec,
        tensor,
        tall_spec,
        data,
        data,
        data,
        wide_spec,
        tensor,
        tall_spec,
        data,
        rows_spec,
    )
    outs = (
        rows_spec,
        rows_spec,
        data,
        data,
        wide_spec,
        tensor,
        wide_spec,
        wide_spec,
        tensor,
        tall_spec,
        data,
        data,
        data,
        wide_spec,
        tensor,
        tall_spec,
        data,
    )
    return jax.shard_map(shards, mesh=mesh, in_specs=placed, out_specs=outs, check_vma=False)
```

```python
import jax
import jax.numpy as jnp
from jax import lax
from jax.experimental import pallas as pl
from jax.experimental.pallas import tpu as pltpu
from jax.sharding import PartitionSpec as P

HEAD_DIM = 80
norm_eps = 1e-05
VEC_ROWS = 8
TILE = 256
FIRST_TILES = 3


def low(values):
    return values.astype(jnp.bfloat16)


def wide(values):
    return values.astype(jnp.float32)


def mm(left, right):
    return jnp.dot(left, right, preferred_element_type=jnp.float32)


def mm_left(left, right):
    return lax.dot_general(left, right, (((0,), (0,)), ((), ())), preferred_element_type=jnp.float32)


def mm_right(left, right):
    return lax.dot_general(left, right, (((1,), (1,)), ((), ())), preferred_element_type=jnp.float32)


def norm_parts(values):
    center = values - jnp.mean(values, axis=-1, keepdims=True)
    spread = jnp.mean(center * center, axis=-1, keepdims=True)
    inverse = lax.rsqrt(spread + norm_eps)
    return center * inverse, inverse


def norm_back(grad, xhat, inverse, gain):
    scaled = grad * gain
    first = jnp.mean(scaled, axis=-1, keepdims=True)
    second = jnp.mean(scaled * xhat, axis=-1, keepdims=True)
    return (scaled - first - xhat * second) * inverse


def gelu_pair(pre):
    half = 0.5 * (1.0 + lax.erf(pre * (0.5 ** 0.5)))
    slope = half + pre * jnp.exp(-0.5 * pre * pre) * 0.3989422804014327
    return pre * half, slope


def tensor_swap(values, mask):
    size = lax.axis_size("tensor")
    return lax.ppermute(values, "tensor", [(i, i ^ mask) for i in range(size)])


def data_swap(values, mask):
    size = lax.axis_size("dp")
    return lax.ppermute(values, "dp", [(i, i ^ mask) for i in range(size)])


def masks_of(size):
    masks = []
    while size > 1:
        size //= 2
        masks.append(size)
    return masks


def pin(values, *others):
    return lax.optimization_barrier((values, others))[0]


def after(values, *others):
    return pin(values, *others) if others else values


class Gather:
    def __init__(self, halves):
        self.masks = masks_of(lax.axis_size("dp"))
        self.held = [item[None] for item in halves]
        self.fresh = [None, None]
        self.order = [[0], [0]]
        self.step = 0

    def mask(self, side):
        count = len(self.masks)
        if side == 1 and self.step >= count - 2:
            return self.masks[2 * count - 3 - self.step]
        return self.masks[self.step]

    def advance(self, *others):
        for side in range(2):
            if self.fresh[side] is not None:
                self.held[side] = jnp.concatenate([self.held[side], self.fresh[side]], axis=0)
            mask = self.mask(side)
            self.fresh[side] = data_swap(after(self.held[side], *others), mask)
            self.order[side] = self.order[side] + [item ^ mask for item in self.order[side]]
        self.step += 1
        return tuple(self.fresh)

    def early(self, *others):
        got = ()
        while self.step < len(self.masks) - 2:
            got = self.advance(*others)
        return got


def vmem(count):
    return [pl.BlockSpec(memory_space=pltpu.VMEM)] * count


def settle(*items):
    gathers = [item for item in items if isinstance(item, Gather)]
    others = [item for item in items if not isinstance(item, Gather)]
    arrays = [(item.held, item.fresh) for item in gathers]
    arrays, others = lax.optimization_barrier((arrays, others))
    for item, (held, fresh) in zip(gathers, arrays):
        item.held, item.fresh = list(held), list(fresh)
    return others


def place_body(gathered, depth, extra, joined, me_ref, *refs):
    pieces, outs, sems = refs[:4], refs[4:-1], refs[-1]
    me = me_ref[0]
    copies = []
    for side in range(2):
        held, fresh = pieces[2 * side : 2 * side + 2]
        columns = held.shape[2]
        for position, item in enumerate(gathered.order[side]):
            count = held.shape[0]
            piece, row = (held, position) if position < count else (fresh, position - count)
            if joined:
                target = outs[0].at[me ^ item, pl.ds(0, depth), pl.ds(side * columns, columns)]
            else:
                target = outs[side].at[me ^ item]
            source = piece.at[row, pl.ds(0, depth)] if extra else piece.at[row]
            copies.append(pltpu.make_async_copy(source, target, sems.at[len(copies)]))
            if extra and side == 0:
                source = piece.at[row, pl.ds(depth, extra)]
                copies.append(pltpu.make_async_copy(source, outs[-1].at[me ^ item], sems.at[len(copies)]))
    for item in copies:
        item.start()
    for item in copies:
        item.wait()


def place_blocks(gathered, depth, extra=0, joined=False):
    size = lax.axis_size("dp")
    pieces = [gathered.held[0], gathered.fresh[0], gathered.held[1], gathered.fresh[1]]
    columns = pieces[0].shape[2]
    if extra and depth % 8:
        whole = place_blocks(gathered, depth + extra, 0, joined)
        return [item[:, :depth] for item in whole] + [whole[0][:, depth:, :columns]]
    me = lax.axis_index("dp").reshape(1)
    main = jax.ShapeDtypeStruct((size, depth, (2 if joined else 1) * columns), jnp.bfloat16)
    shapes = [main] if joined else [main, main]
    if extra:
        shapes.append(jax.ShapeDtypeStruct((size, extra, columns), jnp.bfloat16))
    return pl.pallas_call(
        lambda *refs: place_body(gathered, depth, extra, joined, *refs),
        in_specs=[pl.BlockSpec(memory_space=pltpu.SMEM)] + [pl.BlockSpec(memory_space=pl.ANY)] * 4,
        out_specs=vmem(len(shapes)),
        out_shape=shapes,
        compiler_params=pltpu.CompilerParams(vmem_limit_bytes=16 << 20),
        scratch_shapes=[pltpu.SemaphoreType.DMA((3 * size if extra else 2 * size,))],
        cost_estimate=pl.CostEstimate(flops=1024, bytes_accessed=1024, transcendentals=0),
        name="place",
    )(me, *pieces)


class Scatter:
    def __init__(self, own, other):
        size = lax.axis_size("dp")
        self.bits = size.bit_length() - 1
        shape = (2,) * self.bits + (own[0].shape[0] // size, own[0].shape[1])
        self.terms = [[own[side].reshape(shape), other[side].reshape(shape)] for side in range(2)]
        self.axes = [list(range(self.bits)) for side in range(2)]
        masks = masks_of(size)[::-1]
        self.masks = [masks, [masks[1], masks[0]] + masks[2:]]
        self.step = 0

    def part(self, side, index):
        total = None
        for term in self.terms[side]:
            item = wide(lax.dynamic_index_in_dim(term, index, axis=self.where, keepdims=False))
            total = item if total is None else total + item
        return total

    def advance(self, *others):
        me = lax.axis_index("dp")
        sends, kept, masks = [], [], []
        for side in range(2):
            mask = self.masks[side][self.step]
            number = self.bits - mask.bit_length()
            self.where = self.axes[side].index(number)
            bit = (me // mask) % 2
            sends.append(low(self.part(side, 1 - bit)))
            kept.append(self.part(side, bit))
            self.axes[side].remove(number)
            masks.append(mask)
        sends = after(sends, *others)
        self.terms = [[keep, data_swap(send, mask)] for keep, send, mask in zip(kept, sends, masks)]
        self.step += 1

    def finish(self):
        return [wide(item[0]) + wide(item[1]) for item in self.terms]

    def rest(self):
        while self.step < self.bits:
            self.advance()


def settle_scatters(scatters, *others):
    gots = [[item.terms[side][1] for side in range(2)] for item in scatters]
    gots, others = lax.optimization_barrier((gots, others))
    for item, got in zip(scatters, gots):
        for side in range(2):
            item.terms[side][1] = got[side]
    return others


def ff_body(first, tiles, half, *refs):
    n2, cot, n2t, cott, own_up, own_down, sib_up, sib_down, own_b, sib_b = refs[:10]
    refs = refs[10:]
    if not first:
        prev_b, prev_g = refs[:2]
        refs = refs[2:]
    if first:
        acc_b, acc_g = refs[:2]
        own_gu, own_gd, sib_gu, sib_gd, b_own, b_sib = refs[2:]
    else:
        out_keep, out_send, grad_keep, grad_one, grad_two, *refs = refs
        own_gu, own_gd, sib_gu, sib_gd, b_own, b_sib, acc_b, acc_g = refs
    side, tile = pl.program_id(0), pl.program_id(1)

    @pl.when((side == 0) & (tile == 0))
    def _():
        if first:
            acc_b[...] = jnp.zeros_like(acc_b)
            acc_g[...] = jnp.zeros_like(acc_g)
        else:
            acc_b[...] = prev_b[...]
            acc_g[...] = prev_g[...]

    def step(up_ref, down_ref, bias, up_grad, down_grad, bias_sum):
        up, down = up_ref[...], down_ref[...]
        pre = mm(n2[...], up) + wide(bias[...])
        act, slope = gelu_pair(pre)
        hidden = low(act)
        grad_pre = low(mm(cot[...], down) * slope)
        acc_b[...] += mm_right(hidden, down)
        acc_g[...] += mm_right(grad_pre, up)
        up_grad[...] = low(mm(n2t[...], grad_pre))
        down_grad[...] = low(mm(cott[...], hidden))
        bias_sum[...] = jnp.sum(wide(grad_pre), axis=0, keepdims=True)

    @pl.when(side == 0)
    def _():
        step(sib_up, sib_down, sib_b, sib_gu, sib_gd, b_sib)

    @pl.when(side == 1)
    def _():
        step(own_up, own_down, own_b, own_gu, own_gd, b_own)

    if not first:

        @pl.when((side == 1) & (tile == tiles - 1))
        def _():
            out_keep[...] = acc_b[:half]
            out_send[...] = low(acc_b[half:])
            grad_keep[...] = acc_g[...]
            grad_one[...] = low(acc_g[half:])
            grad_two[...] = low(acc_g[:half])


def prepare_body(columns, *refs):
    vectors, (w_query, w_key, w_value, w_out_t), (first, second) = refs[:6], refs[6:10], refs[10:]
    depth, width = w_query.shape
    joined = jnp.concatenate([w_query[...], w_key[...], w_value[...], w_out_t[...]], axis=1)
    first[:depth] = joined[:, :columns]
    second[:depth] = joined[:, columns:]
    first[depth:] = jnp.zeros_like(first[depth:])
    second[depth:] = jnp.zeros_like(second[depth:])
    for k, vector in enumerate(vectors):
        first[depth + k : depth + k + 1, :depth] = vector[...]


def prepare(vectors, weights):
    depth, width = weights[0].shape
    columns = 2 * width
    vectors = [item.reshape(1, depth) for item in vectors]
    return pl.pallas_call(
        lambda *refs: prepare_body(columns, *refs),
        in_specs=vmem(10),
        out_specs=vmem(2),
        out_shape=[jax.ShapeDtypeStruct((depth + VEC_ROWS, columns), jnp.bfloat16)] * 2,
        cost_estimate=pl.CostEstimate(flops=1024, bytes_accessed=1024, transcendentals=0),
        name="prepare",
    )(*vectors, *weights)


def feed_forward(n2, cot, n2t, cott, own_w, sib_w, own_b, sib_b, tile, previous=None):
    rows, model = n2.shape
    hidden = own_b.shape[1]
    tiles = hidden // tile
    first = previous is None
    half = rows // 2

    def const(shape):
        return pl.BlockSpec(shape, lambda s, i: (0, 0), pipeline_mode=pl.Buffered(1))

    def second(shape):
        return pl.BlockSpec(shape, lambda s, i: (0, jnp.where(s == 1, i, 0)))

    def initial(shape):
        return pl.BlockSpec(shape, lambda s, i: (0, jnp.where(s == 0, i, tiles - 1)))

    in_specs = [const((rows, model))] * 2 + [const((model, rows))] * 2
    in_specs += [second((model, tile))] * 2 + [initial((model, tile))] * 2 + [second((1, tile)), initial((1, tile))]
    operands = [n2, cot, n2t, cott, *own_w, *sib_w, own_b, sib_b]
    full = jax.ShapeDtypeStruct((rows, model), jnp.float32)
    grads = jax.ShapeDtypeStruct((model, hidden), jnp.bfloat16)
    sums = jax.ShapeDtypeStruct((1, hidden), jnp.float32)
    tail_shapes = [grads] * 4 + [sums, sums]
    tail_specs = [second((model, tile))] * 2 + [initial((model, tile))] * 2 + [second((1, tile)), initial((1, tile))]
    scratch = []
    if first:
        shapes = [full, full] + tail_shapes
        specs = [const((rows, model))] * 2 + tail_specs
    else:
        operands += list(previous)
        in_specs += [const((rows, model))] * 2
        shapes = [
            jax.ShapeDtypeStruct((half, model), jnp.float32),
            jax.ShapeDtypeStruct((half, model), jnp.bfloat16),
            full,
            jax.ShapeDtypeStruct((half, model), jnp.bfloat16),
            jax.ShapeDtypeStruct((half, model), jnp.bfloat16),
        ] + tail_shapes
        specs = [const((half, model))] * 2 + [const((rows, model))] + [const((half, model))] * 2 + tail_specs
        scratch = [pltpu.VMEM((rows, model), jnp.float32)] * 2
    return pl.pallas_call(
        lambda *refs: ff_body(first, tiles, half, *refs),
        grid=(2, tiles),
        in_specs=in_specs,
        out_specs=specs,
        out_shape=shapes,
        scratch_shapes=scratch,
        compiler_params=pltpu.CompilerParams(vmem_limit_bytes=56 << 20),
        cost_estimate=pl.CostEstimate(flops=1024, bytes_accessed=1024, transcendentals=0),
        name="feed_forward",
    )(*operands)


def dot_t(left, right):
    return lax.dot_general(left, right, (((0,), (0,)), ((), ())), preferred_element_type=jnp.float32)


def norm_rows(values, gain, shift):
    xhat, inverse = norm_parts(values)
    return low(xhat * gain + shift)


def attn_head(joined, head, width, mask):
    scale = HEAD_DIM ** (-0.5)
    begin = pl.multiple_of(head * HEAD_DIM, 16)
    query = joined[pl.ds(begin, HEAD_DIM), :]
    keys = joined[pl.ds(pl.multiple_of(width + begin, 16), HEAD_DIM), :]
    values = joined[pl.ds(pl.multiple_of(2 * width + begin, 16), HEAD_DIM), :]
    scores = jnp.where(mask[...] > 0.5, dot_t(keys, query) * scale, -1000000000.0)
    return begin, query, keys, values, scores


def attn_forward_body(first, width, *refs):
    if first:
        x, gain, shift, weights, bias, mask, n1, n1t, joined, mixed, totals, part = refs
        n1[...] = norm_rows(wide(x[...]), gain[...], shift[...])
        n1t[...] = n1[...].T
    else:
        n1, previous, weights, bias, mask, joined, mixed, totals, part, send_one, send_two = refs
    joined[...] = low(mm(n1[...], weights[:, : 3 * width]) + bias[...]).T

    def one(head, carry):
        begin, query, keys, values, scores = attn_head(joined, head, width, mask)
        top = jnp.max(scores, axis=0, keepdims=True)
        expo = jnp.exp(scores - top)
        total = jnp.sum(expo, axis=0, keepdims=True)
        probs = low(expo * (1.0 / total))
        mixed[pl.ds(begin, HEAD_DIM), :] = low(mm(values, probs))
        totals[pl.ds(head, 1), :] = top + jnp.log(total)
        return carry

    lax.fori_loop(0, width // HEAD_DIM, one, 0)
    term = mm_right(mixed[...].T, weights[:, 3 * width :])
    if first:
        part[...] = term
    else:
        term = previous[...] + term
        half = term.shape[0] // 2
        part[...] = term
        send_one[...] = low(term[half:])
        send_two[...] = low(term[:half])


def attn_forward(head_in, weights, bias, mask, width, first):
    rows, model = head_in[0].shape
    low_shape = lambda *shape: jax.ShapeDtypeStruct(shape, jnp.bfloat16)
    wide_shape = lambda *shape: jax.ShapeDtypeStruct(shape, jnp.float32)
    shapes = [low_shape(3 * width, rows), low_shape(width, rows), wide_shape(width // HEAD_DIM, rows), wide_shape(rows, model)]
    shapes = [low_shape(rows, model), low_shape(model, rows)] + shapes if first else shapes + [low_shape(rows // 2, model)] * 2
    operands = list(head_in) + [weights, bias, mask]
    return pl.pallas_call(
        lambda *refs: attn_forward_body(first, width, *refs),
        in_specs=vmem(len(operands)),
        out_specs=vmem(len(shapes)),
        out_shape=shapes,
        compiler_params=pltpu.CompilerParams(vmem_limit_bytes=56 << 20),
        cost_estimate=pl.CostEstimate(flops=1024, bytes_accessed=1024, transcendentals=0),
        name="attn_forward",
    )(*operands)


def attn_backward_body(first, width, half, *refs):
    gb, gbt, n1t, weights, joined, mixed, totals, mask = refs[:8]
    refs = refs[8:]
    if first:
        part, grads_one, grads_two, sums, gmt, djoined = refs
    else:
        previous, keep, send, grads_one, grads_two, sums, gmt, djoined = refs
    scale = HEAD_DIM ** (-0.5)
    gmt[...] = low(mm(gb[...], weights[:, 3 * width :])).T

    def one(head, carry):
        begin, query, keys, values, scores = attn_head(joined, head, width, mask)
        probs = jnp.exp(scores - totals[pl.ds(head, 1), :])
        gm = gmt[pl.ds(begin, HEAD_DIM), :]
        grad_probs = dot_t(values, gm)
        delta = jnp.sum(grad_probs * probs, axis=0, keepdims=True)
        grad_scores = low(probs * (grad_probs - delta))
        djoined[pl.ds(begin, HEAD_DIM), :] = low(mm(keys, grad_scores) * scale)
        djoined[pl.ds(pl.multiple_of(width + begin, 16), HEAD_DIM), :] = low(mm_right(query, grad_scores) * scale)
        djoined[pl.ds(pl.multiple_of(2 * width + begin, 16), HEAD_DIM), :] = low(mm_right(gm, low(probs)))
        return carry

    lax.fori_loop(0, width // HEAD_DIM, one, 0)
    grads_one[...] = low(mm_right(n1t[...], djoined[: 2 * width]))
    grads_two[:, :width] = low(mm_right(n1t[...], djoined[2 * width :]))
    grads_two[:, width:] = low(mm_right(gbt[...], mixed[...]))
    ones = jnp.ones((8, gb.shape[0]), jnp.bfloat16)
    sums[...] = mm_right(ones, djoined[...])
    term = mm_right(djoined[...].T, weights[:, : 3 * width])
    if first:
        part[...] = term
    else:
        term = previous[...] + term
        keep[...] = term[:half]
        send[...] = low(term[half:])


def attn_backward(gb, gbt, n1t, weights, saved, mask, width, previous=None):
    rows, model = gb.shape
    first = previous is None
    half = rows // 2
    operands = [gb, gbt, n1t, weights, *saved, mask]
    shapes = [jax.ShapeDtypeStruct((model, 2 * width), jnp.bfloat16)] * 2 + [jax.ShapeDtypeStruct((8, 3 * width), jnp.float32)]
    if first:
        shapes = [jax.ShapeDtypeStruct((rows, model), jnp.float32)] + shapes
    else:
        operands.append(previous)
        shapes = [
            jax.ShapeDtypeStruct((half, model), jnp.float32),
            jax.ShapeDtypeStruct((half, model), jnp.bfloat16),
        ] + shapes
    return pl.pallas_call(
        lambda *refs: attn_backward_body(first, width, half, *refs),
        in_specs=vmem(len(operands)),
        out_specs=vmem(len(shapes)),
        out_shape=shapes,
        scratch_shapes=[pltpu.VMEM((width, rows), jnp.bfloat16), pltpu.VMEM((3 * width, rows), jnp.bfloat16)],
        compiler_params=pltpu.CompilerParams(vmem_limit_bytes=56 << 20),
        cost_estimate=pl.CostEstimate(flops=1024, bytes_accessed=1024, transcendentals=0),
        name="attn_backward",
    )(*operands)


def middle_body(half, x, part, got_first, got_second, bias, gain, shift, inner, n2, n2t):
    for k, got in enumerate((got_first, got_second)):
        part_rows = slice(k * half, (k + 1) * half)
        value = wide(x[part_rows]) + (part[part_rows] + wide(got[...]) + bias[...])
        inner[part_rows] = value
        n2[part_rows] = norm_rows(value, gain[...], shift[...])
    n2t[...] = n2[...].T


def middle(x, part, got_first, got_second, bias, gain, shift):
    rows, model = x.shape
    shapes = [
        jax.ShapeDtypeStruct((rows, model), jnp.float32),
        jax.ShapeDtypeStruct((rows, model), jnp.bfloat16),
        jax.ShapeDtypeStruct((model, rows), jnp.bfloat16),
    ]
    return pl.pallas_call(
        lambda *refs: middle_body(rows // 2, *refs),
        in_specs=vmem(7),
        out_specs=vmem(3),
        out_shape=shapes,
        compiler_params=pltpu.CompilerParams(vmem_limit_bytes=40 << 20),
        cost_estimate=pl.CostEstimate(flops=1024, bytes_accessed=1024, transcendentals=0),
        name="middle",
    )(x, part, got_first, got_second, bias, gain, shift)


def turn_body(half, inner, grad, got_first, got_second, cot, gain, keep, gb, gbt, vectors):
    for k, got in enumerate((got_first, got_second)):
        part_rows = slice(k * half, (k + 1) * half)
        value = grad[part_rows] + wide(got[...])
        xhat, inverse = norm_parts(inner[part_rows])
        top = wide(cot[part_rows])
        total = top + norm_back(value, xhat, inverse, gain[...])
        gb[part_rows] = low(total)
        if k == 0:
            keep[...] = total
            vectors[0:1, :] = jnp.sum(wide(low(total)), axis=0, keepdims=True)
            vectors[1:2, :] = jnp.sum(value * xhat, axis=0, keepdims=True)
            vectors[2:3, :] = jnp.sum(value, axis=0, keepdims=True)
            vectors[3:4, :] = jnp.sum(top, axis=0, keepdims=True)
    gbt[...] = gb[...].T


def turn(inner, grad, got_first, got_second, cot, gain):
    rows, model = inner.shape
    shapes = [
        jax.ShapeDtypeStruct((rows // 2, model), jnp.float32),
        jax.ShapeDtypeStruct((rows, model), jnp.bfloat16),
        jax.ShapeDtypeStruct((model, rows), jnp.bfloat16),
        jax.ShapeDtypeStruct((4, model), jnp.float32),
    ]
    return pl.pallas_call(
        lambda *refs: turn_body(rows // 2, *refs),
        in_specs=vmem(6),
        out_specs=vmem(4),
        out_shape=shapes,
        compiler_params=pltpu.CompilerParams(vmem_limit_bytes=40 << 20),
        cost_estimate=pl.CostEstimate(flops=1024, bytes_accessed=1024, transcendentals=0),
        name="turn",
    )(inner, grad, got_first, got_second, cot, gain)


def pick(pair, index):
    return lax.dynamic_index_in_dim(pair, index, axis=0, keepdims=False)


def order_pair(mine, other, core):
    return jnp.where(core == 0, jnp.stack([mine, other]), jnp.stack([other, mine]))


def shards(
    clips,
    lengths,
    norm1_gain,
    norm1_bias,
    w_query,
    bias_query,
    w_key,
    w_value,
    bias_value,
    w_out,
    bias_out,
    norm2_gain,
    norm2_bias,
    w_up,
    bias_up,
    w_down,
    bias_down,
    cotangent,
):
    rows = clips.shape[1]
    model = clips.shape[2]
    depth, width = w_query.shape
    hidden_width = w_up.shape[1]
    data_size = lax.axis_size("dp")
    place = lax.axis_index("tensor")
    core = place % 2
    masks = masks_of(data_size)

    sent = jnp.concatenate([pick(clips, 1 - core), pick(cotangent, 1 - core)], axis=0)
    vectors = (norm1_gain, norm1_bias, bias_out, norm2_gain, norm2_bias, bias_down)
    attn = Gather(prepare(vectors, (w_query, w_key, w_value, w_out.T)))
    got = tensor_swap(sent, 1)
    half_rows = jnp.concatenate([pick(clips, core), got[:rows], pick(cotangent, core), got[rows:]], axis=0)
    other_half = tensor_swap(half_rows, 2)
    local_bias = jnp.concatenate([bias_up, bias_query, bias_value])
    sib_bias = tensor_swap(local_bias.reshape(1, -1), 1)[0]

    cut = FIRST_TILES * TILE
    down_t = w_down.T
    ff_one = Gather([w_up[:, :cut], down_t[:, :cut]])
    ff_two = Gather([w_up[:, cut:], down_t[:, cut:]])
    attn.early()
    other_half, sib_bias = settle(attn, ff_one, ff_two, other_half, sib_bias)
    attn.advance()
    ff_one.early()
    low_rows = jnp.concatenate([half_rows[: 2 * rows], other_half[: 2 * rows]], axis=0)
    cot = jnp.concatenate([half_rows[2 * rows :], other_half[2 * rows :]], axis=0)
    cott = cot.T
    low_rows, cot, cott = settle(attn, ff_one, low_rows, cot, cott)
    attn.advance()
    ff_one.advance()
    ff_two.early()
    length = pick(lengths, core)
    block = place ^ lax.iota(jnp.int32, 4)
    position = (block[:, None] * rows + lax.iota(jnp.int32, rows)[None, :]).reshape(-1)
    mask = (position < length).astype(jnp.float32).reshape(-1, 1)
    biases = (local_bias.reshape(1, -1), sib_bias.reshape(1, -1))
    joined_biases = []
    for item in biases:
        item = wide(item[:, hidden_width:])
        joined_biases.append(jnp.concatenate([item[:, :width], jnp.zeros((1, width), jnp.float32), item[:, width:]], axis=1))
    mask, joined_biases = settle(attn, ff_one, ff_two, mask, joined_biases)
    ff_one.advance()
    ff_two.advance()

    attn_all, vector_all = place_blocks(attn, depth, VEC_ROWS, True)
    attn_own = attn_all.reshape(model, model)
    attn_sib = tensor_swap(attn_own, 1)
    attn_w = (attn_own, attn_sib)
    vectors_full = wide(vector_all[:, :6, :depth].transpose(1, 0, 2).reshape(6, model))
    gain_one, shift_one, out_bias, gain_two, shift_two, down_bias = [vectors_full[k : k + 1] for k in range(6)]
    outs = attn_forward((low_rows, gain_one, shift_one), attn_own, joined_biases[0], mask, width, True)
    normed_one, n1t = outs[:2]
    saved = [outs[2:5]]
    outs = attn_forward((normed_one, outs[5]), attn_sib, joined_biases[1], mask, width, False)
    saved.append(outs[:3])
    part_keep, *part_send = outs[3:]

    def exchange(send):
        return tensor_swap(send[0], 2), tensor_swap(send[1], 2)

    (part_send,) = settle(ff_one, ff_two, part_send)
    ff_two.advance()
    first, second = exchange(part_send)

    def ff_weights(gathered):
        own_w = [item.reshape(model, -1) for item in place_blocks(gathered, depth)]
        return own_w, [tensor_swap(item, 1) for item in own_w]

    one_own, one_sib = ff_weights(ff_one)
    first, second, one_sib = settle(ff_two, first, second, one_sib)
    two_own, two_sib = ff_weights(ff_two)
    inner, normed_two, n2t = middle(low_rows, part_keep, first, second, out_bias, gain_two, shift_two)
    bias_rows = [[item[:, :cut], item[:, cut:hidden_width]] for item in biases]
    outs = feed_forward(normed_two, cot, n2t, cott, one_own, one_sib, bias_rows[0][0], bias_rows[1][0], TILE)
    one_sums = outs[6:]
    one_grads, one_sent = outs[2:4], [tensor_swap(item, 1) for item in outs[4:6]]
    outs = feed_forward(normed_two, cot, n2t, cott, two_own, two_sib, bias_rows[0][1], bias_rows[1][1], TILE, outs[:2])
    out_keep, out_send, grad_keep, *grad_send = outs[:5]
    two_sums = outs[9:]
    two_grads, two_sent = outs[5:7], [tensor_swap(item, 1) for item in outs[7:9]]

    first, second = exchange(grad_send)
    scatter_one, scatter_two = Scatter(one_grads, one_sent), Scatter(two_grads, two_sent)
    scatter_one.advance()
    first, second, out_send, two_sent = settle_scatters([scatter_one], first, second, out_send, two_sent)
    out_got = tensor_swap(out_send, 2)
    scatter_one.advance()
    scatter_two.advance()
    inner_keep, grad_branch, gbt, vectors_two = turn(inner, grad_keep, first, second, cot, gain_two)
    part, *other_grads, other_sums = attn_backward(grad_branch, gbt, n1t, attn_w[1], saved[1], mask, width)
    part, out_got, other_grads = settle_scatters([scatter_one, scatter_two], part, out_got, other_grads)
    scatter_one.advance()
    scatter_two.advance()
    attn_sent = [tensor_swap(item, 1) for item in other_grads]
    one_keep, one_send, *own_grads, own_sums = attn_backward(grad_branch, gbt, n1t, attn_w[0], saved[0], mask, width, part)
    own_grads, one_send, attn_sent, out_got = settle_scatters([scatter_one, scatter_two], own_grads, one_send, attn_sent, out_got)
    scatter_attn = Scatter(own_grads, attn_sent)
    scatter_one.rest()
    scatter_two.advance()
    scatter_attn.advance()
    one_got = tensor_swap(one_send, 2)
    one_got, out_got = settle_scatters([scatter_two, scatter_attn], one_got, out_got)
    scatter_two.rest()
    scatter_attn.advance()

    out_half = inner[: 2 * rows] + (out_keep + wide(out_got) + down_bias)
    out_low = low(out_half)
    output = order_pair(out_low[:rows], tensor_swap(out_low[rows:], 1), core)
    xhat_one, inverse_one = norm_parts(wide(low_rows[: 2 * rows]))
    grad_normed_one = one_keep + wide(one_got)
    v_gain_one = jnp.sum(grad_normed_one * xhat_one, axis=0, keepdims=True)
    v_shift_one = jnp.sum(grad_normed_one, axis=0, keepdims=True)
    clip_half = inner_keep + norm_back(grad_normed_one, xhat_one, inverse_one, gain_one)
    clip_grad = order_pair(clip_half[:rows], tensor_swap(clip_half[rows:], 1), core)

    small = jnp.concatenate([v_gain_one, v_shift_one, vectors_two], axis=0)

    def bias_pair(up_sums, sums):
        first_row = jnp.pad(jnp.concatenate(up_sums, axis=1), ((0, 0), (0, model - hidden_width)))
        second_row = jnp.concatenate([sums[:1, :width], sums[:1, 2 * width :], jnp.zeros((1, model - 2 * width), jnp.float32)], axis=1)
        return jnp.concatenate([first_row, second_row], axis=0)

    from_sib = tensor_swap(jnp.concatenate([small, bias_pair((one_sums[1], two_sums[1]), other_sums)], axis=0), 1)
    small = small + from_sib[:6]
    small = small + tensor_swap(small, 2)
    small = jnp.concatenate([small, bias_pair((one_sums[0], two_sums[0]), own_sums) + from_sib[6:]], axis=0)
    for mask_bit in masks[::-1]:
        small = small + data_swap(small, mask_bit)
    vector_own = lax.dynamic_slice_in_dim(small[:6], lax.axis_index("dp") * depth, depth, axis=1)

    scatter_attn.rest()
    one_up, one_down = scatter_one.finish()
    two_up, two_down = scatter_two.finish()
    attn_one, attn_two = scatter_attn.finish()
    return (
        output,
        clip_grad,
        vector_own[0],
        vector_own[1],
        attn_one[:, :width],
        small[7, :width],
        attn_one[:, width:],
        attn_two[:, :width],
        small[7, width : 2 * width],
        attn_two[:, width:].T,
        vector_own[2],
        vector_own[3],
        vector_own[4],
        jnp.concatenate([one_up, two_up], axis=1),
        small[6, :hidden_width],
        jnp.concatenate([one_down, two_down], axis=1).T,
        vector_own[5],
    )


def solution(mesh):
    rows_spec = P("dp", "tensor", None)
    data, tensor = P("dp"), P("tensor")
    wide_spec, tall_spec = P("dp", "tensor"), P("tensor", "dp")
    placed = (
        rows_spec,
        data,
        data,
        data,
        wide_spec,
        tensor,
        wide_spec,
        wide_spec,
        tensor,
        tall_spec,
        data,
        data,
        data,
        wide_spec,
        tensor,
        tall_spec,
        data,
        rows_spec,
    )
    outs = (
        rows_spec,
        rows_spec,
        data,
        data,
        wide_spec,
        tensor,
        wide_spec,
        wide_spec,
        tensor,
        tall_spec,
        data,
        data,
        data,
        wide_spec,
        tensor,
        tall_spec,
        data,
    )
    return jax.shard_map(shards, mesh=mesh, in_specs=placed, out_specs=outs, check_vma=False)
```

```python
import jax
import jax.numpy as jnp
from jax import lax
from jax.experimental import pallas as pl
from jax.experimental.pallas import tpu as pltpu
from jax.sharding import PartitionSpec as P

HEAD_DIM = 80
norm_eps = 1e-05
VEC_ROWS = 8
TILE = 256
FIRST_TILES = 3
VMEM_LIMIT = 60 << 20


def low(values):
    return values.astype(jnp.bfloat16)


def wide(values):
    return values.astype(jnp.float32)


def mm(left, right):
    return jnp.dot(left, right, preferred_element_type=jnp.float32)


def mm_left(left, right):
    return lax.dot_general(left, right, (((0,), (0,)), ((), ())), preferred_element_type=jnp.float32)


def mm_right(left, right):
    return lax.dot_general(left, right, (((1,), (1,)), ((), ())), preferred_element_type=jnp.float32)


def norm_parts(values):
    center = values - jnp.mean(values, axis=-1, keepdims=True)
    spread = jnp.mean(center * center, axis=-1, keepdims=True)
    inverse = lax.rsqrt(spread + norm_eps)
    return center * inverse, inverse


def norm_back(grad, xhat, inverse, gain):
    scaled = grad * gain
    first = jnp.mean(scaled, axis=-1, keepdims=True)
    second = jnp.mean(scaled * xhat, axis=-1, keepdims=True)
    return (scaled - first - xhat * second) * inverse


def gelu_pair(pre):
    half = 0.5 * (1.0 + lax.erf(pre * (0.5 ** 0.5)))
    slope = half + pre * jnp.exp(-0.5 * pre * pre) * 0.3989422804014327
    return pre * half, slope


def tensor_swap(values, mask):
    size = lax.axis_size("tensor")
    return lax.ppermute(values, "tensor", [(i, i ^ mask) for i in range(size)])


def data_swap(values, mask):
    size = lax.axis_size("dp")
    return lax.ppermute(values, "dp", [(i, i ^ mask) for i in range(size)])


def masks_of(size):
    masks = []
    while size > 1:
        size //= 2
        masks.append(size)
    return masks


def pin(values, *others):
    return lax.optimization_barrier((values, others))[0]


def after(values, *others):
    return pin(values, *others) if others else values


def vmem(count):
    return [pl.BlockSpec(memory_space=pltpu.VMEM)] * count


def tiny_cost():
    return pl.CostEstimate(flops=1024, bytes_accessed=1024, transcendentals=0)


def join_body(plan, inputs, *refs):
    sources, outs, sems = refs[:inputs], refs[inputs:-1], refs[-1]
    copies = []
    for k, (source, start, columns, out, row) in enumerate(plan):
        count = sources[source].shape[0]
        origin = sources[source]
        if columns != origin.shape[2]:
            origin = origin.at[:, :, pl.ds(start, columns)]
        copies.append(pltpu.make_async_copy(origin, outs[out].at[pl.ds(row, count)], sems.at[k]))
    for item in copies:
        item.start()
    for item in copies:
        item.wait()


def join(sources, plan, shapes):
    return pl.pallas_call(
        lambda *refs: join_body(plan, len(sources), *refs),
        in_specs=[pl.BlockSpec(memory_space=pl.ANY)] * len(sources),
        out_specs=vmem(len(shapes)),
        out_shape=[jax.ShapeDtypeStruct(shape, jnp.bfloat16) for shape in shapes],
        compiler_params=pltpu.CompilerParams(vmem_limit_bytes=16 << 20),
        scratch_shapes=[pltpu.SemaphoreType.DMA((len(plan),))],
        cost_estimate=tiny_cost(),
        name="join",
    )(*sources)


class Gather:
    def __init__(self, shard):
        self.masks = masks_of(lax.axis_size("dp"))
        self.held, self.fresh = [shard[None]], []
        self.order = [[0], [0]]

    def extend(self, side, mask):
        self.order[side] = self.order[side] + [item ^ mask for item in self.order[side]]

    def early(self):
        for mask in self.masks[:-2]:
            if self.fresh:
                self.held = [jnp.concatenate([self.held[0], self.fresh[0]], axis=0)]
            self.fresh = [data_swap(self.held[0], mask)]
            self.extend(0, mask)
            self.extend(1, mask)

    def send(self, masks):
        self.fresh = [data_swap(self.held[side], masks[side]) for side in range(2)]
        for side in range(2):
            self.extend(side, masks[side])

    def second(self):
        count, rows, columns = self.held[0].shape
        half = columns // 2
        plan = [(k, side * half, half, side, k * count) for k in range(2) for side in range(2)]
        self.held = join(self.held + self.fresh, plan, [(2 * count, rows, half)] * 2)
        self.send([self.masks[-2], self.masks[-1]])

    def third(self):
        count, rows, half = self.held[0].shape
        plan = [(2 * k + side, 0, half, side, k * count) for k in range(2) for side in range(2)]
        self.held = join(list(self.held) + self.fresh, plan, [(2 * count, rows, half)] * 2)
        self.send([self.masks[-1], self.masks[-2]])


def settle(*items):
    gathers = [item for item in items if isinstance(item, Gather)]
    others = [item for item in items if not isinstance(item, Gather)]
    arrays = [(item.held, item.fresh) for item in gathers]
    arrays, others = lax.optimization_barrier((arrays, others))
    for item, (held, fresh) in zip(gathers, arrays):
        item.held, item.fresh = list(held), list(fresh)
    return others


def place_body(gathered, depth, extra, me_ref, *refs):
    pieces, outs, sems = refs[:4], refs[4:-1], refs[-1]
    me = me_ref[0]
    copies = []
    for side in range(2):
        held, fresh = pieces[2 * side : 2 * side + 2]
        columns = held.shape[2]
        for position, item in enumerate(gathered.order[side]):
            count = held.shape[0]
            piece, row = (held, position) if position < count else (fresh, position - count)
            target = outs[0].at[me ^ item, pl.ds(0, depth), pl.ds(side * columns, columns)]
            source = piece.at[row, pl.ds(0, depth)] if extra else piece.at[row]
            copies.append(pltpu.make_async_copy(source, target, sems.at[len(copies)]))
            if extra and side == 0:
                source = piece.at[row, pl.ds(depth, extra)]
                copies.append(pltpu.make_async_copy(source, outs[-1].at[me ^ item], sems.at[len(copies)]))
    for item in copies:
        item.start()
    for item in copies:
        item.wait()


def place_blocks(gathered, depth, extra=0):
    size = lax.axis_size("dp")
    pieces = [gathered.held[0], gathered.fresh[0], gathered.held[1], gathered.fresh[1]]
    columns = pieces[0].shape[2]
    if extra and depth % 8:
        whole = place_blocks(gathered, depth + extra)[0]
        return [whole[:, :depth], whole[:, depth:, :columns]]
    me = lax.axis_index("dp").reshape(1)
    shapes = [jax.ShapeDtypeStruct((size, depth, 2 * columns), jnp.bfloat16)]
    if extra:
        shapes.append(jax.ShapeDtypeStruct((size, extra, columns), jnp.bfloat16))
    return pl.pallas_call(
        lambda *refs: place_body(gathered, depth, extra, *refs),
        in_specs=[pl.BlockSpec(memory_space=pltpu.SMEM)] + [pl.BlockSpec(memory_space=pl.ANY)] * 4,
        out_specs=vmem(len(shapes)),
        out_shape=shapes,
        compiler_params=pltpu.CompilerParams(vmem_limit_bytes=VMEM_LIMIT),
        scratch_shapes=[pltpu.SemaphoreType.DMA((3 * size if extra else 2 * size,))],
        cost_estimate=tiny_cost(),
        name="place",
    )(me, *pieces)


def spread(number, masks):
    return sum(((number >> k) & 1) * mask for k, mask in enumerate(masks))


def compress(number, masks):
    return sum(((number // mask) & 1) << k for k, mask in enumerate(masks))


def sum_body(counts, merged, split, me_ref, *refs):
    outs = refs[sum(counts) :]
    start = 0
    for side, count in enumerate(counts):
        total = wide(refs[start][...])
        for ref in refs[start + 1 : start + count]:
            total = total + wide(ref[...])
        start += count
        if split:
            for k in range(2):
                out = outs[2 * side + k]
                out[...] = total[0, :, k * out.shape[1] : (k + 1) * out.shape[1]]
        elif merged:
            columns = total.shape[-1]
            outs[0][:, :, side * columns : (side + 1) * columns] = total.astype(outs[0].dtype)
        else:
            outs[side][...] = total.astype(outs[side].dtype)


class Scatter:
    def __init__(self, own, other):
        self.size = lax.axis_size("dp")
        self.half = own.shape[1] // 2
        self.depth = own.shape[0] // self.size
        shape = (self.size, self.depth, own.shape[1])
        self.own, self.other = own.reshape(shape), other.reshape(shape)
        masks = masks_of(self.size)[::-1]
        self.masks = [masks, [masks[1], masks[0]] + masks[2:]]
        self.gots = []
        self.step = 0

    def remaining(self, side, step):
        return sorted(set(self.masks[side]) - set(self.masks[side][: step + 1]))

    def total(self, final, merged, split=False):
        step = self.step
        last = len(self.masks[0]) == step
        specs, operands, counts = [], [], []
        for side in range(2):
            rest = [] if last else self.remaining(side, step)
            before = sum(self.masks[side][:step])
            flip = 0 if last else self.masks[side][step]

            def block(i, me, rest=rest, before=before, flip=flip):
                mine = me[0]
                return (mine & before) | ((mine ^ flip) & flip) | spread(i, rest)

            shape = (1, self.depth, self.half)
            for array in (self.own, self.other):
                specs.append(pl.BlockSpec(shape, lambda i, me, block=block, side=side: (block(i, me), 0, side)))
                operands.append(array)
            for number, got in enumerate(self.gots):
                kept = self.remaining(side, number)
                wide_got = len(got) == 1

                def place(i, me, block=block, kept=kept, side=side, wide_got=wide_got):
                    return compress(block(i, me), kept), 0, side if wide_got else 0

                specs.append(pl.BlockSpec(shape, place))
                operands.append(got[0] if wide_got else got[side])
            counts.append(2 + len(self.gots))
        count = 1 if last else self.size >> (step + 1)
        dtype = jnp.float32 if final else jnp.bfloat16
        columns = 2 * self.half if merged else self.half
        outs = [jax.ShapeDtypeStruct((count, self.depth, columns), dtype)] * (1 if merged else 2)
        out_specs = [pl.BlockSpec((1, self.depth, columns), lambda i, me: (i, 0, 0))] * len(outs)
        if split:
            outs = [jax.ShapeDtypeStruct((self.depth, self.half // 2), dtype)] * 4
            out_specs = [pl.BlockSpec((self.depth, self.half // 2), lambda i, me: (0, 0))] * 4
        return pl.pallas_call(
            lambda *refs: sum_body(counts, merged, split, *refs),
            grid_spec=pltpu.PrefetchScalarGridSpec(
                num_scalar_prefetch=1,
                grid=(count,),
                in_specs=specs,
                out_specs=out_specs,
            ),
            out_shape=outs,
            compiler_params=pltpu.CompilerParams(vmem_limit_bytes=VMEM_LIMIT),
            cost_estimate=tiny_cost(),
            name="sum_blocks",
        )(lax.axis_index("dp").reshape(1), *operands)

    def prepare(self):
        self.sends = self.total(False, self.step >= 2)
        return self.sends

    def launch(self):
        masks = [self.masks[side][self.step] for side in range(len(self.sends))]
        self.gots = self.gots + [[data_swap(send, mask) for send, mask in zip(self.sends, masks)]]
        self.step += 1

    def advance(self):
        self.prepare()
        self.launch()

    def rest(self):
        while self.step < len(self.masks[0]):
            self.advance()

    def finish(self):
        return [item[0] for item in self.total(True, False)]


def settle_scatters(scatters, *others):
    gots, others = lax.optimization_barrier(([item.gots for item in scatters], others))
    for item, got in zip(scatters, gots):
        item.gots = got
    return others


def ff_body(first, tiles, half, *refs):
    n2, cot, n2t, cott, own_up, own_down, sib_up, sib_down, own_b, sib_b = refs[:10]
    refs = refs[10:]
    if not first:
        prev_b, prev_g = refs[:2]
        refs = refs[2:]
    if first:
        acc_b, acc_g = refs[:2]
        g_own, g_sib, b_own, b_sib = refs[2:]
    else:
        out_keep, out_send, grad_keep, grad_send, g_own, g_sib, b_own, b_sib, acc_b, acc_g = refs
    side, tile = pl.program_id(0), pl.program_id(1)

    @pl.when((side == 0) & (tile == 0))
    def _():
        if first:
            acc_b[...] = jnp.zeros_like(acc_b)
            acc_g[...] = jnp.zeros_like(acc_g)
        else:
            acc_b[...] = prev_b[...]
            acc_g[...] = prev_g[...]

    def step(up_ref, down_ref, bias, grads, bias_sum):
        up, down = up_ref[...], down_ref[...]
        width = up.shape[1]
        pre = mm(n2[...], up) + wide(bias[...])
        act, slope = gelu_pair(pre)
        hidden = low(act)
        grad_pre = low(mm(cot[...], down) * slope)
        acc_b[...] += mm_right(hidden, down)
        acc_g[...] += mm_right(grad_pre, up)
        grads[:, :width] = low(mm(n2t[...], grad_pre))
        grads[:, width:] = low(mm(cott[...], hidden))
        bias_sum[...] = jnp.sum(wide(grad_pre), axis=0, keepdims=True)

    @pl.when(side == 0)
    def _():
        step(sib_up, sib_down, sib_b, g_sib, b_sib)

    @pl.when(side == 1)
    def _():
        step(own_up, own_down, own_b, g_own, b_own)

    if not first:

        @pl.when((side == 1) & (tile == tiles - 1))
        def _():
            out_keep[...] = acc_b[:half]
            out_send[...] = low(acc_b[half:])
            grad_keep[...] = acc_g[...]
            grad_send[:half] = low(acc_g[half:])
            grad_send[half:] = low(acc_g[:half])


def prepare_body(*refs):
    vectors, (w_query, w_key, w_value, w_out_t), out = refs[:6], refs[6:10], refs[10]
    depth, width = w_query.shape
    out[:depth] = jnp.concatenate([w_query[...], w_key[...], w_value[...], w_out_t[...]], axis=1)
    out[depth:] = jnp.zeros_like(out[depth:])
    for k, vector in enumerate(vectors):
        out[depth + k : depth + k + 1, :depth] = vector[...].reshape(1, depth)


def prepare(vectors, weights):
    depth, width = weights[0].shape
    return pl.pallas_call(
        prepare_body,
        in_specs=vmem(10),
        out_specs=pl.BlockSpec(memory_space=pltpu.VMEM),
        out_shape=jax.ShapeDtypeStruct((depth + VEC_ROWS, 4 * width), jnp.bfloat16),
        compiler_params=pltpu.CompilerParams(vmem_limit_bytes=VMEM_LIMIT),
        cost_estimate=tiny_cost(),
        name="prepare",
    )(*vectors, *weights)


def assemble_body(half, mine, other_rows, other_cot, rows, cot, cot_t):
    rows[:half] = mine[:half]
    rows[half:] = other_rows[...]
    cot[:half] = mine[half:]
    cot[half:] = other_cot[...]
    cot_t[...] = cot[...].T


def assemble(mine, other_rows, other_cot):
    rows, model = mine.shape
    shape = jax.ShapeDtypeStruct((rows, model), jnp.bfloat16)
    return pl.pallas_call(
        lambda *refs: assemble_body(rows // 2, *refs),
        in_specs=vmem(3),
        out_specs=vmem(3),
        out_shape=[shape, shape, jax.ShapeDtypeStruct((model, rows), jnp.bfloat16)],
        compiler_params=pltpu.CompilerParams(vmem_limit_bytes=VMEM_LIMIT),
        cost_estimate=tiny_cost(),
        name="assemble",
    )(mine, other_rows, other_cot)


def feed_forward(n2, cot, n2t, cott, own_w, sib_w, own_b, sib_b, tile, previous=None):
    rows, model = n2.shape
    hidden = own_b.shape[1]
    tiles = hidden // tile
    first = previous is None
    half = rows // 2

    def const(shape):
        return pl.BlockSpec(shape, lambda s, i: (0, 0), pipeline_mode=pl.Buffered(1))

    def second(shape, start=0):
        return pl.BlockSpec(shape, lambda s, i: (0, start + jnp.where(s == 1, i, 0)))

    def initial(shape, start=0):
        return pl.BlockSpec(shape, lambda s, i: (0, start + jnp.where(s == 0, i, tiles - 1)))

    in_specs = [const((rows, model))] * 2 + [const((model, rows))] * 2
    in_specs += [second((model, tile)), second((model, tile), tiles), initial((model, tile)), initial((model, tile), tiles)]
    in_specs += [second((1, tile)), initial((1, tile))]
    operands = [n2, cot, n2t, cott, own_w, own_w, sib_w, sib_w, own_b, sib_b]
    full = jax.ShapeDtypeStruct((rows, model), jnp.float32)
    grads = jax.ShapeDtypeStruct((model, 2 * hidden), jnp.bfloat16)
    sums = jax.ShapeDtypeStruct((1, hidden), jnp.float32)
    tail_shapes = [grads, grads, sums, sums]
    tail_specs = [second((model, 2 * tile)), initial((model, 2 * tile)), second((1, tile)), initial((1, tile))]
    scratch = []
    if first:
        shapes = [full, full] + tail_shapes
        specs = [const((rows, model))] * 2 + tail_specs
    else:
        operands += list(previous)
        in_specs += [const((rows, model))] * 2
        shapes = [
            jax.ShapeDtypeStruct((half, model), jnp.float32),
            jax.ShapeDtypeStruct((half, model), jnp.bfloat16),
            full,
            jax.ShapeDtypeStruct((rows, model), jnp.bfloat16),
        ] + tail_shapes
        specs = [const((half, model))] * 2 + [const((rows, model))] * 2 + tail_specs
        scratch = [pltpu.VMEM((rows, model), jnp.float32)] * 2
    return pl.pallas_call(
        lambda *refs: ff_body(first, tiles, half, *refs),
        grid=(2, tiles),
        in_specs=in_specs,
        out_specs=specs,
        out_shape=shapes,
        scratch_shapes=scratch,
        compiler_params=pltpu.CompilerParams(vmem_limit_bytes=VMEM_LIMIT),
        cost_estimate=tiny_cost(),
        name="feed_forward",
    )(*operands)


def dot_t(left, right):
    return lax.dot_general(left, right, (((0,), (0,)), ((), ())), preferred_element_type=jnp.float32)


def norm_rows(values, gain, shift):
    xhat, inverse = norm_parts(values)
    return low(xhat * gain + shift)


def attn_head(joined, head, width, mask):
    scale = HEAD_DIM ** (-0.5)
    begin = pl.multiple_of(head * HEAD_DIM, 16)
    query = joined[pl.ds(begin, HEAD_DIM), :]
    keys = joined[pl.ds(pl.multiple_of(width + begin, 16), HEAD_DIM), :]
    values = joined[pl.ds(pl.multiple_of(2 * width + begin, 16), HEAD_DIM), :]
    scores = jnp.where(mask[...] > 0.5, dot_t(keys, query) * scale, -1000000000.0)
    return begin, query, keys, values, scores


def attn_forward_body(first, width, *refs):
    if first:
        x, gain, shift, weights, bias, mask, n1, n1t, joined, mixed, totals, part = refs
        n1[...] = norm_rows(wide(x[...]), gain[...], shift[...])
        n1t[...] = n1[...].T
    else:
        n1, previous, weights, bias, mask, joined, mixed, totals, part, send = refs
    joined[...] = low(mm(n1[...], weights[:, : 3 * width]) + bias[...]).T

    def one(head, carry):
        begin, query, keys, values, scores = attn_head(joined, head, width, mask)
        top = jnp.max(scores, axis=0, keepdims=True)
        expo = jnp.exp(scores - top)
        total = jnp.sum(expo, axis=0, keepdims=True)
        probs = low(expo * (1.0 / total))
        mixed[pl.ds(begin, HEAD_DIM), :] = low(mm(values, probs))
        totals[pl.ds(head, 1), :] = top + jnp.log(total)
        return carry

    lax.fori_loop(0, width // HEAD_DIM, one, 0)
    term = mm_right(mixed[...].T, weights[:, 3 * width :])
    if first:
        part[...] = term
    else:
        term = previous[...] + term
        half = term.shape[0] // 2
        part[...] = term
        send[:half] = low(term[half:])
        send[half:] = low(term[:half])


def attn_forward(head_in, weights, bias, mask, width, first):
    rows, model = head_in[0].shape
    low_shape = lambda *shape: jax.ShapeDtypeStruct(shape, jnp.bfloat16)
    wide_shape = lambda *shape: jax.ShapeDtypeStruct(shape, jnp.float32)
    shapes = [low_shape(3 * width, rows), low_shape(width, rows), wide_shape(width // HEAD_DIM, rows), wide_shape(rows, model)]
    shapes = [low_shape(rows, model), low_shape(model, rows)] + shapes if first else shapes + [low_shape(rows, model)]
    operands = list(head_in) + [weights, bias, mask]
    return pl.pallas_call(
        lambda *refs: attn_forward_body(first, width, *refs),
        in_specs=vmem(len(operands)),
        out_specs=vmem(len(shapes)),
        out_shape=shapes,
        compiler_params=pltpu.CompilerParams(vmem_limit_bytes=VMEM_LIMIT),
        cost_estimate=tiny_cost(),
        name="attn_forward",
    )(*operands)


def attn_backward_body(first, width, half, *refs):
    gb, gbt, n1t, weights, joined, mixed, totals, mask = refs[:8]
    refs = refs[8:]
    if first:
        part, grads, sums, gmt, djoined = refs
    else:
        previous, keep, send, grads, sums, gmt, djoined = refs
    scale = HEAD_DIM ** (-0.5)
    gmt[...] = low(mm(gb[...], weights[:, 3 * width :])).T

    def one(head, carry):
        begin, query, keys, values, scores = attn_head(joined, head, width, mask)
        probs = jnp.exp(scores - totals[pl.ds(head, 1), :])
        gm = gmt[pl.ds(begin, HEAD_DIM), :]
        grad_probs = dot_t(values, gm)
        delta = jnp.sum(grad_probs * probs, axis=0, keepdims=True)
        grad_scores = low(probs * (grad_probs - delta))
        djoined[pl.ds(begin, HEAD_DIM), :] = low(mm(keys, grad_scores) * scale)
        djoined[pl.ds(pl.multiple_of(width + begin, 16), HEAD_DIM), :] = low(mm_right(query, grad_scores) * scale)
        djoined[pl.ds(pl.multiple_of(2 * width + begin, 16), HEAD_DIM), :] = low(mm_right(gm, low(probs)))
        return carry

    lax.fori_loop(0, width // HEAD_DIM, one, 0)
    grads[:, : 3 * width] = low(mm_right(n1t[...], djoined[...]))
    grads[:, 3 * width :] = low(mm_right(gbt[...], mixed[...]))
    ones = jnp.ones((8, gb.shape[0]), jnp.bfloat16)
    sums[...] = mm_right(ones, djoined[...])
    term = mm_right(djoined[...].T, weights[:, : 3 * width])
    if first:
        part[...] = term
    else:
        term = previous[...] + term
        keep[...] = term
        send[...] = low(term[half:])


def attn_backward(gb, gbt, n1t, weights, saved, mask, width, previous=None):
    rows, model = gb.shape
    first = previous is None
    half = rows // 2
    operands = [gb, gbt, n1t, weights, *saved, mask]
    shapes = [jax.ShapeDtypeStruct((model, 4 * width), jnp.bfloat16), jax.ShapeDtypeStruct((8, 3 * width), jnp.float32)]
    if first:
        shapes = [jax.ShapeDtypeStruct((rows, model), jnp.float32)] + shapes
    else:
        operands.append(previous)
        shapes = [
            jax.ShapeDtypeStruct((rows, model), jnp.float32),
            jax.ShapeDtypeStruct((half, model), jnp.bfloat16),
        ] + shapes
    return pl.pallas_call(
        lambda *refs: attn_backward_body(first, width, half, *refs),
        in_specs=vmem(len(operands)),
        out_specs=vmem(len(shapes)),
        out_shape=shapes,
        scratch_shapes=[pltpu.VMEM((width, rows), jnp.bfloat16), pltpu.VMEM((3 * width, rows), jnp.bfloat16)],
        compiler_params=pltpu.CompilerParams(vmem_limit_bytes=VMEM_LIMIT),
        cost_estimate=tiny_cost(),
        name="attn_backward",
    )(*operands)


def middle_body(half, x, part, got, bias, gain, shift, inner, n2, n2t):
    for k in range(2):
        part_rows = slice(k * half, (k + 1) * half)
        value = wide(x[part_rows]) + (part[part_rows] + wide(got[part_rows]) + bias[...])
        inner[part_rows] = value
        n2[part_rows] = norm_rows(value, gain[...], shift[...])
    n2t[...] = n2[...].T


def middle(x, part, got, bias, gain, shift):
    rows, model = x.shape
    shapes = [
        jax.ShapeDtypeStruct((rows, model), jnp.float32),
        jax.ShapeDtypeStruct((rows, model), jnp.bfloat16),
        jax.ShapeDtypeStruct((model, rows), jnp.bfloat16),
    ]
    return pl.pallas_call(
        lambda *refs: middle_body(rows // 2, *refs),
        in_specs=vmem(6),
        out_specs=vmem(3),
        out_shape=shapes,
        compiler_params=pltpu.CompilerParams(vmem_limit_bytes=VMEM_LIMIT),
        cost_estimate=tiny_cost(),
        name="middle",
    )(x, part, got, bias, gain, shift)


def turn_body(half, inner, grad, got, cot, gain, keep, gb, gbt, vectors):
    for k in range(2):
        part_rows = slice(k * half, (k + 1) * half)
        value = grad[part_rows] + wide(got[part_rows])
        xhat, inverse = norm_parts(inner[part_rows])
        top = wide(cot[part_rows])
        total = top + norm_back(value, xhat, inverse, gain[...])
        gb[part_rows] = low(total)
        if k == 0:
            keep[...] = total
            vectors[0:1, :] = jnp.sum(wide(low(total)), axis=0, keepdims=True)
            vectors[1:2, :] = jnp.sum(value * xhat, axis=0, keepdims=True)
            vectors[2:3, :] = jnp.sum(value, axis=0, keepdims=True)
            vectors[3:4, :] = jnp.sum(top, axis=0, keepdims=True)
    gbt[...] = gb[...].T


def turn(inner, grad, got, cot, gain):
    rows, model = inner.shape
    shapes = [
        jax.ShapeDtypeStruct((rows // 2, model), jnp.float32),
        jax.ShapeDtypeStruct((rows, model), jnp.bfloat16),
        jax.ShapeDtypeStruct((model, rows), jnp.bfloat16),
        jax.ShapeDtypeStruct((4, model), jnp.float32),
    ]
    return pl.pallas_call(
        lambda *refs: turn_body(rows // 2, *refs),
        in_specs=vmem(5),
        out_specs=vmem(4),
        out_shape=shapes,
        compiler_params=pltpu.CompilerParams(vmem_limit_bytes=VMEM_LIMIT),
        cost_estimate=tiny_cost(),
        name="turn",
    )(inner, grad, got, cot, gain)


def pick(pair, index):
    return lax.dynamic_index_in_dim(pair, index, axis=0, keepdims=False)


def order_pair(mine, other, core):
    return jnp.where(core == 0, jnp.stack([mine, other]), jnp.stack([other, mine]))


def shards(
    clips,
    lengths,
    norm1_gain,
    norm1_bias,
    w_query,
    bias_query,
    w_key,
    w_value,
    bias_value,
    w_out,
    bias_out,
    norm2_gain,
    norm2_bias,
    w_up,
    bias_up,
    w_down,
    bias_down,
    cotangent,
):
    rows = clips.shape[1]
    model = clips.shape[2]
    depth, width = w_query.shape
    hidden_width = w_up.shape[1]
    data_size = lax.axis_size("dp")
    place = lax.axis_index("tensor")
    core = place % 2
    masks = masks_of(data_size)

    vectors = (norm1_gain, norm1_bias, bias_out, norm2_gain, norm2_bias, bias_down)
    attn = Gather(prepare(vectors, (w_query, w_key, w_value, w_out.T)))
    attn.early()
    pair, cot_pair = after((clips, cotangent), attn.held)
    sent = jnp.concatenate([pick(pair, 1 - core), pick(cot_pair, 1 - core)], axis=0)
    got = tensor_swap(sent, 1)
    half_clip = jnp.concatenate([pick(pair, core), got[:rows]], axis=0)
    half_cot = jnp.concatenate([pick(cot_pair, core), got[rows:]], axis=0)
    other_clip = tensor_swap(half_clip, 2)
    local_bias = jnp.concatenate([bias_up, bias_query, bias_value])
    sib_bias = tensor_swap(local_bias.reshape(1, -1), 1)[0]
    cut = FIRST_TILES * TILE
    down_t = w_down.T
    ff_one = Gather(jnp.concatenate([w_up[:, :cut], down_t[:, :cut]], axis=1))
    ff_two = Gather(jnp.concatenate([w_up[:, cut:], down_t[:, cut:]], axis=1))
    length = pick(lengths, core)
    block = place ^ lax.iota(jnp.int32, 4)
    position = (block[:, None] * rows + lax.iota(jnp.int32, rows)[None, :]).reshape(-1)
    mask = (position < length).astype(jnp.float32).reshape(-1, 1)
    other_clip, half_cot, sib_bias, mask = settle(attn, ff_one, ff_two, other_clip, half_cot, sib_bias, mask)

    attn.second()
    other_cot = tensor_swap(half_cot, 2)
    biases = (local_bias.reshape(1, -1), sib_bias.reshape(1, -1))
    joined_biases = []
    for item in biases:
        item = wide(item[:, hidden_width:])
        joined_biases.append(jnp.concatenate([item[:, :width], jnp.zeros((1, width), jnp.float32), item[:, width:]], axis=1))
    joined_biases, other_clip = settle(attn, ff_one, joined_biases, other_clip)

    attn.third()
    ff_one.early()
    low_rows, cot, cott = assemble(jnp.concatenate([half_clip, half_cot], axis=0), other_clip, other_cot)
    low_rows, cot, cott = settle(attn, ff_one, ff_two, low_rows, cot, cott)

    attn_all, vector_all = place_blocks(attn, depth, VEC_ROWS)
    attn_own = attn_all.reshape(model, model)
    attn_sib = tensor_swap(attn_own, 1)
    attn_w = (attn_own, attn_sib)
    ff_one.second()
    ff_two.early()
    vectors_full = wide(vector_all[:, :6, :depth].transpose(1, 0, 2).reshape(6, model))
    gain_one, shift_one, out_bias, gain_two, shift_two, down_bias = [vectors_full[k : k + 1] for k in range(6)]
    outs = attn_forward((low_rows, gain_one, shift_one), attn_own, joined_biases[0], mask, width, True)
    normed_one, n1t = outs[:2]
    saved = [outs[2:5]]
    outs = attn_forward((normed_one, outs[5]), attn_sib, joined_biases[1], mask, width, False)
    saved.append(outs[:3])
    part_keep, part_send = outs[3:]

    def ff_weights(gathered):
        own_w = place_blocks(gathered, depth)[0].reshape(model, -1)
        return own_w, tensor_swap(own_w, 1)

    (part_send,) = settle(ff_one, ff_two, part_send)
    part_got = tensor_swap(part_send, 2)
    ff_one.third()
    ff_two.second()
    (part_got,) = settle(ff_one, ff_two, part_got)
    ff_two.third()
    one_own, one_sib = ff_weights(ff_one)
    inner_in = after(part_keep, one_own)
    inner, normed_two, n2t = middle(low_rows, inner_in, part_got, out_bias, gain_two, shift_two)
    bias_rows = [[item[:, :cut], item[:, cut:hidden_width]] for item in biases]
    one_sib, normed_two = settle(ff_two, one_sib, normed_two)
    two_own, two_sib = ff_weights(ff_two)
    normed_two = after(normed_two, two_own)
    outs = feed_forward(normed_two, cot, n2t, cott, one_own, one_sib, bias_rows[0][0], bias_rows[1][0], TILE)
    one_own_grad, one_sib_grad, *one_sums = outs[2:]
    one_sent = tensor_swap(one_sib_grad, 1)
    outs = feed_forward(normed_two, cot, n2t, cott, two_own, two_sib, bias_rows[0][1], bias_rows[1][1], TILE, outs[:2])
    out_keep, out_send, grad_keep, grad_send, two_own_grad, two_sib_grad, *two_sums = outs

    grad_got = tensor_swap(grad_send, 2)
    two_sent = tensor_swap(two_sib_grad, 1)
    scatter_one = Scatter(one_own_grad, after(one_sent, grad_send))
    scatter_one.advance()
    scatter_two = Scatter(two_own_grad, two_sent)
    sends = scatter_two.prepare()
    grad_got, out_send, sends = settle_scatters([scatter_one], grad_got, out_send, sends)
    scatter_two.sends = sends
    scatter_two.launch()
    scatter_one.advance()
    out_got = tensor_swap(out_send, 2)
    inner_keep, grad_branch, gbt, vectors_two = turn(inner, grad_keep, grad_got, cot, gain_two)
    part, other_grad, other_sums = attn_backward(grad_branch, gbt, n1t, attn_w[1], saved[1], mask, width)
    part, out_got, other_grad = settle_scatters([scatter_one, scatter_two], part, out_got, other_grad)
    attn_sent = tensor_swap(other_grad, 1)
    scatter_one.rest()
    scatter_two.advance()
    one_keep, one_send, own_grad, own_sums = attn_backward(grad_branch, gbt, n1t, attn_w[0], saved[0], mask, width, part)
    own_grad, one_send, one_keep, attn_sent, own_sums = settle_scatters([scatter_one, scatter_two], own_grad, one_send, one_keep, attn_sent, own_sums)
    scatter_attn = Scatter(own_grad, attn_sent)
    sends = scatter_attn.prepare()
    scatter_attn.launch()
    one_got = tensor_swap(one_send, 2)
    scatter_two.rest()

    one_keep, out_got, bias_sums = after((one_keep, out_got, (one_sums, two_sums, own_sums, other_sums)), sends)
    one_sums, two_sums, own_sums, other_sums = bias_sums
    xhat_one, inverse_one = norm_parts(wide(low_rows))
    v_gain_one = jnp.sum(one_keep * xhat_one, axis=0, keepdims=True)
    v_shift_one = jnp.sum(one_keep, axis=0, keepdims=True)
    small = jnp.concatenate([v_gain_one, v_shift_one, vectors_two], axis=0)

    def bias_pair(up_sums, sums):
        first_row = jnp.pad(jnp.concatenate(up_sums, axis=1), ((0, 0), (0, model - hidden_width)))
        second_row = jnp.concatenate([sums[:1, :width], sums[:1, 2 * width :], jnp.zeros((1, model - 2 * width), jnp.float32)], axis=1)
        return jnp.concatenate([first_row, second_row], axis=0)

    from_sib = tensor_swap(jnp.concatenate([small, bias_pair((one_sums[1], two_sums[1]), other_sums)], axis=0), 1)
    small = small + from_sib[:6]
    from_y = tensor_swap(small, 2)
    own_biases = bias_pair((one_sums[0], two_sums[0]), own_sums) + from_sib[6:]
    small = jnp.concatenate([small + from_y, own_biases], axis=0)
    out_half = inner[: 2 * rows] + (out_keep + wide(out_got) + down_bias)
    out_low = low(out_half)
    one_got, out_low, small = settle_scatters([scatter_two, scatter_attn], one_got, out_low, small)

    sends = scatter_attn.prepare()
    scatter_attn.launch()
    one_got, out_low, small = after((one_got, out_low, small), sends)
    out_other = tensor_swap(out_low[rows:], 1)
    own = slice(0, 2 * rows)
    grad_normed_one = one_keep[own] + wide(one_got)
    clip_half = inner_keep + norm_back(grad_normed_one, xhat_one[own], inverse_one[own], gain_one)
    clip_other = tensor_swap(clip_half[rows:], 1)
    for mask_bit in masks:
        small = small + data_swap(small, mask_bit)
    ff_parts = scatter_one.finish() + scatter_two.finish()
    out_other, clip_half, clip_other, small, ff_parts = settle_scatters([scatter_attn], out_other, clip_half, clip_other, small, ff_parts)
    sends = scatter_attn.prepare()
    scatter_attn.launch()
    scatter_attn.rest()
    out_other, clip_half, clip_other, small, ff_parts = after((out_other, clip_half, clip_other, small, ff_parts), sends)
    output = order_pair(out_low[:rows], out_other, core)
    clip_grad = order_pair(clip_half[:rows], clip_other, core)
    vector_own = lax.dynamic_slice_in_dim(small[:6], lax.axis_index("dp") * depth, depth, axis=1)
    joined = jnp.concatenate(ff_parts, axis=1)
    ups = [joined[:, 2 * i : 2 * i + TILE] for i in range(0, hidden_width, TILE)]
    downs = [joined[:, 2 * i + TILE : 2 * i + 2 * TILE] for i in range(0, hidden_width, TILE)]
    q_grad, k_grad, v_grad, out_grad = scatter_attn.total(True, False, True)
    return (
        output,
        clip_grad,
        vector_own[0],
        vector_own[1],
        q_grad,
        small[7, :width],
        k_grad,
        v_grad,
        small[7, width : 2 * width],
        out_grad.T,
        vector_own[2],
        vector_own[3],
        vector_own[4],
        jnp.concatenate(ups, axis=1),
        small[6, :hidden_width],
        jnp.concatenate(downs, axis=1).T,
        vector_own[5],
    )


def solution(mesh):
    rows_spec = P("dp", "tensor", None)
    data, tensor = P("dp"), P("tensor")
    wide_spec, tall_spec = P("dp", "tensor"), P("tensor", "dp")
    placed = (
        rows_spec,
        data,
        data,
        data,
        wide_spec,
        tensor,
        wide_spec,
        wide_spec,
        tensor,
        tall_spec,
        data,
        data,
        data,
        wide_spec,
        tensor,
        tall_spec,
        data,
        rows_spec,
    )
    outs = (
        rows_spec,
        rows_spec,
        data,
        data,
        wide_spec,
        tensor,
        wide_spec,
        wide_spec,
        tensor,
        tall_spec,
        data,
        data,
        data,
        wide_spec,
        tensor,
        tall_spec,
        data,
    )
    return jax.shard_map(shards, mesh=mesh, in_specs=placed, out_specs=outs, check_vma=False)
```

```python
import jax
import jax.numpy as jnp
from jax import lax
from jax.experimental import pallas as pl
from jax.experimental.pallas import tpu as pltpu
from jax.sharding import PartitionSpec as P

HEAD_DIM = 80
norm_eps = 1e-05
VEC_ROWS = 8
TILE = 256
FIRST_TILES = 2
VMEM_LIMIT = 60 << 20


def low(values):
    return values.astype(jnp.bfloat16)


def wide(values):
    return values.astype(jnp.float32)


def mm(left, right):
    return jnp.dot(left, right, preferred_element_type=jnp.float32)


def mm_left(left, right):
    return lax.dot_general(left, right, (((0,), (0,)), ((), ())), preferred_element_type=jnp.float32)


def mm_right(left, right):
    return lax.dot_general(left, right, (((1,), (1,)), ((), ())), preferred_element_type=jnp.float32)


def norm_parts(values):
    center = values - jnp.mean(values, axis=-1, keepdims=True)
    spread = jnp.mean(center * center, axis=-1, keepdims=True)
    inverse = lax.rsqrt(spread + norm_eps)
    return center * inverse, inverse


def norm_back(grad, xhat, inverse, gain):
    scaled = grad * gain
    first = jnp.mean(scaled, axis=-1, keepdims=True)
    second = jnp.mean(scaled * xhat, axis=-1, keepdims=True)
    return (scaled - first - xhat * second) * inverse


def gelu_pair(pre):
    half = 0.5 * (1.0 + lax.erf(pre * (0.5 ** 0.5)))
    slope = half + pre * jnp.exp(-0.5 * pre * pre) * 0.3989422804014327
    return pre * half, slope


def tensor_swap(values, mask):
    size = lax.axis_size("tensor")
    return lax.ppermute(values, "tensor", [(i, i ^ mask) for i in range(size)])


def data_swap(values, mask):
    size = lax.axis_size("dp")
    return lax.ppermute(values, "dp", [(i, i ^ mask) for i in range(size)])


def masks_of(size):
    masks = []
    while size > 1:
        size //= 2
        masks.append(size)
    return masks


def pin(values, *others):
    return lax.optimization_barrier((values, others))[0]


def after(values, *others):
    return pin(values, *others) if others else values


def vmem(count):
    return [pl.BlockSpec(memory_space=pltpu.VMEM)] * count


def tiny_cost():
    return pl.CostEstimate(flops=1024, bytes_accessed=1024, transcendentals=0)


def join_body(plan, inputs, *refs):
    sources, outs, sems = refs[:inputs], refs[inputs:-1], refs[-1]
    copies = []
    for k, (source, start, columns, out, row) in enumerate(plan):
        count = sources[source].shape[0]
        origin = sources[source]
        if columns != origin.shape[2]:
            origin = origin.at[:, :, pl.ds(start, columns)]
        copies.append(pltpu.make_async_copy(origin, outs[out].at[pl.ds(row, count)], sems.at[k]))
    for item in copies:
        item.start()
    for item in copies:
        item.wait()


def join(sources, plan, shapes):
    return pl.pallas_call(
        lambda *refs: join_body(plan, len(sources), *refs),
        in_specs=[pl.BlockSpec(memory_space=pl.ANY)] * len(sources),
        out_specs=vmem(len(shapes)),
        out_shape=[jax.ShapeDtypeStruct(shape, jnp.bfloat16) for shape in shapes],
        compiler_params=pltpu.CompilerParams(vmem_limit_bytes=16 << 20),
        scratch_shapes=[pltpu.SemaphoreType.DMA((len(plan),))],
        cost_estimate=tiny_cost(),
        name="join",
    )(*sources)


class Gather:
    def __init__(self, shard):
        self.masks = masks_of(lax.axis_size("dp"))
        self.held, self.fresh = [shard[None]], []
        self.order = [[0], [0]]

    def extend(self, side, mask):
        self.order[side] = self.order[side] + [item ^ mask for item in self.order[side]]

    def early(self):
        for mask in self.masks[:-2]:
            if self.fresh:
                self.held = [jnp.concatenate([self.held[0], self.fresh[0]], axis=0)]
            self.fresh = [data_swap(self.held[0], mask)]
            self.extend(0, mask)
            self.extend(1, mask)

    def send(self, masks):
        self.fresh = [data_swap(self.held[side], masks[side]) for side in range(2)]
        for side in range(2):
            self.extend(side, masks[side])

    def second(self):
        count, rows, columns = self.held[0].shape
        half = columns // 2
        plan = [(k, side * half, half, side, k * count) for k in range(2) for side in range(2)]
        self.held = join(self.held + self.fresh, plan, [(2 * count, rows, half)] * 2)
        self.send([self.masks[-2], self.masks[-1]])

    def third(self):
        count, rows, half = self.held[0].shape
        plan = [(2 * k + side, 0, half, side, k * count) for k in range(2) for side in range(2)]
        self.held = join(list(self.held) + self.fresh, plan, [(2 * count, rows, half)] * 2)
        self.send([self.masks[-1], self.masks[-2]])


def settle(*items):
    gathers = [item for item in items if isinstance(item, Gather)]
    others = [item for item in items if not isinstance(item, Gather)]
    arrays = [(item.held, item.fresh) for item in gathers]
    arrays, others = lax.optimization_barrier((arrays, others))
    for item, (held, fresh) in zip(gathers, arrays):
        item.held, item.fresh = list(held), list(fresh)
    return others


def place_body(gathered, depth, extra, me_ref, *refs):
    pieces, outs, sems = refs[:4], refs[4:-1], refs[-1]
    me = me_ref[0]
    copies = []
    for side in range(2):
        held, fresh = pieces[2 * side : 2 * side + 2]
        columns = held.shape[2]
        for position, item in enumerate(gathered.order[side]):
            count = held.shape[0]
            piece, row = (held, position) if position < count else (fresh, position - count)
            target = outs[0].at[me ^ item, pl.ds(0, depth), pl.ds(side * columns, columns)]
            source = piece.at[row, pl.ds(0, depth)] if extra else piece.at[row]
            copies.append(pltpu.make_async_copy(source, target, sems.at[len(copies)]))
            if extra and side == 0:
                source = piece.at[row, pl.ds(depth, extra)]
                copies.append(pltpu.make_async_copy(source, outs[-1].at[me ^ item], sems.at[len(copies)]))
    for item in copies:
        item.start()
    for item in copies:
        item.wait()


def place_blocks(gathered, depth, extra=0):
    size = lax.axis_size("dp")
    pieces = [gathered.held[0], gathered.fresh[0], gathered.held[1], gathered.fresh[1]]
    columns = pieces[0].shape[2]
    if extra and depth % 8:
        whole = place_blocks(gathered, depth + extra)[0]
        return [whole[:, :depth], whole[:, depth:, :columns]]
    me = lax.axis_index("dp").reshape(1)
    shapes = [jax.ShapeDtypeStruct((size, depth, 2 * columns), jnp.bfloat16)]
    if extra:
        shapes.append(jax.ShapeDtypeStruct((size, extra, columns), jnp.bfloat16))
    return pl.pallas_call(
        lambda *refs: place_body(gathered, depth, extra, *refs),
        in_specs=[pl.BlockSpec(memory_space=pltpu.SMEM)] + [pl.BlockSpec(memory_space=pl.ANY)] * 4,
        out_specs=vmem(len(shapes)),
        out_shape=shapes,
        compiler_params=pltpu.CompilerParams(vmem_limit_bytes=VMEM_LIMIT),
        scratch_shapes=[pltpu.SemaphoreType.DMA((3 * size if extra else 2 * size,))],
        cost_estimate=tiny_cost(),
        name="place",
    )(me, *pieces)


def spread(number, masks):
    return sum(((number >> k) & 1) * mask for k, mask in enumerate(masks))


def compress(number, masks):
    return sum(((number // mask) & 1) << k for k, mask in enumerate(masks))


def sum_body(plan, counts, merged, split, me_ref, *refs):
    operands = 1 + max(item[0] for side in plan for item in side)
    outs = refs[operands : -sum(counts) - 1]
    buffers, sems = refs[-sum(counts) - 1 : -1], refs[-1]
    me = me_ref[0]
    copies = []
    k = 0
    for side in plan:
        for operand, start, index in side:
            rows, columns = buffers[k].shape[1:]
            for number in range(buffers[k].shape[0]):
                source = refs[operand].at[index(number, me), :, pl.ds(start, columns)]
                copies.append(pltpu.make_async_copy(source, buffers[k].at[number], sems.at[len(copies)]))
                copies[-1].start()
            k += 1
    for item in copies:
        item.wait()
    k = 0
    for side, count in enumerate(counts):
        total = wide(buffers[k][...])
        for buffer in buffers[k + 1 : k + count]:
            total = total + wide(buffer[...])
        k += count
        columns = total.shape[-1]
        if split:
            for part in range(2):
                outs[2 * side + part][...] = total[0, :, part * columns // 2 : (part + 1) * columns // 2]
        elif merged:
            outs[0][:, :, side * columns : (side + 1) * columns] = total.astype(outs[0].dtype)
        else:
            outs[side][...] = total.astype(outs[side].dtype)


def scatter_masks(size):
    masks = masks_of(size)[::-1]
    return [masks, [masks[1], masks[0]] + masks[2:]]


class Scatter:
    def __init__(self, own, sends=None):
        self.sends = sends
        self.size = lax.axis_size("dp")
        self.half = own.shape[1] // 2
        self.depth = own.shape[0] // self.size
        self.own = own.reshape(self.size, self.depth, own.shape[1])
        self.masks = scatter_masks(self.size)
        self.gots = []
        self.step = 0

    def remaining(self, side, step):
        return sorted(set(self.masks[side]) - set(self.masks[side][: step + 1]))

    def total(self, final, merged, split=False):
        step = self.step
        last = len(self.masks[0]) == step
        count = 1 if last else self.size >> (step + 1)
        operands = [self.own]
        for got in self.gots:
            operands += got
        plan = []
        for side in range(2):
            rest = [] if last else self.remaining(side, step)
            before = sum(self.masks[side][:step])
            flip = 0 if last else self.masks[side][step]

            def block(number, me, rest=rest, before=before, flip=flip):
                return (me & before) | ((me ^ flip) & flip) | spread(number, rest)

            terms = [(0, side * self.half, block)]
            operand = 1
            for number, got in enumerate(self.gots):
                kept = self.remaining(side, number)
                which, start = (operand, side * self.half) if len(got) == 1 else (operand + side, 0)
                terms.append((which, start, lambda item, me, block=block, kept=kept: compress(block(item, me), kept)))
                operand += len(got)
            plan.append(terms)
        counts = [len(item) for item in plan]
        dtype = jnp.float32 if final else jnp.bfloat16
        columns = 2 * self.half if merged else self.half
        outs = [jax.ShapeDtypeStruct((count, self.depth, columns), dtype)] * (1 if merged else 2)
        if split:
            outs = [jax.ShapeDtypeStruct((self.depth, self.half // 2), dtype)] * 4
        return pl.pallas_call(
            lambda *refs: sum_body(plan, counts, merged, split, *refs),
            in_specs=[pl.BlockSpec(memory_space=pltpu.SMEM)] + [pl.BlockSpec(memory_space=pl.ANY)] * len(operands),
            out_specs=vmem(len(outs)),
            out_shape=outs,
            scratch_shapes=[pltpu.VMEM((count, self.depth, self.half), jnp.bfloat16)] * sum(counts)
            + [pltpu.SemaphoreType.DMA((count * sum(counts),))],
            compiler_params=pltpu.CompilerParams(vmem_limit_bytes=VMEM_LIMIT),
            cost_estimate=tiny_cost(),
            name="sum_blocks",
        )(lax.axis_index("dp").reshape(1), *operands)

    def prepare(self):
        self.sends = self.total(False, self.step >= 2)
        return self.sends

    def launch(self):
        masks = [self.masks[side][self.step] for side in range(len(self.sends))]
        self.gots = self.gots + [[data_swap(send, mask) for send, mask in zip(self.sends, masks)]]
        self.step += 1

    def advance(self):
        if self.step > 0 or self.sends is None:
            self.prepare()
        self.launch()

    def rest(self):
        while self.step < len(self.masks[0]):
            self.advance()

    def finish(self):
        return [item[0] for item in self.total(True, False)]


def settle_scatters(scatters, *others):
    gots, others = lax.optimization_barrier(([item.gots for item in scatters], others))
    for item, got in zip(scatters, gots):
        item.gots = got
    return others


def ff_body(first, tiles, half, *refs):
    n2, cot, own_up, own_down, sib_up, sib_down, own_b, sib_b = refs[:8]
    if first:
        acc_b, acc_g, own_acts, sib_acts = refs[8:]
    else:
        prev_b, prev_g, out_keep, out_send, grad_keep, grad_send, own_acts, sib_acts, acc_b, acc_g = refs[8:]
    side, tile = pl.program_id(0), pl.program_id(1)

    @pl.when((side == 0) & (tile == 0))
    def _():
        if first:
            acc_b[...] = jnp.zeros_like(acc_b)
            acc_g[...] = jnp.zeros_like(acc_g)
        else:
            acc_b[...] = prev_b[...]
            acc_g[...] = prev_g[...]

    def step(up_ref, down_ref, bias, acts):
        up, down = up_ref[...], down_ref[...]
        width = up.shape[1]
        pre = mm(n2[...], up) + wide(bias[...])
        act, slope = gelu_pair(pre)
        hidden = low(act)
        grad_pre = low(mm(cot[...], down) * slope)
        acc_b[...] += mm_right(hidden, down)
        acc_g[...] += mm_right(grad_pre, up)
        acts[:, :width] = grad_pre
        acts[:, width:] = hidden

    @pl.when(side == 0)
    def _():
        step(sib_up, sib_down, sib_b, sib_acts)

    @pl.when(side == 1)
    def _():
        step(own_up, own_down, own_b, own_acts)

    if not first:

        @pl.when((side == 1) & (tile == tiles - 1))
        def _():
            out_keep[...] = acc_b[:half]
            out_send[...] = low(acc_b[half:])
            grad_keep[...] = acc_g[...]
            grad_send[:half] = low(acc_g[half:])
            grad_send[half:] = low(acc_g[:half])


def side_specs(tiles):
    def second(shape, start=0):
        return pl.BlockSpec(shape, lambda s, i: (0, start + jnp.where(s == 1, i, 0)))

    def initial(shape, start=0):
        return pl.BlockSpec(shape, lambda s, i: (0, start + jnp.where(s == 0, i, tiles - 1)))

    return second, initial


def const_spec(shape):
    return pl.BlockSpec(shape, lambda s, i: (0, 0), pipeline_mode=pl.Buffered(1))


def feed_forward(n2, cot, own_w, sib_w, own_b, sib_b, tile, previous=()):
    rows, model = n2.shape
    hidden = own_b.shape[1]
    tiles = hidden // tile
    first = not previous
    half = rows // 2
    second, initial = side_specs(tiles)
    in_specs = [const_spec(n2.shape)] * 2
    in_specs += [second((model, tile)), second((model, tile), tiles), initial((model, tile)), initial((model, tile), tiles)]
    in_specs += [second((1, tile)), initial((1, tile))]
    in_specs += [const_spec(item.shape) for item in previous]
    operands = [n2, cot, own_w, own_w, sib_w, sib_w, own_b, sib_b, *previous]
    full = jax.ShapeDtypeStruct((rows, model), jnp.float32)
    acts = jax.ShapeDtypeStruct((rows, 2 * hidden), jnp.bfloat16)
    shapes = [full, full]
    scratch = []
    if not first:
        shapes = [
            jax.ShapeDtypeStruct((half, model), jnp.float32),
            jax.ShapeDtypeStruct((half, model), jnp.bfloat16),
            full,
            jax.ShapeDtypeStruct((rows, model), jnp.bfloat16),
        ]
        scratch = [pltpu.VMEM((rows, model), jnp.float32)] * 2
    specs = [const_spec(item.shape) for item in shapes]
    specs += [second((rows, 2 * tile)), initial((rows, 2 * tile))]
    return pl.pallas_call(
        lambda *refs: ff_body(first, tiles, half, *refs),
        grid=(2, tiles),
        in_specs=in_specs,
        out_specs=specs,
        out_shape=shapes + [acts, acts],
        scratch_shapes=scratch,
        compiler_params=pltpu.CompilerParams(vmem_limit_bytes=VMEM_LIMIT),
        cost_estimate=tiny_cost(),
        name="feed_forward",
    )(*operands)


def weight_grads_body(n2t, sib_n2t, cott, sib_cott, acts, sib_acts, grads, sums):
    width = acts.shape[1] // 2
    grads[:, :width] = low(mm(n2t[...], acts[:, :width]) + mm(sib_n2t[...], sib_acts[:, :width]))
    grads[:, width:] = low(mm(cott[...], acts[:, width:]) + mm(sib_cott[...], sib_acts[:, width:]))
    total = jnp.sum(wide(acts[:, :width]), axis=0, keepdims=True)
    sums[...] = total + jnp.sum(wide(sib_acts[:, :width]), axis=0, keepdims=True)


def weight_grads(left, acts, sib_acts, tile):
    model, rows = left[0].shape
    tiles = acts.shape[1] // (2 * tile)
    const = pl.BlockSpec((model, rows), lambda i: (0, 0), pipeline_mode=pl.Buffered(1))
    return pl.pallas_call(
        weight_grads_body,
        grid=(tiles,),
        in_specs=[const] * 4 + [pl.BlockSpec((rows, 2 * tile), lambda i: (0, i))] * 2,
        out_specs=[pl.BlockSpec((model, 2 * tile), lambda i: (0, i)), pl.BlockSpec((1, tile), lambda i: (0, i))],
        out_shape=[
            jax.ShapeDtypeStruct((model, acts.shape[1]), jnp.bfloat16),
            jax.ShapeDtypeStruct((1, acts.shape[1] // 2), jnp.float32),
        ],
        compiler_params=pltpu.CompilerParams(vmem_limit_bytes=VMEM_LIMIT),
        cost_estimate=tiny_cost(),
        name="weight_grads",
    )(*left, acts, sib_acts)


def prepare_body(*refs):
    vectors, (w_query, w_key, w_value, w_out_t), out = refs[:6], refs[6:10], refs[10]
    depth, width = w_query.shape
    out[:depth] = jnp.concatenate([w_query[...], w_key[...], w_value[...], w_out_t[...]], axis=1)
    out[depth:] = jnp.zeros_like(out[depth:])
    for k, vector in enumerate(vectors):
        out[depth + k : depth + k + 1, :depth] = vector[...].reshape(1, depth)


def prepare(vectors, weights):
    depth, width = weights[0].shape
    return pl.pallas_call(
        prepare_body,
        in_specs=vmem(10),
        out_specs=pl.BlockSpec(memory_space=pltpu.VMEM),
        out_shape=jax.ShapeDtypeStruct((depth + VEC_ROWS, 4 * width), jnp.bfloat16),
        compiler_params=pltpu.CompilerParams(vmem_limit_bytes=VMEM_LIMIT),
        cost_estimate=tiny_cost(),
        name="prepare",
    )(*vectors, *weights)


def assemble_body(half, mine, other_rows, other_cot, rows, cot, cot_t):
    rows[:half] = mine[:half]
    rows[half:] = other_rows[...]
    cot[:half] = mine[half:]
    cot[half:] = other_cot[...]
    cot_t[...] = cot[...].T


def assemble(mine, other_rows, other_cot):
    rows, model = mine.shape
    shape = jax.ShapeDtypeStruct((rows, model), jnp.bfloat16)
    return pl.pallas_call(
        lambda *refs: assemble_body(rows // 2, *refs),
        in_specs=vmem(3),
        out_specs=vmem(3),
        out_shape=[shape, shape, jax.ShapeDtypeStruct((model, rows), jnp.bfloat16)],
        compiler_params=pltpu.CompilerParams(vmem_limit_bytes=VMEM_LIMIT),
        cost_estimate=tiny_cost(),
        name="assemble",
    )(mine, other_rows, other_cot)


def dot_t(left, right):
    return lax.dot_general(left, right, (((0,), (0,)), ((), ())), preferred_element_type=jnp.float32)


def norm_rows(values, gain, shift):
    xhat, inverse = norm_parts(values)
    return low(xhat * gain + shift)


def fill_mask(where, mask):
    count = mask.shape[0] // 4
    for k in range(4):
        position = (where[0] ^ k) * count + lax.broadcasted_iota(jnp.int32, (count, 1), 0)
        mask[k * count : (k + 1) * count] = (position < where[1]).astype(jnp.float32)


def attn_head(joined, head, width, mask):
    scale = HEAD_DIM ** (-0.5)
    begin = pl.multiple_of(head * HEAD_DIM, 16)
    query = joined[pl.ds(begin, HEAD_DIM), :]
    keys = joined[pl.ds(pl.multiple_of(width + begin, 16), HEAD_DIM), :]
    values = joined[pl.ds(pl.multiple_of(2 * width + begin, 16), HEAD_DIM), :]
    scores = jnp.where(mask[...] > 0.5, dot_t(keys, query) * scale, -1000000000.0)
    return begin, query, keys, values, scores


def attn_forward_body(first, width, *refs):
    if first:
        where, x, vectors, weights, bias, n1, n1t, joined, mixed, totals, part, mask = refs
        n1[...] = norm_rows(wide(x[...]), vectors[0:1], vectors[1:2])
        n1t[...] = n1[...].T
    else:
        where, n1, previous, weights, bias, joined, mixed, totals, part, send_one, send_two, mask = refs
    fill_mask(where, mask)
    joined[...] = low(mm(n1[...], weights[:, : 3 * width]) + bias[...]).T

    def one(head, carry):
        begin, query, keys, values, scores = attn_head(joined, head, width, mask)
        top = jnp.max(scores, axis=0, keepdims=True)
        expo = jnp.exp(scores - top)
        total = jnp.sum(expo, axis=0, keepdims=True)
        probs = low(expo * (1.0 / total))
        mixed[pl.ds(begin, HEAD_DIM), :] = low(mm(values, probs))
        totals[pl.ds(head, 1), :] = top + jnp.log(total)
        return carry

    lax.fori_loop(0, width // HEAD_DIM, one, 0)
    term = mm_right(mixed[...].T, weights[:, 3 * width :])
    if first:
        part[...] = term
    else:
        term = previous[...] + term
        half = term.shape[0] // 2
        part[...] = term
        send_one[...] = low(term[half:])
        send_two[...] = low(term[:half])


def attn_forward(where, head_in, weights, bias, width, first):
    rows, model = head_in[0].shape
    low_shape = lambda *shape: jax.ShapeDtypeStruct(shape, jnp.bfloat16)
    wide_shape = lambda *shape: jax.ShapeDtypeStruct(shape, jnp.float32)
    shapes = [low_shape(3 * width, rows), low_shape(width, rows), wide_shape(width // HEAD_DIM, rows), wide_shape(rows, model)]
    shapes = [low_shape(rows, model), low_shape(model, rows)] + shapes if first else shapes + [low_shape(rows // 2, model)] * 2
    operands = [where] + list(head_in) + [weights, bias]
    return pl.pallas_call(
        lambda *refs: attn_forward_body(first, width, *refs),
        in_specs=[pl.BlockSpec(memory_space=pltpu.SMEM)] + vmem(len(operands) - 1),
        out_specs=vmem(len(shapes)),
        out_shape=shapes,
        scratch_shapes=[pltpu.VMEM((rows, 1), jnp.float32)],
        compiler_params=pltpu.CompilerParams(vmem_limit_bytes=VMEM_LIMIT),
        cost_estimate=tiny_cost(),
        name="attn_forward",
    )(*operands)


def attn_backward_body(first, width, size, *refs):
    where, gb, weights, joined, totals = refs[:5]
    half = gb.shape[0] // 2
    if first:
        mixed, part, acts, gmt, djoined, mask = refs[5:]
    else:
        late, outs, scratch = refs[5:12], refs[12:-13], refs[-13:]
        gmt, djoined, mask, *buffers, keep, send, sems = scratch
        grads = outs[2]
        copies = [pltpu.make_async_copy(item, buffer, sems.at[k]) for k, (item, buffer) in enumerate(zip(late, buffers))]
        for item in copies:
            item.start()
        previous, gbt, sib_gbt, n1t, sib_n1t, mixed, sib_acts = buffers
    scale = HEAD_DIM ** (-0.5)
    fill_mask(where, mask)
    gmt[...] = low(mm(gb[...], weights[:, 3 * width :])).T

    def one(head, carry):
        begin, query, keys, values, scores = attn_head(joined, head, width, mask)
        probs = jnp.exp(scores - totals[pl.ds(head, 1), :])
        gm = gmt[pl.ds(begin, HEAD_DIM), :]
        grad_probs = dot_t(values, gm)
        delta = jnp.sum(grad_probs * probs, axis=0, keepdims=True)
        grad_scores = low(probs * (grad_probs - delta))
        djoined[pl.ds(begin, HEAD_DIM), :] = low(mm(keys, grad_scores) * scale)
        djoined[pl.ds(pl.multiple_of(width + begin, 16), HEAD_DIM), :] = low(mm_right(query, grad_scores) * scale)
        djoined[pl.ds(pl.multiple_of(2 * width + begin, 16), HEAD_DIM), :] = low(mm_right(gm, low(probs)))
        return carry

    lax.fori_loop(0, width // HEAD_DIM, one, 0)
    if first:
        acts[: 3 * width] = djoined[...]
        acts[3 * width :] = mixed[...]
        part[...] = mm_right(djoined[...].T, weights[:, : 3 * width])
        return
    for item in copies:
        item.wait()
    term = previous[...] + mm_right(djoined[...].T, weights[:, : 3 * width])
    keep[...] = term
    send[...] = low(term[half:])
    copies = [pltpu.make_async_copy(keep, outs[0], sems.at[7]), pltpu.make_async_copy(send, outs[1], sems.at[8])]
    for item in copies:
        item.start()
    ones = jnp.ones((8, gb.shape[0]), jnp.bfloat16)
    outs[3][...] = mm_right(ones, djoined[...]) + mm_right(ones, sib_acts[: 3 * width])
    grad_qkv = low(mm_right(n1t[...], djoined[...]) + mm_right(sib_n1t[...], sib_acts[: 3 * width]))
    grad_out = low(mm_right(gbt[...], mixed[...]) + mm_right(sib_gbt[...], sib_acts[3 * width :]))
    if size:
        grads[:, :, : 3 * width] = grad_qkv.reshape(size, -1, 3 * width)
        grads[:, :, 3 * width :] = grad_out.reshape(size, -1, width)
        masks = scatter_masks(size)
        for side in range(2):
            mask = masks[side][0]
            rest = sorted(set(masks[side]) - {mask})
            for number in range(size // 2):
                block = ((where[2] ^ mask) & mask) | spread(number, rest)
                source = grads.at[block, :, pl.ds(side * 2 * width, 2 * width)]
                copies.append(pltpu.make_async_copy(source, outs[4 + side].at[number], sems.at[2 + 5 + len(copies)]))
                copies[-1].start()
    else:
        grads[:, : 3 * width] = grad_qkv
        grads[:, 3 * width :] = grad_out
    for item in copies:
        item.wait()


def attn_backward(where, gb, weights, saved, width, late=(), size=0):
    rows, model = gb.shape
    half = rows // 2
    first = not late
    joined, mixed, totals = saved
    operands = [where, gb, weights, joined, totals]
    specs = [pl.BlockSpec(memory_space=pltpu.SMEM)] + vmem(4)
    low_shape = lambda *shape: jax.ShapeDtypeStruct(shape, jnp.bfloat16)
    full = jax.ShapeDtypeStruct((rows, model), jnp.float32)
    scratch = [
        pltpu.VMEM((width, rows), jnp.bfloat16),
        pltpu.VMEM((3 * width, rows), jnp.bfloat16),
        pltpu.VMEM((rows, 1), jnp.float32),
    ]
    if first:
        operands.append(mixed)
        specs += vmem(1)
        shapes = [full, low_shape(4 * width, rows)]
        out_specs = vmem(2)
    else:
        previous, gbt, sib_gbt, n1t, sib_n1t, sib_acts = late
        late = [previous, gbt, sib_gbt, n1t, sib_n1t, mixed, sib_acts]
        operands += late
        specs += [pl.BlockSpec(memory_space=pl.ANY)] * len(late)
        scratch += [pltpu.VMEM(item.shape, item.dtype) for item in late]
        scratch += [pltpu.VMEM((rows, model), jnp.float32), pltpu.VMEM((half, model), jnp.bfloat16)]
        scratch += [pltpu.SemaphoreType.DMA((len(late) + 2 + size,))]
        grads = low_shape(size, model // size, 4 * width) if size else low_shape(model, 4 * width)
        shapes = [full, low_shape(half, model), grads, jax.ShapeDtypeStruct((8, 3 * width), jnp.float32)]
        out_specs = [pl.BlockSpec(memory_space=pl.ANY)] * 2 + vmem(2)
        if size:
            shapes += [low_shape(size // 2, model // size, 2 * width)] * 2
            out_specs += [pl.BlockSpec(memory_space=pl.ANY)] * 2
    return pl.pallas_call(
        lambda *refs: attn_backward_body(first, width, size, *refs),
        in_specs=specs,
        out_specs=out_specs,
        out_shape=shapes,
        scratch_shapes=scratch,
        compiler_params=pltpu.CompilerParams(vmem_limit_bytes=VMEM_LIMIT),
        cost_estimate=tiny_cost(),
        name="attn_backward",
    )(*operands)


def middle_body(x, part, got_one, got_two, vectors, inner, n2, n2t):
    got = jnp.where(pl.program_id(0) < 2, wide(got_one[...]), wide(got_two[...]))
    value = wide(x[...]) + (part[...] + got + vectors[2:3])
    inner[...] = value
    n2[...] = norm_rows(value, vectors[3:4], vectors[4:5])
    n2t[...] = n2[...].T


def row_spec(block, model):
    return pl.BlockSpec((block, model), lambda i: (i, 0))


def middle(x, part, got_one, got_two, vectors):
    rows, model = x.shape
    block = rows // 4
    shapes = [
        jax.ShapeDtypeStruct((rows, model), jnp.float32),
        jax.ShapeDtypeStruct((rows, model), jnp.bfloat16),
        jax.ShapeDtypeStruct((model, rows), jnp.bfloat16),
    ]
    return pl.pallas_call(
        middle_body,
        grid=(4,),
        in_specs=[row_spec(block, model)] * 2
        + [pl.BlockSpec((block, model), lambda i: (jnp.minimum(i, 1), 0)), pl.BlockSpec((block, model), lambda i: (jnp.maximum(i - 2, 0), 0))]
        + [pl.BlockSpec(vectors.shape, lambda i: (0, 0))],
        out_specs=[row_spec(block, model)] * 2 + [pl.BlockSpec((model, block), lambda i: (0, i))],
        out_shape=shapes,
        compiler_params=pltpu.CompilerParams(vmem_limit_bytes=VMEM_LIMIT),
        cost_estimate=tiny_cost(),
        name="middle",
    )(x, part, got_one, got_two, vectors)


def turn_body(inner, grad, got, cot, vectors, keep, gb, gbt, sums):
    step = pl.program_id(0)
    value = grad[...] + wide(got[...])
    xhat, inverse = norm_parts(inner[...])
    top = wide(cot[...])
    total = top + norm_back(value, xhat, inverse, vectors[3:4])
    gb[...] = low(total)
    gbt[...] = gb[...].T

    @pl.when(step < 2)
    def _():
        keep[...] = total
        parts = [jnp.sum(item, axis=0, keepdims=True) for item in (wide(low(total)), value * xhat, value, top)]
        joined = jnp.concatenate(parts, axis=0)
        sums[...] = jnp.where(step == 0, joined, sums[...] + joined)


def turn(inner, grad, got, cot, vectors):
    rows, model = inner.shape
    block = rows // 4
    shapes = [
        jax.ShapeDtypeStruct((rows // 2, model), jnp.float32),
        jax.ShapeDtypeStruct((rows, model), jnp.bfloat16),
        jax.ShapeDtypeStruct((model, rows), jnp.bfloat16),
        jax.ShapeDtypeStruct((4, model), jnp.float32),
    ]
    return pl.pallas_call(
        turn_body,
        grid=(4,),
        in_specs=[row_spec(block, model)] * 4 + [pl.BlockSpec(vectors.shape, lambda i: (0, 0))],
        out_specs=[
            pl.BlockSpec((block, model), lambda i: (jnp.minimum(i, 1), 0)),
            row_spec(block, model),
            pl.BlockSpec((model, block), lambda i: (0, i)),
            pl.BlockSpec((4, model), lambda i: (0, 0)),
        ],
        out_shape=shapes,
        compiler_params=pltpu.CompilerParams(vmem_limit_bytes=VMEM_LIMIT),
        cost_estimate=tiny_cost(),
        name="turn",
    )(inner, grad, got, cot, vectors)


def pick(pair, index):
    return lax.dynamic_index_in_dim(pair, index, axis=0, keepdims=False)


def order_pair(mine, other, core):
    return jnp.where(core == 0, jnp.stack([mine, other]), jnp.stack([other, mine]))


def shards(
    clips,
    lengths,
    norm1_gain,
    norm1_bias,
    w_query,
    bias_query,
    w_key,
    w_value,
    bias_value,
    w_out,
    bias_out,
    norm2_gain,
    norm2_bias,
    w_up,
    bias_up,
    w_down,
    bias_down,
    cotangent,
):
    rows = clips.shape[1]
    model = clips.shape[2]
    depth, width = w_query.shape
    hidden_width = w_up.shape[1]
    data_size = lax.axis_size("dp")
    place = lax.axis_index("tensor")
    core = place % 2
    masks = masks_of(data_size)

    vectors = (norm1_gain, norm1_bias, bias_out, norm2_gain, norm2_bias, bias_down)
    attn = Gather(prepare(vectors, (w_query, w_key, w_value, w_out.T)))
    attn.early()
    pair, cot_pair = after((clips, cotangent), attn.held)
    sent = jnp.concatenate([pick(pair, 1 - core), pick(cot_pair, 1 - core)], axis=0)
    got = tensor_swap(sent, 1)
    half_clip = jnp.concatenate([pick(pair, core), got[:rows]], axis=0)
    half_cot = jnp.concatenate([pick(cot_pair, core), got[rows:]], axis=0)
    other_clip = tensor_swap(half_clip, 2)
    local_bias = jnp.concatenate([bias_up, bias_query, bias_value])
    sib_bias = tensor_swap(local_bias.reshape(1, -1), 1)[0]
    cut = FIRST_TILES * TILE
    down_t = w_down.T
    ff_one = Gather(jnp.concatenate([w_up[:, :cut], down_t[:, :cut]], axis=1))
    ff_two = Gather(jnp.concatenate([w_up[:, cut:], down_t[:, cut:]], axis=1))
    where = jnp.stack([place, pick(lengths, core), lax.axis_index("dp")]).astype(jnp.int32)
    other_clip, half_cot, sib_bias, where = settle(attn, ff_one, ff_two, other_clip, half_cot, sib_bias, where)

    attn.second()
    other_cot = tensor_swap(half_cot, 2)
    biases = (local_bias.reshape(1, -1), sib_bias.reshape(1, -1))
    joined_biases = []
    for item in biases:
        item = wide(item[:, hidden_width:])
        joined_biases.append(jnp.concatenate([item[:, :width], jnp.zeros((1, width), jnp.float32), item[:, width:]], axis=1))
    joined_biases, other_clip = settle(attn, ff_one, joined_biases, other_clip)

    attn.third()
    ff_one.early()
    low_rows, cot, cott = assemble(jnp.concatenate([half_clip, half_cot], axis=0), other_clip, other_cot)
    low_rows, cot, cott = settle(attn, ff_one, ff_two, low_rows, cot, cott)

    attn_all, vector_all = place_blocks(attn, depth, VEC_ROWS)
    attn_own = attn_all.reshape(model, model)
    attn_sib = tensor_swap(attn_own, 1)
    attn_w = (attn_own, attn_sib)
    ff_one.second()
    ff_two.early()
    sib_cott = tensor_swap(cott, 1)
    vectors_full = wide(vector_all[:, :6, :depth].transpose(1, 0, 2).reshape(6, model))
    outs = attn_forward(where, (low_rows, vectors_full), attn_own, joined_biases[0], width, True)
    normed_one, n1t = outs[:2]
    saved = [outs[2:5]]
    outs = attn_forward(where, (normed_one, outs[5]), attn_sib, joined_biases[1], width, False)
    saved.append(outs[:3])
    part_keep, *part_send = outs[3:]

    def ff_weights(gathered):
        own_w = place_blocks(gathered, depth)[0].reshape(model, -1)
        return own_w, tensor_swap(own_w, 1)

    part_send, sib_cott, n1t = settle(ff_one, ff_two, part_send, sib_cott, n1t)
    got_one = tensor_swap(part_send[0], 2)
    ff_one.third()
    got_one, part_two, n1t = settle(ff_one, got_one, part_send[1], n1t)
    got_two = tensor_swap(part_two, 2)
    ff_two.second()
    one_own, one_sib = ff_weights(ff_one)
    sib_n1t = tensor_swap(n1t, 1)
    got_one, got_two, one_own = settle(ff_two, got_one, got_two, one_own)
    ff_two.third()
    inner, normed_two, n2t = middle(low_rows, part_keep, got_one, got_two, vectors_full)
    bias_rows = [[item[:, :cut], item[:, cut:hidden_width]] for item in biases]
    outs = feed_forward(normed_two, cot, one_own, one_sib, bias_rows[0][0], bias_rows[1][0], TILE)
    sums_so_far, own_acts, other_acts = outs[:2], outs[2], outs[3]
    sums_so_far, other_acts, n2t, sib_n1t = settle(ff_two, sums_so_far, other_acts, n2t, sib_n1t)
    sib_n2t = tensor_swap(n2t, 1)
    sib_acts = tensor_swap(other_acts, 1)
    two_own = place_blocks(ff_two, depth)[0].reshape(model, -1)
    sib_acts, sib_n2t, two_own = settle(sib_acts, sib_n2t, two_own)
    two_sib = tensor_swap(two_own, 1)
    left = (n2t, sib_n2t, cott, sib_cott)
    one_grad, one_sums = weight_grads(left, own_acts, sib_acts, TILE)
    scatter_one = Scatter(one_grad)
    scatter_one.advance()
    sums_so_far, two_sib = after((sums_so_far, two_sib), scatter_one.sends)
    outs = feed_forward(normed_two, cot, two_own, two_sib, bias_rows[0][1], bias_rows[1][1], TILE, sums_so_far)
    out_keep, out_send, grad_keep, grad_send, own_acts, other_acts = settle_scatters([scatter_one], *outs)

    grad_got = tensor_swap(grad_send, 2)
    sib_acts = tensor_swap(other_acts, 1)
    scatter_one.advance()
    two_grad, two_sums = weight_grads(left, own_acts, sib_acts, TILE)
    out_send, two_grad = settle_scatters([scatter_one], out_send, two_grad)
    scatter_two = Scatter(two_grad)
    scatter_two.advance()
    grad_got = after(grad_got, scatter_two.sends)
    inner_keep, grad_branch, gbt, vectors_two = turn(inner, grad_keep, grad_got, cot, vectors_full)
    grad_branch, gbt, out_send = settle_scatters([scatter_two], grad_branch, gbt, out_send)
    sib_gbt = tensor_swap(gbt, 1)
    out_got = tensor_swap(out_send, 2)
    scatter_one.rest()
    scatter_two.advance()
    grad_branch = after(grad_branch, scatter_one.sends, scatter_two.sends)
    part, other_acts = attn_backward(where, grad_branch, attn_w[1], saved[1], width)
    part, other_acts, sib_gbt, out_got = settle_scatters([scatter_one, scatter_two], part, other_acts, sib_gbt, out_got)
    sib_acts = tensor_swap(other_acts, 1)
    scatter_two.rest()
    late = (after(part, scatter_two.sends), gbt, sib_gbt, n1t, sib_n1t, sib_acts)
    direct = data_size if depth % 16 == 0 else 0
    one_keep, one_send, own_grad, own_sums, *first_sends = attn_backward(where, grad_branch, attn_w[0], saved[0], width, late, direct)
    scatter_attn = Scatter(own_grad.reshape(model, -1), first_sends or None)
    scatter_attn.advance()

    rest = (one_keep, out_got, one_sums, two_sums, own_sums, low_rows, vectors_full)
    one_keep, out_got, one_sums, two_sums, own_sums, low_rows, vectors_full = after(rest, scatter_attn.sends)
    gain_one, down_bias = vectors_full[0:1], vectors_full[5:6]
    xhat_one, inverse_one = norm_parts(wide(low_rows))
    v_gain_one = jnp.sum(one_keep * xhat_one, axis=0, keepdims=True)
    v_shift_one = jnp.sum(one_keep, axis=0, keepdims=True)
    small = jnp.concatenate([v_gain_one, v_shift_one, vectors_two], axis=0)
    first_row = jnp.pad(jnp.concatenate((one_sums, two_sums), axis=1), ((0, 0), (0, model - hidden_width)))
    spare = jnp.zeros((1, model - 2 * width), jnp.float32)
    second_row = jnp.concatenate([own_sums[:1, :width], own_sums[:1, 2 * width :], spare], axis=1)
    small = small + tensor_swap(small, 1)
    from_y = tensor_swap(small, 2)
    small = jnp.concatenate([small + from_y, first_row, second_row], axis=0)
    out_half = inner[: 2 * rows] + (out_keep + wide(out_got) + down_bias)
    out_low = low(out_half)
    scatter_one.gots = after(scatter_one.gots, scatter_attn.sends)
    one_parts = scatter_one.finish()
    out_low, small, one_parts = settle_scatters([scatter_two, scatter_attn], out_low, small, one_parts)

    scatter_attn.advance()
    out_low, small, one_send = after((out_low, small, one_send), scatter_attn.sends)
    one_got = tensor_swap(one_send, 2)
    out_other = tensor_swap(out_low[rows:], 1)
    for mask_bit in masks:
        small = small + data_swap(small, mask_bit)
    one_got, out_other, small = settle_scatters([scatter_attn], one_got, out_other, small)
    scatter_attn.rest()
    last = (one_got, out_other, small, scatter_two.gots)
    one_got, out_other, small, scatter_two.gots = after(last, scatter_attn.sends)
    own = slice(0, 2 * rows)
    grad_normed_one = one_keep[own] + wide(one_got)
    clip_half = inner_keep + norm_back(grad_normed_one, xhat_one[own], inverse_one[own], gain_one)
    clip_other = tensor_swap(clip_half[rows:], 1)
    ff_parts = one_parts + scatter_two.finish()
    output = order_pair(out_low[:rows], out_other, core)
    clip_grad = order_pair(clip_half[:rows], clip_other, core)
    vector_own = lax.dynamic_slice_in_dim(small[:6], lax.axis_index("dp") * depth, depth, axis=1)
    joined = jnp.concatenate(ff_parts, axis=1)
    ups = [joined[:, 2 * i : 2 * i + TILE] for i in range(0, hidden_width, TILE)]
    downs = [joined[:, 2 * i + TILE : 2 * i + 2 * TILE] for i in range(0, hidden_width, TILE)]
    q_grad, k_grad, v_grad, out_grad = scatter_attn.total(True, False, True)
    return (
        output,
        clip_grad,
        vector_own[0],
        vector_own[1],
        q_grad,
        small[7, :width],
        k_grad,
        v_grad,
        small[7, width : 2 * width],
        out_grad.T,
        vector_own[2],
        vector_own[3],
        vector_own[4],
        jnp.concatenate(ups, axis=1),
        small[6, :hidden_width],
        jnp.concatenate(downs, axis=1).T,
        vector_own[5],
    )


def solution(mesh):
    rows_spec = P("dp", "tensor", None)
    data, tensor = P("dp"), P("tensor")
    wide_spec, tall_spec = P("dp", "tensor"), P("tensor", "dp")
    placed = (
        rows_spec,
        data,
        data,
        data,
        wide_spec,
        tensor,
        wide_spec,
        wide_spec,
        tensor,
        tall_spec,
        data,
        data,
        data,
        wide_spec,
        tensor,
        tall_spec,
        data,
        rows_spec,
    )
    outs = (
        rows_spec,
        rows_spec,
        data,
        data,
        wide_spec,
        tensor,
        wide_spec,
        wide_spec,
        tensor,
        tall_spec,
        data,
        data,
        data,
        wide_spec,
        tensor,
        tall_spec,
        data,
    )
    return jax.shard_map(shards, mesh=mesh, in_specs=placed, out_specs=outs, check_vma=False)
```

```python
import jax
import jax.numpy as jnp
from jax import lax
from jax.experimental import pallas as pl
from jax.experimental.pallas import tpu as pltpu
from jax.sharding import PartitionSpec as P

HEAD_DIM = 80
norm_eps = 1e-05
VEC_ROWS = 8
TILE = 256
FIRST_TILES = 2
VMEM_LIMIT = 60 << 20


def low(values):
    return values.astype(jnp.bfloat16)


def wide(values):
    return values.astype(jnp.float32)


def mm(left, right):
    return jnp.dot(left, right, preferred_element_type=jnp.float32)


def mm_left(left, right):
    return lax.dot_general(left, right, (((0,), (0,)), ((), ())), preferred_element_type=jnp.float32)


def mm_right(left, right):
    return lax.dot_general(left, right, (((1,), (1,)), ((), ())), preferred_element_type=jnp.float32)


def norm_parts(values):
    center = values - jnp.mean(values, axis=-1, keepdims=True)
    spread = jnp.mean(center * center, axis=-1, keepdims=True)
    inverse = lax.rsqrt(spread + norm_eps)
    return center * inverse, inverse


def norm_back(grad, xhat, inverse, gain):
    scaled = grad * gain
    first = jnp.mean(scaled, axis=-1, keepdims=True)
    second = jnp.mean(scaled * xhat, axis=-1, keepdims=True)
    return (scaled - first - xhat * second) * inverse


def gelu_pair(pre):
    half = 0.5 * (1.0 + lax.erf(pre * (0.5 ** 0.5)))
    slope = half + pre * jnp.exp(-0.5 * pre * pre) * 0.3989422804014327
    return pre * half, slope


def tensor_swap(values, mask):
    size = lax.axis_size("tensor")
    return lax.ppermute(values, "tensor", [(i, i ^ mask) for i in range(size)])


def data_swap(values, mask):
    size = lax.axis_size("dp")
    return lax.ppermute(values, "dp", [(i, i ^ mask) for i in range(size)])


def masks_of(size):
    masks = []
    while size > 1:
        size //= 2
        masks.append(size)
    return masks


def pin(values, *others):
    return lax.optimization_barrier((values, others))[0]


def after(values, *others):
    return pin(values, *others) if others else values


def vmem(count):
    return [pl.BlockSpec(memory_space=pltpu.VMEM)] * count


def tiny_cost():
    return pl.CostEstimate(flops=1024, bytes_accessed=1024, transcendentals=0)


def join_body(plan, inputs, *refs):
    sources, outs, sems = refs[:inputs], refs[inputs:-1], refs[-1]
    copies = []
    for k, (source, start, columns, out, row) in enumerate(plan):
        count = sources[source].shape[0]
        origin = sources[source]
        if columns != origin.shape[2]:
            origin = origin.at[:, :, pl.ds(start, columns)]
        copies.append(pltpu.make_async_copy(origin, outs[out].at[pl.ds(row, count)], sems.at[k]))
    for item in copies:
        item.start()
    for item in copies:
        item.wait()


def join(sources, plan, shapes):
    return pl.pallas_call(
        lambda *refs: join_body(plan, len(sources), *refs),
        in_specs=[pl.BlockSpec(memory_space=pl.ANY)] * len(sources),
        out_specs=vmem(len(shapes)),
        out_shape=[jax.ShapeDtypeStruct(shape, jnp.bfloat16) for shape in shapes],
        compiler_params=pltpu.CompilerParams(vmem_limit_bytes=16 << 20),
        scratch_shapes=[pltpu.SemaphoreType.DMA((len(plan),))],
        cost_estimate=tiny_cost(),
        name="join",
    )(*sources)


class Gather:
    def __init__(self, shard):
        self.masks = masks_of(lax.axis_size("dp"))
        self.held, self.fresh = [shard[None]], []
        self.order = [[0], [0]]

    def extend(self, side, mask):
        self.order[side] = self.order[side] + [item ^ mask for item in self.order[side]]

    def early(self):
        for mask in self.masks[:-2]:
            if self.fresh:
                self.held = [jnp.concatenate([self.held[0], self.fresh[0]], axis=0)]
            self.fresh = [data_swap(self.held[0], mask)]
            self.extend(0, mask)
            self.extend(1, mask)

    def send(self, masks):
        self.fresh = [data_swap(self.held[side], masks[side]) for side in range(2)]
        for side in range(2):
            self.extend(side, masks[side])

    def second(self):
        count, rows, columns = self.held[0].shape
        half = columns // 2
        plan = [(k, side * half, half, side, k * count) for k in range(2) for side in range(2)]
        self.held = join(self.held + self.fresh, plan, [(2 * count, rows, half)] * 2)
        self.send([self.masks[-2], self.masks[-1]])

    def third(self):
        count, rows, half = self.held[0].shape
        plan = [(2 * k + side, 0, half, side, k * count) for k in range(2) for side in range(2)]
        self.held = join(list(self.held) + self.fresh, plan, [(2 * count, rows, half)] * 2)
        self.send([self.masks[-1], self.masks[-2]])


def settle(*items):
    gathers = [item for item in items if isinstance(item, Gather)]
    others = [item for item in items if not isinstance(item, Gather)]
    arrays = [(item.held, item.fresh) for item in gathers]
    arrays, others = lax.optimization_barrier((arrays, others))
    for item, (held, fresh) in zip(gathers, arrays):
        item.held, item.fresh = list(held), list(fresh)
    return others


def place_body(gathered, depth, extra, me_ref, *refs):
    pieces, outs, buffers, (in_sems, out_sems) = refs[:4], refs[4:-3], refs[-3], refs[-2:]
    me = me_ref[0]
    reads, writes = [], []
    for side in range(2):
        held, fresh = pieces[2 * side : 2 * side + 2]
        columns = held.shape[2]
        for position, item in enumerate(gathered.order[side]):
            count = held.shape[0]
            piece, row = (held, position) if position < count else (fresh, position - count)
            buffer = buffers.at[len(reads)]
            reads.append(pltpu.make_async_copy(piece.at[row], buffer, in_sems.at[len(reads)]))
            target = outs[0].at[me ^ item, :, pl.ds(side * columns, columns)]
            source = buffer.at[pl.ds(0, depth)] if extra else buffer
            group = [pltpu.make_async_copy(source, target, out_sems.at[len(writes)])]
            if extra and side == 0:
                slot = out_sems.at[2 * len(gathered.order[0]) + position]
                group.append(pltpu.make_async_copy(buffer.at[pl.ds(depth, extra)], outs[1].at[me ^ item], slot))
            writes.append(group)
    for item in reads:
        item.start()
    for item, group in zip(reads, writes):
        item.wait()
        for copy in group:
            copy.start()
    for group in writes:
        for copy in group:
            copy.wait()


def place_blocks(gathered, depth, extra=0):
    size = lax.axis_size("dp")
    pieces = [gathered.held[0], gathered.fresh[0], gathered.held[1], gathered.fresh[1]]
    columns = pieces[0].shape[2]
    if extra and depth % 8:
        whole = place_blocks(gathered, depth + extra)[0]
        return [whole[:, :depth], whole[:, depth:, :columns]]
    me = lax.axis_index("dp").reshape(1)
    shapes = [jax.ShapeDtypeStruct((size, depth, 2 * columns), jnp.bfloat16)]
    if extra:
        shapes.append(jax.ShapeDtypeStruct((size, extra, columns), jnp.bfloat16))
    return pl.pallas_call(
        lambda *refs: place_body(gathered, depth, extra, *refs),
        in_specs=[pl.BlockSpec(memory_space=pltpu.SMEM)] + [pl.BlockSpec(memory_space=pl.ANY)] * 4,
        out_specs=[pl.BlockSpec(memory_space=pl.ANY)] * len(shapes),
        out_shape=shapes,
        compiler_params=pltpu.CompilerParams(vmem_limit_bytes=VMEM_LIMIT),
        scratch_shapes=[
            pltpu.VMEM((2 * size, depth + extra, columns), jnp.bfloat16),
            pltpu.SemaphoreType.DMA((2 * size,)),
            pltpu.SemaphoreType.DMA((3 * size if extra else 2 * size,)),
        ],
        cost_estimate=tiny_cost(),
        name="place",
    )(me, *pieces)


def spread(number, masks):
    return sum(((number >> k) & 1) * mask for k, mask in enumerate(masks))


def compress(number, masks):
    return sum(((number // mask) & 1) << k for k, mask in enumerate(masks))


def sum_body(jobs, me_ref, *refs):
    me = me_ref[0]
    sems = refs[-1]
    inputs = sum(item["inputs"] for item in jobs)
    results = sum(len(item["outs"]) for item in jobs)
    buffers = refs[inputs + results : -1]
    copies = []
    first, k = 0, 0
    for job in jobs:
        for side in job["plan"]:
            for operand, start, index in side:
                columns = buffers[k].shape[2]
                for number in range(buffers[k].shape[0]):
                    source = refs[first + operand].at[index(number, me), :, pl.ds(start, columns)]
                    copies.append(pltpu.make_async_copy(source, buffers[k].at[number], sems.at[len(copies)]))
                    copies[-1].start()
                k += 1
        first += job["inputs"]
    for item in copies:
        item.wait()
    k = 0
    for job in jobs:
        outs = refs[first : first + len(job["outs"])]
        first += len(job["outs"])
        for side, terms in enumerate(job["plan"]):
            total = wide(buffers[k][...])
            for buffer in buffers[k + 1 : k + len(terms)]:
                total = total + wide(buffer[...])
            k += len(terms)
            columns = total.shape[-1]
            if job["split"]:
                for part in range(2):
                    outs[2 * side + part][...] = total[0, :, part * columns // 2 : (part + 1) * columns // 2]
            elif job["merged"]:
                outs[0][:, :, side * columns : (side + 1) * columns] = total.astype(outs[0].dtype)
            else:
                outs[side][...] = total.astype(outs[side].dtype)


def run_sums(jobs):
    operands, outs, scratch, count = [], [], [], 0
    for job in jobs:
        operands += job["operands"]
        outs += job["outs"]
        scratch += job["scratch"]
        count += job["copies"]
    results = pl.pallas_call(
        lambda *refs: sum_body(jobs, *refs),
        in_specs=[pl.BlockSpec(memory_space=pltpu.SMEM)] + [pl.BlockSpec(memory_space=pl.ANY)] * len(operands),
        out_specs=vmem(len(outs)),
        out_shape=outs,
        scratch_shapes=scratch + [pltpu.SemaphoreType.DMA((count,))],
        compiler_params=pltpu.CompilerParams(vmem_limit_bytes=VMEM_LIMIT),
        cost_estimate=tiny_cost(),
        name="sum_blocks",
    )(lax.axis_index("dp").reshape(1), *operands)
    groups = []
    for job in jobs:
        groups.append(list(results[: len(job["outs"])]))
        results = results[len(job["outs"]) :]
    return groups


def scatter_masks(size):
    masks = masks_of(size)[::-1]
    return [masks, [masks[1], masks[0]] + masks[2:]]


class Scatter:
    def __init__(self, own, sends=None):
        self.sends = sends
        self.size = lax.axis_size("dp")
        self.half = own.shape[1] // 2
        self.depth = own.shape[0] // self.size
        self.own = own.reshape(self.size, self.depth, own.shape[1])
        self.masks = scatter_masks(self.size)
        self.gots = []
        self.step = 0

    def remaining(self, side, step):
        return sorted(set(self.masks[side]) - set(self.masks[side][: step + 1]))

    def total(self, final, merged, split=False):
        return run_sums([self.job(final, merged, split)])[0]

    def job(self, final, merged, split=False):
        step = self.step
        last = len(self.masks[0]) == step
        count = 1 if last else self.size >> (step + 1)
        operands = [self.own]
        for got in self.gots:
            operands += got
        plan = []
        for side in range(2):
            rest = [] if last else self.remaining(side, step)
            before = sum(self.masks[side][:step])
            flip = 0 if last else self.masks[side][step]

            def block(number, me, rest=rest, before=before, flip=flip):
                return (me & before) | ((me ^ flip) & flip) | spread(number, rest)

            terms = [(0, side * self.half, block)]
            operand = 1
            for number, got in enumerate(self.gots):
                kept = self.remaining(side, number)
                which, start = (operand, side * self.half) if len(got) == 1 else (operand + side, 0)
                terms.append((which, start, lambda item, me, block=block, kept=kept: compress(block(item, me), kept)))
                operand += len(got)
            plan.append(terms)
        counts = [len(item) for item in plan]
        dtype = jnp.float32 if final else jnp.bfloat16
        columns = 2 * self.half if merged else self.half
        outs = [jax.ShapeDtypeStruct((count, self.depth, columns), dtype)] * (1 if merged else 2)
        if split:
            outs = [jax.ShapeDtypeStruct((self.depth, self.half // 2), dtype)] * 4
        buffers = [pltpu.VMEM((count, self.depth, self.half), jnp.bfloat16)] * sum(counts)
        return dict(
            plan=plan,
            merged=merged,
            split=split,
            operands=operands,
            inputs=len(operands),
            outs=outs,
            scratch=buffers,
            copies=count * sum(counts),
        )

    def prepare(self):
        self.sends = self.total(False, self.step >= 2)
        return self.sends

    def launch(self):
        masks = [self.masks[side][self.step] for side in range(len(self.sends))]
        self.gots = self.gots + [[data_swap(send, mask) for send, mask in zip(self.sends, masks)]]
        self.step += 1

    def advance(self):
        if self.step > 0 or self.sends is None:
            self.prepare()
        self.launch()

    def rest(self):
        while self.step < len(self.masks[0]):
            self.advance()

    def finish(self):
        return [item[0] for item in self.total(True, False)]


def advance_both(*scatters):
    sends = run_sums([item.job(False, item.step >= 2) for item in scatters])
    for item, send in zip(scatters, sends):
        item.sends = send
        item.launch()


def settle_scatters(scatters, *others):
    gots, others = lax.optimization_barrier(([item.gots for item in scatters], others))
    for item, got in zip(scatters, gots):
        item.gots = got
    return others


def ff_body(first, tiles, half, *refs):
    n2, cot, own_up, own_down, sib_up, sib_down, own_b, sib_b = refs[:8]
    if first:
        acc_b, acc_g, own_acts, sib_acts = refs[8:]
    else:
        prev_b, prev_g, out_keep, out_send, grad_keep, grad_send, own_acts, sib_acts, acc_b, acc_g, *late, sems = refs[8:]
        copies = [pltpu.make_async_copy(item, late[k], sems.at[k]) for k, item in enumerate((prev_b, prev_g))]
    side, tile = pl.program_id(0), pl.program_id(1)

    @pl.when((side == 0) & (tile == 0))
    def _():
        acc_b[...] = jnp.zeros_like(acc_b)
        acc_g[...] = jnp.zeros_like(acc_g)
        if not first:
            for item in copies:
                item.start()

    def step(up_ref, down_ref, bias, acts):
        up, down = up_ref[...], down_ref[...]
        width = up.shape[1]
        pre = mm(n2[...], up) + wide(bias[...])
        act, slope = gelu_pair(pre)
        hidden = low(act)
        grad_pre = low(mm(cot[...], down) * slope)
        acc_b[...] += mm_right(hidden, down)
        acc_g[...] += mm_right(grad_pre, up)
        acts[:, :width] = grad_pre
        acts[:, width:] = hidden

    @pl.when(side == 0)
    def _():
        step(sib_up, sib_down, sib_b, sib_acts)

    @pl.when(side == 1)
    def _():
        step(own_up, own_down, own_b, own_acts)

    if not first:

        @pl.when((side == 1) & (tile == tiles - 1))
        def _():
            for item in copies:
                item.wait()
            out_keep[...] = acc_b[:half] + late[0][:half]
            out_send[...] = low(acc_b[half:] + late[0][half:])
            grad_keep[...] = acc_g[...] + late[1][...]
            grad_send[:half] = low(grad_keep[half:])
            grad_send[half:] = low(grad_keep[:half])


def side_specs(tiles):
    def second(shape, start=0):
        return pl.BlockSpec(shape, lambda s, i: (0, start + jnp.where(s == 1, i, 0)))

    def initial(shape, start=0):
        return pl.BlockSpec(shape, lambda s, i: (0, start + jnp.where(s == 0, i, tiles - 1)))

    return second, initial


def const_spec(shape):
    return pl.BlockSpec(shape, lambda s, i: (0, 0), pipeline_mode=pl.Buffered(1))


def feed_forward(n2, cot, own_w, sib_w, own_b, sib_b, tile, previous=()):
    rows, model = n2.shape
    hidden = own_b.shape[1]
    tiles = hidden // tile
    first = not previous
    half = rows // 2
    second, initial = side_specs(tiles)
    in_specs = [const_spec(n2.shape)] * 2
    in_specs += [second((model, tile)), second((model, tile), tiles), initial((model, tile)), initial((model, tile), tiles)]
    in_specs += [second((1, tile)), initial((1, tile))]
    in_specs += [pl.BlockSpec(memory_space=pl.ANY) for item in previous]
    operands = [n2, cot, own_w, own_w, sib_w, sib_w, own_b, sib_b, *previous]
    full = jax.ShapeDtypeStruct((rows, model), jnp.float32)
    acts = jax.ShapeDtypeStruct((rows, 2 * hidden), jnp.bfloat16)
    shapes = [full, full]
    scratch = []
    if not first:
        shapes = [
            jax.ShapeDtypeStruct((half, model), jnp.float32),
            jax.ShapeDtypeStruct((half, model), jnp.bfloat16),
            full,
            jax.ShapeDtypeStruct((rows, model), jnp.bfloat16),
        ]
        scratch = [pltpu.VMEM((rows, model), jnp.float32)] * 4 + [pltpu.SemaphoreType.DMA((2,))]
    specs = [const_spec(item.shape) for item in shapes]
    specs += [second((rows, 2 * tile)), initial((rows, 2 * tile))]
    return pl.pallas_call(
        lambda *refs: ff_body(first, tiles, half, *refs),
        grid=(2, tiles),
        in_specs=in_specs,
        out_specs=specs,
        out_shape=shapes + [acts, acts],
        scratch_shapes=scratch,
        compiler_params=pltpu.CompilerParams(vmem_limit_bytes=VMEM_LIMIT),
        cost_estimate=tiny_cost(),
        name="feed_forward",
    )(*operands)


def weight_grads_body(n2t, sib_n2t, cott, sib_cott, acts, sib_acts, grads, sums):
    width = acts.shape[1] // 2
    grads[:, :width] = low(mm(n2t[...], acts[:, :width]) + mm(sib_n2t[...], sib_acts[:, :width]))
    grads[:, width:] = low(mm(cott[...], acts[:, width:]) + mm(sib_cott[...], sib_acts[:, width:]))
    total = jnp.sum(wide(acts[:, :width]), axis=0, keepdims=True)
    sums[...] = total + jnp.sum(wide(sib_acts[:, :width]), axis=0, keepdims=True)


def weight_grads(left, acts, sib_acts, tile):
    model, rows = left[0].shape
    tiles = acts.shape[1] // (2 * tile)
    const = pl.BlockSpec((model, rows), lambda i: (0, 0), pipeline_mode=pl.Buffered(1))
    return pl.pallas_call(
        weight_grads_body,
        grid=(tiles,),
        in_specs=[const] * 4 + [pl.BlockSpec((rows, 2 * tile), lambda i: (0, i))] * 2,
        out_specs=[pl.BlockSpec((model, 2 * tile), lambda i: (0, i)), pl.BlockSpec((1, tile), lambda i: (0, i))],
        out_shape=[
            jax.ShapeDtypeStruct((model, acts.shape[1]), jnp.bfloat16),
            jax.ShapeDtypeStruct((1, acts.shape[1] // 2), jnp.float32),
        ],
        compiler_params=pltpu.CompilerParams(vmem_limit_bytes=VMEM_LIMIT),
        cost_estimate=tiny_cost(),
        name="weight_grads",
    )(*left, acts, sib_acts)


def prepare_body(*refs):
    vectors, (w_query, w_key, w_value, w_out_t), out = refs[:6], refs[6:10], refs[10]
    depth, width = w_query.shape
    out[:depth] = jnp.concatenate([w_query[...], w_key[...], w_value[...], w_out_t[...]], axis=1)
    out[depth:] = jnp.zeros_like(out[depth:])
    for k, vector in enumerate(vectors):
        out[depth + k : depth + k + 1, :depth] = vector[...].reshape(1, depth)


def prepare(vectors, weights):
    depth, width = weights[0].shape
    return pl.pallas_call(
        prepare_body,
        in_specs=vmem(10),
        out_specs=pl.BlockSpec(memory_space=pltpu.VMEM),
        out_shape=jax.ShapeDtypeStruct((depth + VEC_ROWS, 4 * width), jnp.bfloat16),
        compiler_params=pltpu.CompilerParams(vmem_limit_bytes=VMEM_LIMIT),
        cost_estimate=tiny_cost(),
        name="prepare",
    )(*vectors, *weights)


def assemble_body(half, mine, other_rows, other_cot, rows, cot, cot_t):
    rows[:half] = mine[:half]
    rows[half:] = other_rows[...]
    cot[:half] = mine[half:]
    cot[half:] = other_cot[...]
    cot_t[...] = cot[...].T


def assemble(mine, other_rows, other_cot):
    rows, model = mine.shape
    shape = jax.ShapeDtypeStruct((rows, model), jnp.bfloat16)
    return pl.pallas_call(
        lambda *refs: assemble_body(rows // 2, *refs),
        in_specs=vmem(3),
        out_specs=vmem(3),
        out_shape=[shape, shape, jax.ShapeDtypeStruct((model, rows), jnp.bfloat16)],
        compiler_params=pltpu.CompilerParams(vmem_limit_bytes=VMEM_LIMIT),
        cost_estimate=tiny_cost(),
        name="assemble",
    )(mine, other_rows, other_cot)


def dot_t(left, right):
    return lax.dot_general(left, right, (((0,), (0,)), ((), ())), preferred_element_type=jnp.float32)


def norm_rows(values, gain, shift):
    xhat, inverse = norm_parts(values)
    return low(xhat * gain + shift)


def fill_mask(where, mask):
    count = mask.shape[0] // 4
    for k in range(4):
        position = (where[0] ^ k) * count + lax.broadcasted_iota(jnp.int32, (count, 1), 0)
        mask[k * count : (k + 1) * count] = (position < where[1]).astype(jnp.float32)


def attn_head(joined, head, width, mask):
    scale = HEAD_DIM ** (-0.5)
    begin = pl.multiple_of(head * HEAD_DIM, 16)
    query = joined[pl.ds(begin, HEAD_DIM), :]
    keys = joined[pl.ds(pl.multiple_of(width + begin, 16), HEAD_DIM), :]
    values = joined[pl.ds(pl.multiple_of(2 * width + begin, 16), HEAD_DIM), :]
    scores = jnp.where(mask[...] > 0.5, dot_t(keys, query) * scale, -1000000000.0)
    return begin, query, keys, values, scores


def attn_forward_body(first, width, *refs):
    if first:
        where, x, vectors, weights, bias, n1, n1t, joined, mixed, totals, part, mask = refs
        n1[...] = norm_rows(wide(x[...]), vectors[0:1], vectors[1:2])
        n1t[...] = n1[...].T
    else:
        where, n1, previous, weights, bias, joined, mixed, totals, part, send_one, send_two, mask = refs
    fill_mask(where, mask)
    joined[...] = low(mm(n1[...], weights[:, : 3 * width]) + bias[...]).T

    def one(head, carry):
        begin, query, keys, values, scores = attn_head(joined, head, width, mask)
        top = jnp.max(scores, axis=0, keepdims=True)
        expo = jnp.exp(scores - top)
        total = jnp.sum(expo, axis=0, keepdims=True)
        probs = low(expo * (1.0 / total))
        mixed[pl.ds(begin, HEAD_DIM), :] = low(mm(values, probs))
        totals[pl.ds(head, 1), :] = top + jnp.log(total)
        return carry

    lax.fori_loop(0, width // HEAD_DIM, one, 0, unroll=True)
    term = mm_right(mixed[...].T, weights[:, 3 * width :])
    if first:
        part[...] = term
    else:
        term = previous[...] + term
        half = term.shape[0] // 2
        part[...] = term
        send_one[...] = low(term[half:])
        send_two[...] = low(term[:half])


def attn_forward(where, head_in, weights, bias, width, first):
    rows, model = head_in[0].shape
    low_shape = lambda *shape: jax.ShapeDtypeStruct(shape, jnp.bfloat16)
    wide_shape = lambda *shape: jax.ShapeDtypeStruct(shape, jnp.float32)
    shapes = [low_shape(3 * width, rows), low_shape(width, rows), wide_shape(width // HEAD_DIM, rows), wide_shape(rows, model)]
    shapes = [low_shape(rows, model), low_shape(model, rows)] + shapes if first else shapes + [low_shape(rows // 2, model)] * 2
    operands = [where] + list(head_in) + [weights, bias]
    return pl.pallas_call(
        lambda *refs: attn_forward_body(first, width, *refs),
        in_specs=[pl.BlockSpec(memory_space=pltpu.SMEM)] + vmem(len(operands) - 1),
        out_specs=vmem(len(shapes)),
        out_shape=shapes,
        scratch_shapes=[pltpu.VMEM((rows, 1), jnp.float32)],
        compiler_params=pltpu.CompilerParams(vmem_limit_bytes=VMEM_LIMIT),
        cost_estimate=tiny_cost(),
        name="attn_forward",
    )(*operands)


def attn_backward_body(first, width, size, *refs):
    where, gb, weights, joined, totals = refs[:5]
    if first:
        mixed, part, acts, gmt, djoined, mask = refs[5:]
    else:
        late, outs, scratch = refs[5:11], refs[11:-9], refs[-9:]
        gmt, mask, *buffers, sems = scratch
        djoined, grads = outs[0], outs[1]
        copies = [pltpu.make_async_copy(item, buffer, sems.at[k]) for k, (item, buffer) in enumerate(zip(late, buffers))]
        for item in copies:
            item.start()
        gbt, sib_gbt, n1t, sib_n1t, mixed, sib_acts = buffers
    scale = HEAD_DIM ** (-0.5)
    fill_mask(where, mask)
    gmt[...] = low(mm(gb[...], weights[:, 3 * width :])).T

    def one(head, carry):
        begin, query, keys, values, scores = attn_head(joined, head, width, mask)
        probs = jnp.exp(scores - totals[pl.ds(head, 1), :])
        gm = gmt[pl.ds(begin, HEAD_DIM), :]
        grad_probs = dot_t(values, gm)
        delta = jnp.sum(grad_probs * probs, axis=0, keepdims=True)
        grad_scores = low(probs * (grad_probs - delta))
        djoined[pl.ds(begin, HEAD_DIM), :] = low(mm(keys, grad_scores) * scale)
        djoined[pl.ds(pl.multiple_of(width + begin, 16), HEAD_DIM), :] = low(mm_right(query, grad_scores) * scale)
        djoined[pl.ds(pl.multiple_of(2 * width + begin, 16), HEAD_DIM), :] = low(mm_right(gm, low(probs)))
        return carry

    lax.fori_loop(0, width // HEAD_DIM, one, 0, unroll=True)
    if first:
        acts[: 3 * width] = djoined[...]
        acts[3 * width :] = mixed[...]
        part[...] = mm_right(djoined[...].T, weights[:, : 3 * width])
        return
    for item in copies:
        item.wait()
    copies = []
    ones = jnp.ones((8, gb.shape[0]), jnp.bfloat16)
    outs[2][...] = mm_right(ones, djoined[...]) + mm_right(ones, sib_acts[: 3 * width])
    grad_qkv = low(mm_right(n1t[...], djoined[...]) + mm_right(sib_n1t[...], sib_acts[: 3 * width]))
    grad_out = low(mm_right(gbt[...], mixed[...]) + mm_right(sib_gbt[...], sib_acts[3 * width :]))
    if size:
        grads[:, :, : 3 * width] = grad_qkv.reshape(size, -1, 3 * width)
        grads[:, :, 3 * width :] = grad_out.reshape(size, -1, width)
        masks = scatter_masks(size)
        for side in range(2):
            mask = masks[side][0]
            rest = sorted(set(masks[side]) - {mask})
            for number in range(size // 2):
                block = ((where[2] ^ mask) & mask) | spread(number, rest)
                source = grads.at[block, :, pl.ds(side * 2 * width, 2 * width)]
                copies.append(pltpu.make_async_copy(source, outs[3 + side].at[number], sems.at[6 + len(copies)]))
                copies[-1].start()
    else:
        grads[:, : 3 * width] = grad_qkv
        grads[:, 3 * width :] = grad_out
    for item in copies:
        item.wait()


def attn_backward(where, gb, weights, saved, width, late=(), size=0):
    rows, model = gb.shape
    first = not late
    joined, mixed, totals = saved
    operands = [where, gb, weights, joined, totals]
    specs = [pl.BlockSpec(memory_space=pltpu.SMEM)] + vmem(4)
    low_shape = lambda *shape: jax.ShapeDtypeStruct(shape, jnp.bfloat16)
    full = jax.ShapeDtypeStruct((rows, model), jnp.float32)
    scratch = [
        pltpu.VMEM((width, rows), jnp.bfloat16),
        pltpu.VMEM((3 * width, rows), jnp.bfloat16),
        pltpu.VMEM((rows, 1), jnp.float32),
    ]
    if first:
        operands.append(mixed)
        specs += vmem(1)
        shapes = [full, low_shape(4 * width, rows)]
        out_specs = vmem(2)
    else:
        gbt, sib_gbt, n1t, sib_n1t, sib_acts = late
        late = [gbt, sib_gbt, n1t, sib_n1t, mixed, sib_acts]
        operands += late
        specs += [pl.BlockSpec(memory_space=pl.ANY)] * len(late)
        del scratch[1]
        scratch += [pltpu.VMEM(item.shape, item.dtype) for item in late] + [pltpu.SemaphoreType.DMA((len(late) + size,))]
        grads = low_shape(size, model // size, 4 * width) if size else low_shape(model, 4 * width)
        shapes = [low_shape(3 * width, rows), grads, jax.ShapeDtypeStruct((8, 3 * width), jnp.float32)]
        out_specs = vmem(3)
        if size:
            shapes += [low_shape(size // 2, model // size, 2 * width)] * 2
            out_specs += [pl.BlockSpec(memory_space=pl.ANY)] * 2
    return pl.pallas_call(
        lambda *refs: attn_backward_body(first, width, size, *refs),
        in_specs=specs,
        out_specs=out_specs,
        out_shape=shapes,
        scratch_shapes=scratch,
        compiler_params=pltpu.CompilerParams(vmem_limit_bytes=VMEM_LIMIT),
        cost_estimate=tiny_cost(),
        name="attn_backward",
    )(*operands)


def input_grad_body(width, half, previous, acts, weights, keep, send):
    term = previous[...] + mm_right(acts[...].T, weights[:, : 3 * width])
    keep[...] = term
    send[...] = low(term[half:])


def input_grad(previous, acts, weights, width):
    rows, model = previous.shape
    return pl.pallas_call(
        lambda *refs: input_grad_body(width, rows // 2, *refs),
        in_specs=vmem(3),
        out_specs=vmem(2),
        out_shape=[jax.ShapeDtypeStruct((rows, model), jnp.float32), jax.ShapeDtypeStruct((rows // 2, model), jnp.bfloat16)],
        compiler_params=pltpu.CompilerParams(vmem_limit_bytes=VMEM_LIMIT),
        cost_estimate=tiny_cost(),
        name="input_grad",
    )(previous, acts, weights)


def middle_body(x, part, got_one, got_two, vectors, inner, n2, n2t, stats):
    got = jnp.where(pl.program_id(0) < 2, wide(got_one[...]), wide(got_two[...]))
    value = wide(x[...]) + (part[...] + got + vectors[2:3])
    inner[...] = value
    mean = jnp.mean(value, axis=-1, keepdims=True)
    center = value - mean
    inverse = lax.rsqrt(jnp.mean(center * center, axis=-1, keepdims=True) + norm_eps)
    n2[...] = low(center * inverse * vectors[3:4] + vectors[4:5])
    stats[:, 0:1] = mean
    stats[:, 1:2] = inverse
    n2t[...] = n2[...].T


def row_spec(block, model):
    return pl.BlockSpec((block, model), lambda i: (i, 0))


def middle(x, part, got_one, got_two, vectors):
    rows, model = x.shape
    block = rows // 4
    shapes = [
        jax.ShapeDtypeStruct((rows, model), jnp.float32),
        jax.ShapeDtypeStruct((rows, model), jnp.bfloat16),
        jax.ShapeDtypeStruct((model, rows), jnp.bfloat16),
        jax.ShapeDtypeStruct((rows, 2), jnp.float32),
    ]
    return pl.pallas_call(
        middle_body,
        grid=(4,),
        in_specs=[row_spec(block, model)] * 2
        + [pl.BlockSpec((block, model), lambda i: (jnp.minimum(i, 1), 0)), pl.BlockSpec((block, model), lambda i: (jnp.maximum(i - 2, 0), 0))]
        + [pl.BlockSpec(vectors.shape, lambda i: (0, 0))],
        out_specs=[row_spec(block, model)] * 2 + [pl.BlockSpec((model, block), lambda i: (0, i)), row_spec(block, 2)],
        out_shape=shapes,
        compiler_params=pltpu.CompilerParams(vmem_limit_bytes=VMEM_LIMIT),
        cost_estimate=tiny_cost(),
        name="middle",
    )(x, part, got_one, got_two, vectors)


def turn_body(inner, stats, grad, got, cot, vectors, keep, gb, gbt, sums):
    step = pl.program_id(0)
    value = grad[...] + wide(got[...])
    inverse = stats[:, 1:2]
    xhat = (inner[...] - stats[:, 0:1]) * inverse
    top = wide(cot[...])
    total = top + norm_back(value, xhat, inverse, vectors[3:4])
    gb[...] = low(total)
    gbt[...] = gb[...].T

    @pl.when(step < 2)
    def _():
        keep[...] = total
        parts = [jnp.sum(item, axis=0, keepdims=True) for item in (wide(low(total)), value * xhat, value, top)]
        joined = jnp.concatenate(parts, axis=0)
        sums[...] = jnp.where(step == 0, joined, sums[...] + joined)


def turn(inner, stats, grad, got, cot, vectors):
    rows, model = inner.shape
    block = rows // 4
    shapes = [
        jax.ShapeDtypeStruct((rows // 2, model), jnp.float32),
        jax.ShapeDtypeStruct((rows, model), jnp.bfloat16),
        jax.ShapeDtypeStruct((model, rows), jnp.bfloat16),
        jax.ShapeDtypeStruct((4, model), jnp.float32),
    ]
    return pl.pallas_call(
        turn_body,
        grid=(4,),
        in_specs=[row_spec(block, model), row_spec(block, 2)] + [row_spec(block, model)] * 3 + [pl.BlockSpec(vectors.shape, lambda i: (0, 0))],
        out_specs=[
            pl.BlockSpec((block, model), lambda i: (jnp.minimum(i, 1), 0)),
            row_spec(block, model),
            pl.BlockSpec((model, block), lambda i: (0, i)),
            pl.BlockSpec((4, model), lambda i: (0, 0)),
        ],
        out_shape=shapes,
        compiler_params=pltpu.CompilerParams(vmem_limit_bytes=VMEM_LIMIT),
        cost_estimate=tiny_cost(),
        name="turn",
    )(inner, stats, grad, got, cot, vectors)


def pick(pair, index):
    return lax.dynamic_index_in_dim(pair, index, axis=0, keepdims=False)


def order_pair(mine, other, core):
    return jnp.where(core == 0, jnp.stack([mine, other]), jnp.stack([other, mine]))


def shards(
    clips,
    lengths,
    norm1_gain,
    norm1_bias,
    w_query,
    bias_query,
    w_key,
    w_value,
    bias_value,
    w_out,
    bias_out,
    norm2_gain,
    norm2_bias,
    w_up,
    bias_up,
    w_down,
    bias_down,
    cotangent,
):
    rows = clips.shape[1]
    model = clips.shape[2]
    depth, width = w_query.shape
    hidden_width = w_up.shape[1]
    data_size = lax.axis_size("dp")
    place = lax.axis_index("tensor")
    core = place % 2
    masks = masks_of(data_size)

    vectors = (norm1_gain, norm1_bias, bias_out, norm2_gain, norm2_bias, bias_down)
    attn = Gather(prepare(vectors, (w_query, w_key, w_value, w_out.T)))
    attn.early()
    pair, cot_pair = after((clips, cotangent), attn.held)
    sent = jnp.concatenate([pick(pair, 1 - core), pick(cot_pair, 1 - core)], axis=0)
    got = tensor_swap(sent, 1)
    half_clip = jnp.concatenate([pick(pair, core), got[:rows]], axis=0)
    half_cot = jnp.concatenate([pick(cot_pair, core), got[rows:]], axis=0)
    other_clip = tensor_swap(half_clip, 2)
    local_bias = jnp.concatenate([bias_up, bias_query, bias_value])
    sib_bias = tensor_swap(local_bias.reshape(1, -1), 1)[0]
    cut = FIRST_TILES * TILE
    down_t = w_down.T
    ff_one = Gather(jnp.concatenate([w_up[:, :cut], down_t[:, :cut]], axis=1))
    ff_two = Gather(jnp.concatenate([w_up[:, cut:], down_t[:, cut:]], axis=1))
    where = jnp.stack([place, pick(lengths, core), lax.axis_index("dp")]).astype(jnp.int32)
    other_clip, half_cot, sib_bias, where = settle(attn, ff_one, ff_two, other_clip, half_cot, sib_bias, where)

    attn.second()
    other_cot = tensor_swap(half_cot, 2)
    biases = (local_bias.reshape(1, -1), sib_bias.reshape(1, -1))
    joined_biases = []
    for item in biases:
        item = wide(item[:, hidden_width:])
        joined_biases.append(jnp.concatenate([item[:, :width], jnp.zeros((1, width), jnp.float32), item[:, width:]], axis=1))
    joined_biases, other_clip = settle(attn, ff_one, joined_biases, other_clip)

    attn.third()
    ff_one.early()
    low_rows, cot, cott = assemble(jnp.concatenate([half_clip, half_cot], axis=0), other_clip, other_cot)
    low_rows, cot, cott = settle(attn, ff_one, ff_two, low_rows, cot, cott)

    attn_all, vector_all = place_blocks(attn, depth, VEC_ROWS)
    attn_own = attn_all.reshape(model, model)
    attn_sib = tensor_swap(attn_own, 1)
    attn_w = (attn_own, attn_sib)
    ff_one.second()
    ff_two.early()
    sib_cott = tensor_swap(cott, 1)
    vectors_full = wide(vector_all[:, :6, :depth].transpose(1, 0, 2).reshape(6, model))
    outs = attn_forward(where, (low_rows, vectors_full), attn_own, joined_biases[0], width, True)
    normed_one, n1t = outs[:2]
    saved = [outs[2:5]]
    outs = attn_forward(where, (normed_one, outs[5]), attn_sib, joined_biases[1], width, False)
    saved.append(outs[:3])
    part_keep, *part_send = outs[3:]

    def ff_weights(gathered):
        own_w = place_blocks(gathered, depth)[0].reshape(model, -1)
        return own_w, tensor_swap(own_w, 1)

    part_send, sib_cott, n1t = settle(ff_one, ff_two, part_send, sib_cott, n1t)
    got_one = tensor_swap(part_send[0], 2)
    ff_one.third()
    got_one, part_two, n1t = settle(ff_one, got_one, part_send[1], n1t)
    got_two = tensor_swap(part_two, 2)
    ff_two.second()
    one_own, one_sib = ff_weights(ff_one)
    sib_n1t = tensor_swap(n1t, 1)
    got_one, got_two, one_own = settle(ff_two, got_one, got_two, one_own)
    ff_two.third()
    inner, normed_two, n2t, stats = middle(low_rows, part_keep, got_one, got_two, vectors_full)
    bias_rows = [[item[:, :cut], item[:, cut:hidden_width]] for item in biases]
    outs = feed_forward(normed_two, cot, one_own, one_sib, bias_rows[0][0], bias_rows[1][0], TILE)
    sums_so_far, own_acts, other_acts = outs[:2], outs[2], outs[3]
    sums_so_far, other_acts, n2t, sib_n1t = settle(ff_two, sums_so_far, other_acts, n2t, sib_n1t)
    sib_n2t = tensor_swap(n2t, 1)
    sib_acts = tensor_swap(other_acts, 1)
    two_own = place_blocks(ff_two, depth)[0].reshape(model, -1)
    sib_acts, sib_n2t, two_own = settle(sib_acts, sib_n2t, two_own)
    two_sib = tensor_swap(two_own, 1)
    left = (n2t, sib_n2t, cott, sib_cott)
    one_grad, one_sums = weight_grads(left, own_acts, sib_acts, TILE)
    scatter_one = Scatter(one_grad)
    scatter_one.advance()
    sums_so_far, two_sib = after((sums_so_far, two_sib), scatter_one.sends)
    outs = feed_forward(normed_two, cot, two_own, two_sib, bias_rows[0][1], bias_rows[1][1], TILE, sums_so_far)
    out_keep, out_send, grad_keep, grad_send, own_acts, other_acts = settle_scatters([scatter_one], *outs)

    grad_got = tensor_swap(grad_send, 2)
    sib_acts = tensor_swap(other_acts, 1)
    scatter_one.advance()
    two_grad, two_sums = weight_grads(left, own_acts, sib_acts, TILE)
    out_send, two_grad = settle_scatters([scatter_one], out_send, two_grad)
    scatter_two = Scatter(two_grad)
    scatter_two.advance()
    grad_got = after(grad_got, scatter_two.sends)
    inner_keep, grad_branch, gbt, vectors_two = turn(inner, stats, grad_keep, grad_got, cot, vectors_full)
    grad_branch, gbt, out_send = settle_scatters([scatter_two], grad_branch, gbt, out_send)
    sib_gbt = tensor_swap(gbt, 1)
    out_got = tensor_swap(out_send, 2)
    advance_both(scatter_one, scatter_two)
    scatter_one.rest()
    grad_branch = after(grad_branch, scatter_one.sends, scatter_two.sends)
    part, other_acts = attn_backward(where, grad_branch, attn_w[1], saved[1], width)
    part, other_acts, sib_gbt = settle(part, other_acts, sib_gbt)
    sib_acts = tensor_swap(other_acts, 1)
    late = (gbt, sib_gbt, n1t, sib_n1t, sib_acts)
    direct = data_size if depth % 16 == 0 else 0
    own_acts, own_grad, own_sums, *first_sends = attn_backward(where, grad_branch, attn_w[0], saved[0], width, late, direct)
    scatter_attn = Scatter(own_grad.reshape(model, -1), first_sends or None)
    (scatter_attn.sends,) = settle_scatters([scatter_one, scatter_two], scatter_attn.sends)
    scatter_attn.advance()
    scatter_two.gots = after(scatter_two.gots, scatter_attn.sends)
    scatter_two.rest()
    one_keep, one_send = input_grad(after(part, scatter_attn.sends, scatter_two.sends), own_acts, attn_w[0], width)

    rest = (one_keep, out_got, one_sums, two_sums, own_sums, low_rows, vectors_full)
    one_keep, out_got, one_sums, two_sums, own_sums, low_rows, vectors_full = after(rest, scatter_attn.sends)
    gain_one, down_bias = vectors_full[0:1], vectors_full[5:6]
    xhat_one, inverse_one = norm_parts(wide(low_rows))
    v_gain_one = jnp.sum(one_keep * xhat_one, axis=0, keepdims=True)
    v_shift_one = jnp.sum(one_keep, axis=0, keepdims=True)
    small = jnp.concatenate([v_gain_one, v_shift_one, vectors_two], axis=0)
    first_row = jnp.pad(jnp.concatenate((one_sums, two_sums), axis=1), ((0, 0), (0, model - hidden_width)))
    spare = jnp.zeros((1, model - 2 * width), jnp.float32)
    second_row = jnp.concatenate([own_sums[:1, :width], own_sums[:1, 2 * width :], spare], axis=1)
    small = small + tensor_swap(small, 1)
    from_y = tensor_swap(small, 2)
    small = jnp.concatenate([small + from_y, first_row, second_row], axis=0)
    out_half = inner[: 2 * rows] + (out_keep + wide(out_got) + down_bias)
    out_low = low(out_half)
    scatter_one.gots = after(scatter_one.gots, scatter_attn.sends)
    one_parts = scatter_one.finish()
    out_low, small, one_parts, one_send = settle_scatters([scatter_two, scatter_attn], out_low, small, one_parts, one_send)
    one_got = tensor_swap(one_send, 2)

    scatter_attn.advance()
    out_low, small = after((out_low, small), scatter_attn.sends)
    out_other = tensor_swap(out_low[rows:], 1)
    for mask_bit in masks[:-1]:
        small = small + data_swap(small, mask_bit)
    one_got, out_other, small = settle_scatters([scatter_attn], one_got, out_other, small)
    scatter_attn.rest()
    last = (one_got, out_other, small, scatter_two.gots)
    one_got, out_other, small, scatter_two.gots = after(last, scatter_attn.sends)
    small = small + data_swap(small, masks[-1])
    own = slice(0, 2 * rows)
    grad_normed_one = one_keep[own] + wide(one_got)
    clip_half = inner_keep + norm_back(grad_normed_one, xhat_one[own], inverse_one[own], gain_one)
    clip_other = tensor_swap(clip_half[rows:], 1)
    ff_parts = one_parts + scatter_two.finish()
    output = order_pair(out_low[:rows], out_other, core)
    clip_grad = order_pair(clip_half[:rows], clip_other, core)
    vector_own = lax.dynamic_slice_in_dim(small[:6], lax.axis_index("dp") * depth, depth, axis=1)
    joined = jnp.concatenate(ff_parts, axis=1)
    ups = [joined[:, 2 * i : 2 * i + TILE] for i in range(0, hidden_width, TILE)]
    downs = [joined[:, 2 * i + TILE : 2 * i + 2 * TILE] for i in range(0, hidden_width, TILE)]
    up_grad = jnp.concatenate(ups, axis=1)
    down_grad = jnp.concatenate(downs, axis=1).T
    scatter_attn.gots, others = pin((scatter_attn.gots, (output, clip_grad, up_grad, down_grad, small, vector_own)))
    output, clip_grad, up_grad, down_grad, small, vector_own = others
    q_grad, k_grad, v_grad, out_grad = scatter_attn.total(True, False, True)
    return (
        output,
        clip_grad,
        vector_own[0],
        vector_own[1],
        q_grad,
        small[7, :width],
        k_grad,
        v_grad,
        small[7, width : 2 * width],
        out_grad.T,
        vector_own[2],
        vector_own[3],
        vector_own[4],
        up_grad,
        small[6, :hidden_width],
        down_grad,
        vector_own[5],
    )


def solution(mesh):
    rows_spec = P("dp", "tensor", None)
    data, tensor = P("dp"), P("tensor")
    wide_spec, tall_spec = P("dp", "tensor"), P("tensor", "dp")
    placed = (
        rows_spec,
        data,
        data,
        data,
        wide_spec,
        tensor,
        wide_spec,
        wide_spec,
        tensor,
        tall_spec,
        data,
        data,
        data,
        wide_spec,
        tensor,
        tall_spec,
        data,
        rows_spec,
    )
    outs = (
        rows_spec,
        rows_spec,
        data,
        data,
        wide_spec,
        tensor,
        wide_spec,
        wide_spec,
        tensor,
        tall_spec,
        data,
        data,
        data,
        wide_spec,
        tensor,
        tall_spec,
        data,
    )
    return jax.shard_map(shards, mesh=mesh, in_specs=placed, out_specs=outs, check_vma=False)
```

```python
import jax
import jax.numpy as jnp
from jax import lax
from jax.experimental import pallas as pl
from jax.experimental.pallas import tpu as pltpu
from jax.sharding import PartitionSpec as P

HEAD_DIM = 80
norm_eps = 1e-05
VEC_ROWS = 8
TILE = 256
FIRST_TILES = 2
VMEM_LIMIT = 60 << 20


def low(values):
    return values.astype(jnp.bfloat16)


def wide(values):
    return values.astype(jnp.float32)


def mm(left, right):
    return jnp.dot(left, right, preferred_element_type=jnp.float32)


def mm_left(left, right):
    return lax.dot_general(left, right, (((0,), (0,)), ((), ())), preferred_element_type=jnp.float32)


def mm_right(left, right):
    return lax.dot_general(left, right, (((1,), (1,)), ((), ())), preferred_element_type=jnp.float32)


def norm_parts(values):
    center = values - jnp.mean(values, axis=-1, keepdims=True)
    spread = jnp.mean(center * center, axis=-1, keepdims=True)
    inverse = lax.rsqrt(spread + norm_eps)
    return center * inverse, inverse


def norm_back(grad, xhat, inverse, gain):
    scaled = grad * gain
    first = jnp.mean(scaled, axis=-1, keepdims=True)
    second = jnp.mean(scaled * xhat, axis=-1, keepdims=True)
    return (scaled - first - xhat * second) * inverse


def gelu_pair(pre):
    half = 0.5 * (1.0 + lax.erf(pre * (0.5 ** 0.5)))
    slope = half + pre * jnp.exp(-0.5 * pre * pre) * 0.3989422804014327
    return pre * half, slope


def tensor_swap(values, mask):
    size = lax.axis_size("tensor")
    return lax.ppermute(values, "tensor", [(i, i ^ mask) for i in range(size)])


def data_swap(values, mask):
    size = lax.axis_size("dp")
    return lax.ppermute(values, "dp", [(i, i ^ mask) for i in range(size)])


def masks_of(size):
    masks = []
    while size > 1:
        size //= 2
        masks.append(size)
    return masks


def pin(values, *others):
    return lax.optimization_barrier((values, others))[0]


def after(values, *others):
    return pin(values, *others) if others else values


def vmem(count):
    return [pl.BlockSpec(memory_space=pltpu.VMEM)] * count


def tiny_cost():
    return pl.CostEstimate(flops=1024, bytes_accessed=1024, transcendentals=0)


def join_body(plan, inputs, *refs):
    sources, outs, sems = refs[:inputs], refs[inputs:-1], refs[-1]
    copies = []
    for k, (source, start, columns, out, row) in enumerate(plan):
        count = sources[source].shape[0]
        origin = sources[source]
        if columns != origin.shape[2]:
            origin = origin.at[:, :, pl.ds(start, columns)]
        copies.append(pltpu.make_async_copy(origin, outs[out].at[pl.ds(row, count)], sems.at[k]))
    for item in copies:
        item.start()
    for item in copies:
        item.wait()


def join(sources, plan, shapes):
    return pl.pallas_call(
        lambda *refs: join_body(plan, len(sources), *refs),
        in_specs=[pl.BlockSpec(memory_space=pl.ANY)] * len(sources),
        out_specs=vmem(len(shapes)),
        out_shape=[jax.ShapeDtypeStruct(shape, jnp.bfloat16) for shape in shapes],
        compiler_params=pltpu.CompilerParams(vmem_limit_bytes=16 << 20),
        scratch_shapes=[pltpu.SemaphoreType.DMA((len(plan),))],
        cost_estimate=tiny_cost(),
        name="join",
    )(*sources)


class Gather:
    def __init__(self, shard):
        self.masks = masks_of(lax.axis_size("dp"))
        self.held, self.fresh = [shard[None]], []
        self.order = [[0], [0]]

    def extend(self, side, mask):
        self.order[side] = self.order[side] + [item ^ mask for item in self.order[side]]

    def early(self):
        for mask in self.masks[:-2]:
            if self.fresh:
                self.held = [jnp.concatenate([self.held[0], self.fresh[0]], axis=0)]
            self.fresh = [data_swap(self.held[0], mask)]
            self.extend(0, mask)
            self.extend(1, mask)

    def send(self, masks):
        self.fresh = [data_swap(self.held[side], masks[side]) for side in range(2)]
        for side in range(2):
            self.extend(side, masks[side])

    def second(self):
        count, rows, columns = self.held[0].shape
        half = columns // 2
        plan = [(k, side * half, half, side, k * count) for k in range(2) for side in range(2)]
        self.held = join(self.held + self.fresh, plan, [(2 * count, rows, half)] * 2)
        self.send([self.masks[-2], self.masks[-1]])

    def third(self):
        count, rows, half = self.held[0].shape
        plan = [(2 * k + side, 0, half, side, k * count) for k in range(2) for side in range(2)]
        self.held = join(list(self.held) + self.fresh, plan, [(2 * count, rows, half)] * 2)
        self.send([self.masks[-1], self.masks[-2]])


def settle(*items):
    gathers = [item for item in items if isinstance(item, Gather)]
    others = [item for item in items if not isinstance(item, Gather)]
    arrays = [(item.held, item.fresh) for item in gathers]
    arrays, others = lax.optimization_barrier((arrays, others))
    for item, (held, fresh) in zip(gathers, arrays):
        item.held, item.fresh = list(held), list(fresh)
    return others


def place_body(gathered, depth, extra, me_ref, *refs):
    pieces, outs, buffers, (in_sems, out_sems) = refs[:4], refs[4:-3], refs[-3], refs[-2:]
    me = me_ref[0]
    reads, writes = [], []
    for side in range(2):
        held, fresh = pieces[2 * side : 2 * side + 2]
        columns = held.shape[2]
        for position, item in enumerate(gathered.order[side]):
            count = held.shape[0]
            piece, row = (held, position) if position < count else (fresh, position - count)
            buffer = buffers.at[len(reads)]
            reads.append(pltpu.make_async_copy(piece.at[row], buffer, in_sems.at[len(reads)]))
            target = outs[0].at[me ^ item, :, pl.ds(side * columns, columns)]
            source = buffer.at[pl.ds(0, depth)] if extra else buffer
            group = [pltpu.make_async_copy(source, target, out_sems.at[len(writes)])]
            if extra and side == 0:
                slot = out_sems.at[2 * len(gathered.order[0]) + position]
                group.append(pltpu.make_async_copy(buffer.at[pl.ds(depth, extra)], outs[1].at[me ^ item], slot))
            writes.append(group)
    for item in reads:
        item.start()
    for item, group in zip(reads, writes):
        item.wait()
        for copy in group:
            copy.start()
    for group in writes:
        for copy in group:
            copy.wait()


def place_blocks(gathered, depth, extra=0):
    size = lax.axis_size("dp")
    pieces = [gathered.held[0], gathered.fresh[0], gathered.held[1], gathered.fresh[1]]
    columns = pieces[0].shape[2]
    if extra and depth % 8:
        whole = place_blocks(gathered, depth + extra)[0]
        return [whole[:, :depth], whole[:, depth:, :columns]]
    me = lax.axis_index("dp").reshape(1)
    shapes = [jax.ShapeDtypeStruct((size, depth, 2 * columns), jnp.bfloat16)]
    if extra:
        shapes.append(jax.ShapeDtypeStruct((size, extra, columns), jnp.bfloat16))
    return pl.pallas_call(
        lambda *refs: place_body(gathered, depth, extra, *refs),
        in_specs=[pl.BlockSpec(memory_space=pltpu.SMEM)] + [pl.BlockSpec(memory_space=pl.ANY)] * 4,
        out_specs=[pl.BlockSpec(memory_space=pl.ANY)] * len(shapes),
        out_shape=shapes,
        compiler_params=pltpu.CompilerParams(vmem_limit_bytes=VMEM_LIMIT),
        scratch_shapes=[
            pltpu.VMEM((2 * size, depth + extra, columns), jnp.bfloat16),
            pltpu.SemaphoreType.DMA((2 * size,)),
            pltpu.SemaphoreType.DMA((3 * size if extra else 2 * size,)),
        ],
        cost_estimate=tiny_cost(),
        name="place",
    )(me, *pieces)


def spread(number, masks):
    return sum(((number >> k) & 1) * mask for k, mask in enumerate(masks))


def compress(number, masks):
    return sum(((number // mask) & 1) << k for k, mask in enumerate(masks))


def sum_body(jobs, me_ref, *refs):
    me = me_ref[0]
    sems = refs[-1]
    inputs = sum(item["inputs"] for item in jobs)
    results = sum(len(item["outs"]) for item in jobs)
    buffers = refs[inputs + results : -1]
    copies = []
    first, k = 0, 0
    for job in jobs:
        for side in job["plan"]:
            for operand, start, index in side:
                columns = buffers[k].shape[2]
                for number in range(buffers[k].shape[0]):
                    source = refs[first + operand].at[index(number, me), :, pl.ds(start, columns)]
                    copies.append(pltpu.make_async_copy(source, buffers[k].at[number], sems.at[len(copies)]))
                    copies[-1].start()
                k += 1
        first += job["inputs"]
    for item in copies:
        item.wait()
    k = 0
    for job in jobs:
        outs = refs[first : first + len(job["outs"])]
        first += len(job["outs"])
        for side, terms in enumerate(job["plan"]):
            total = wide(buffers[k][...])
            for buffer in buffers[k + 1 : k + len(terms)]:
                total = total + wide(buffer[...])
            k += len(terms)
            columns = total.shape[-1]
            if job["split"]:
                for part in range(2):
                    outs[2 * side + part][...] = total[0, :, part * columns // 2 : (part + 1) * columns // 2]
            elif job["merged"]:
                outs[0][:, :, side * columns : (side + 1) * columns] = total.astype(outs[0].dtype)
            else:
                outs[side][...] = total.astype(outs[side].dtype)


def run_sums(jobs):
    operands, outs, scratch, count = [], [], [], 0
    for job in jobs:
        operands += job["operands"]
        outs += job["outs"]
        scratch += job["scratch"]
        count += job["copies"]
    results = pl.pallas_call(
        lambda *refs: sum_body(jobs, *refs),
        in_specs=[pl.BlockSpec(memory_space=pltpu.SMEM)] + [pl.BlockSpec(memory_space=pl.ANY)] * len(operands),
        out_specs=vmem(len(outs)),
        out_shape=outs,
        scratch_shapes=scratch + [pltpu.SemaphoreType.DMA((count,))],
        compiler_params=pltpu.CompilerParams(vmem_limit_bytes=VMEM_LIMIT),
        cost_estimate=tiny_cost(),
        name="sum_blocks",
    )(lax.axis_index("dp").reshape(1), *operands)
    groups = []
    for job in jobs:
        groups.append(list(results[: len(job["outs"])]))
        results = results[len(job["outs"]) :]
    return groups


def scatter_masks(size):
    masks = masks_of(size)[::-1]
    return [masks, [masks[1], masks[0]] + masks[2:]]


class Scatter:
    def __init__(self, own, sends=None):
        self.sends = sends
        self.size = lax.axis_size("dp")
        self.half = own.shape[1] // 2
        self.depth = own.shape[0] // self.size
        self.own = own.reshape(self.size, self.depth, own.shape[1])
        self.masks = scatter_masks(self.size)
        self.gots = []
        self.step = 0

    def remaining(self, side, step):
        return sorted(set(self.masks[side]) - set(self.masks[side][: step + 1]))

    def total(self, final, merged, split=False):
        return run_sums([self.job(final, merged, split)])[0]

    def job(self, final, merged, split=False):
        step = self.step
        last = len(self.masks[0]) == step
        count = 1 if last else self.size >> (step + 1)
        operands = [self.own]
        for got in self.gots:
            operands += got
        plan = []
        for side in range(2):
            rest = [] if last else self.remaining(side, step)
            before = sum(self.masks[side][:step])
            flip = 0 if last else self.masks[side][step]

            def block(number, me, rest=rest, before=before, flip=flip):
                return (me & before) | ((me ^ flip) & flip) | spread(number, rest)

            terms = [(0, side * self.half, block)]
            operand = 1
            for number, got in enumerate(self.gots):
                kept = self.remaining(side, number)
                which, start = (operand, side * self.half) if len(got) == 1 else (operand + side, 0)
                terms.append((which, start, lambda item, me, block=block, kept=kept: compress(block(item, me), kept)))
                operand += len(got)
            plan.append(terms)
        counts = [len(item) for item in plan]
        dtype = jnp.float32 if final else jnp.bfloat16
        columns = 2 * self.half if merged else self.half
        outs = [jax.ShapeDtypeStruct((count, self.depth, columns), dtype)] * (1 if merged else 2)
        if split:
            outs = [jax.ShapeDtypeStruct((self.depth, self.half // 2), dtype)] * 4
        buffers = [pltpu.VMEM((count, self.depth, self.half), jnp.bfloat16)] * sum(counts)
        return dict(
            plan=plan,
            merged=merged,
            split=split,
            operands=operands,
            inputs=len(operands),
            outs=outs,
            scratch=buffers,
            copies=count * sum(counts),
        )

    def prepare(self):
        self.sends = self.total(False, self.step >= 2)
        return self.sends

    def launch(self):
        masks = [self.masks[side][self.step] for side in range(len(self.sends))]
        self.gots = self.gots + [[data_swap(send, mask) for send, mask in zip(self.sends, masks)]]
        self.step += 1

    def advance(self):
        if self.step > 0 or self.sends is None:
            self.prepare()
        self.launch()

    def rest(self):
        while self.step < len(self.masks[0]):
            self.advance()

    def finish(self):
        return [item[0] for item in self.total(True, False)]


def advance_both(*scatters):
    sends = run_sums([item.job(False, item.step >= 2) for item in scatters])
    for item, send in zip(scatters, sends):
        item.sends = send
        item.launch()


def settle_scatters(scatters, *others):
    gots, others = lax.optimization_barrier(([item.gots for item in scatters], others))
    for item, got in zip(scatters, gots):
        item.gots = got
    return others


def ff_body(first, tiles, half, *refs):
    n2, cot, own_up, own_down, sib_up, sib_down, own_b, sib_b = refs[:8]
    if first:
        acc_b, acc_g, own_acts, sib_acts = refs[8:]
    else:
        prev_b, prev_g, out_keep, out_send, grad_keep, grad_send, own_acts, sib_acts, acc_b, acc_g, *late, sems = refs[8:]
        copies = [pltpu.make_async_copy(item, late[k], sems.at[k]) for k, item in enumerate((prev_b, prev_g))]
    side, tile = pl.program_id(0), pl.program_id(1)

    @pl.when((side == 0) & (tile == 0))
    def _():
        acc_b[...] = jnp.zeros_like(acc_b)
        acc_g[...] = jnp.zeros_like(acc_g)
        if not first:
            for item in copies:
                item.start()

    def step(up_ref, down_ref, bias, acts):
        up, down = up_ref[...], down_ref[...]
        width = up.shape[1]
        pre = mm(n2[...], up) + wide(bias[...])
        act, slope = gelu_pair(pre)
        hidden = low(act)
        grad_pre = low(mm(cot[...], down) * slope)
        acc_b[...] += mm_right(hidden, down)
        acc_g[...] += mm_right(grad_pre, up)
        acts[:, :width] = grad_pre
        acts[:, width:] = hidden

    @pl.when(side == 0)
    def _():
        step(sib_up, sib_down, sib_b, sib_acts)

    @pl.when(side == 1)
    def _():
        step(own_up, own_down, own_b, own_acts)

    if not first:

        @pl.when((side == 1) & (tile == tiles - 1))
        def _():
            for item in copies:
                item.wait()
            out_keep[...] = acc_b[:half] + late[0][:half]
            out_send[...] = low(acc_b[half:] + late[0][half:])
            grad_keep[...] = acc_g[...] + late[1][...]
            grad_send[:half] = low(grad_keep[half:])
            grad_send[half:] = low(grad_keep[:half])


def side_specs(tiles):
    def second(shape, start=0):
        return pl.BlockSpec(shape, lambda s, i: (0, start + jnp.where(s == 1, i, 0)))

    def initial(shape, start=0):
        return pl.BlockSpec(shape, lambda s, i: (0, start + jnp.where(s == 0, i, tiles - 1)))

    return second, initial


def const_spec(shape):
    return pl.BlockSpec(shape, lambda s, i: (0, 0), pipeline_mode=pl.Buffered(1))


def feed_forward(n2, cot, own_w, sib_w, own_b, sib_b, tile, previous=()):
    rows, model = n2.shape
    hidden = own_b.shape[1]
    tiles = hidden // tile
    first = not previous
    half = rows // 2
    second, initial = side_specs(tiles)
    in_specs = [const_spec(n2.shape)] * 2
    in_specs += [second((model, tile)), second((model, tile), tiles), initial((model, tile)), initial((model, tile), tiles)]
    in_specs += [second((1, tile)), initial((1, tile))]
    in_specs += [pl.BlockSpec(memory_space=pl.ANY) for item in previous]
    operands = [n2, cot, own_w, own_w, sib_w, sib_w, own_b, sib_b, *previous]
    full = jax.ShapeDtypeStruct((rows, model), jnp.float32)
    acts = jax.ShapeDtypeStruct((rows, 2 * hidden), jnp.bfloat16)
    shapes = [full, full]
    scratch = []
    if not first:
        shapes = [
            jax.ShapeDtypeStruct((half, model), jnp.float32),
            jax.ShapeDtypeStruct((half, model), jnp.bfloat16),
            full,
            jax.ShapeDtypeStruct((rows, model), jnp.bfloat16),
        ]
        scratch = [pltpu.VMEM((rows, model), jnp.float32)] * 4 + [pltpu.SemaphoreType.DMA((2,))]
    specs = [const_spec(item.shape) for item in shapes]
    specs += [second((rows, 2 * tile)), initial((rows, 2 * tile))]
    return pl.pallas_call(
        lambda *refs: ff_body(first, tiles, half, *refs),
        grid=(2, tiles),
        in_specs=in_specs,
        out_specs=specs,
        out_shape=shapes + [acts, acts],
        scratch_shapes=scratch,
        compiler_params=pltpu.CompilerParams(vmem_limit_bytes=VMEM_LIMIT),
        cost_estimate=tiny_cost(),
        name="feed_forward",
    )(*operands)


def weight_grads_body(size, me_ref, n2t, sib_n2t, cott, sib_cott, acts, sib_acts, grads, sums, *sends):
    width = acts.shape[1] // 2
    grads[:, :width] = low(mm(n2t[...], acts[:, :width]) + mm(sib_n2t[...], sib_acts[:, :width]))
    grads[:, width:] = low(mm(cott[...], acts[:, width:]) + mm(sib_cott[...], sib_acts[:, width:]))
    masks = scatter_masks(size) if sends else []
    for side, send in enumerate(sends):

        @pl.when(pl.program_id(0) == side)
        def _(side=side, send=send):
            mask = masks[side][0]
            rest = sorted(set(masks[side]) - {mask})
            depth = send.shape[1]
            for number in range(size // 2):
                block = ((me_ref[0] ^ mask) & mask) | spread(number, rest)
                send[number] = grads[pl.ds(pl.multiple_of(block * depth, 16), depth), :]

    total = jnp.sum(wide(acts[:, :width]), axis=0, keepdims=True)
    sums[...] = total + jnp.sum(wide(sib_acts[:, :width]), axis=0, keepdims=True)


def weight_grads(left, acts, sib_acts, tile, size=0):
    model, rows = left[0].shape
    tiles = acts.shape[1] // (2 * tile)
    const = pl.BlockSpec((model, rows), lambda i: (0, 0), pipeline_mode=pl.Buffered(1))
    out_specs = [pl.BlockSpec((model, 2 * tile), lambda i: (0, i)), pl.BlockSpec((1, tile), lambda i: (0, i))]
    shapes = [
        jax.ShapeDtypeStruct((model, acts.shape[1]), jnp.bfloat16),
        jax.ShapeDtypeStruct((1, acts.shape[1] // 2), jnp.float32),
    ]
    if size:
        send = (size // 2, model // size, 2 * tile)
        out_specs += [pl.BlockSpec(send, lambda i: (0, 0, 0))] * 2
        shapes += [jax.ShapeDtypeStruct(send, jnp.bfloat16)] * 2
    return pl.pallas_call(
        lambda *refs: weight_grads_body(size, *refs),
        grid=(tiles,),
        in_specs=[pl.BlockSpec(memory_space=pltpu.SMEM)] + [const] * 4 + [pl.BlockSpec((rows, 2 * tile), lambda i: (0, i))] * 2,
        out_specs=out_specs,
        out_shape=shapes,
        compiler_params=pltpu.CompilerParams(vmem_limit_bytes=VMEM_LIMIT),
        cost_estimate=tiny_cost(),
        name="weight_grads",
    )(lax.axis_index("dp").reshape(1), *left, acts, sib_acts)


def prepare_body(*refs):
    vectors, (w_query, w_key, w_value, w_out_t), out = refs[:6], refs[6:10], refs[10]
    depth, width = w_query.shape
    out[:depth] = jnp.concatenate([w_query[...], w_key[...], w_value[...], w_out_t[...]], axis=1)
    out[depth:] = jnp.zeros_like(out[depth:])
    for k, vector in enumerate(vectors):
        out[depth + k : depth + k + 1, :depth] = vector[...].reshape(1, depth)


def prepare(vectors, weights):
    depth, width = weights[0].shape
    return pl.pallas_call(
        prepare_body,
        in_specs=vmem(10),
        out_specs=pl.BlockSpec(memory_space=pltpu.VMEM),
        out_shape=jax.ShapeDtypeStruct((depth + VEC_ROWS, 4 * width), jnp.bfloat16),
        compiler_params=pltpu.CompilerParams(vmem_limit_bytes=VMEM_LIMIT),
        cost_estimate=tiny_cost(),
        name="prepare",
    )(*vectors, *weights)


def assemble_body(half, mine, other_rows, other_cot, rows, cot, cot_t):
    rows[:half] = mine[:half]
    rows[half:] = other_rows[...]
    cot[:half] = mine[half:]
    cot[half:] = other_cot[...]
    cot_t[...] = cot[...].T


def assemble(mine, other_rows, other_cot):
    rows, model = mine.shape
    shape = jax.ShapeDtypeStruct((rows, model), jnp.bfloat16)
    return pl.pallas_call(
        lambda *refs: assemble_body(rows // 2, *refs),
        in_specs=vmem(3),
        out_specs=vmem(3),
        out_shape=[shape, shape, jax.ShapeDtypeStruct((model, rows), jnp.bfloat16)],
        compiler_params=pltpu.CompilerParams(vmem_limit_bytes=VMEM_LIMIT),
        cost_estimate=tiny_cost(),
        name="assemble",
    )(mine, other_rows, other_cot)


def dot_t(left, right):
    return lax.dot_general(left, right, (((0,), (0,)), ((), ())), preferred_element_type=jnp.float32)


def norm_rows(values, gain, shift):
    xhat, inverse = norm_parts(values)
    return low(xhat * gain + shift)


def fill_mask(where, mask):
    count = mask.shape[0] // 4
    for k in range(4):
        position = (where[0] ^ k) * count + lax.broadcasted_iota(jnp.int32, (count, 1), 0)
        mask[k * count : (k + 1) * count] = (position < where[1]).astype(jnp.float32)


def attn_head(joined, head, width, mask):
    scale = HEAD_DIM ** (-0.5)
    begin = pl.multiple_of(head * HEAD_DIM, 16)
    query = joined[pl.ds(begin, HEAD_DIM), :]
    keys = joined[pl.ds(pl.multiple_of(width + begin, 16), HEAD_DIM), :]
    values = joined[pl.ds(pl.multiple_of(2 * width + begin, 16), HEAD_DIM), :]
    scores = jnp.where(mask[...] > 0.5, dot_t(keys, query) * scale, -1000000000.0)
    return begin, query, keys, values, scores


def attn_forward_body(first, width, *refs):
    if first:
        where, x, vectors, weights, bias, n1, n1t, joined, mixed, totals, part, mask = refs
        n1[...] = norm_rows(wide(x[...]), vectors[0:1], vectors[1:2])
        n1t[...] = n1[...].T
    else:
        where, n1, previous, weights, bias, joined, mixed, totals, part, send_one, send_two, mask = refs
    fill_mask(where, mask)
    joined[...] = low(mm(n1[...], weights[:, : 3 * width]) + bias[...]).T

    def one(head, carry):
        begin, query, keys, values, scores = attn_head(joined, head, width, mask)
        top = jnp.max(scores, axis=0, keepdims=True)
        expo = jnp.exp(scores - top)
        total = jnp.sum(expo, axis=0, keepdims=True)
        probs = low(expo * (1.0 / total))
        mixed[pl.ds(begin, HEAD_DIM), :] = low(mm(values, probs))
        totals[pl.ds(head, 1), :] = top + jnp.log(total)
        return carry

    lax.fori_loop(0, width // HEAD_DIM, one, 0, unroll=True)
    term = mm_right(mixed[...].T, weights[:, 3 * width :])
    if first:
        part[...] = term
    else:
        term = previous[...] + term
        half = term.shape[0] // 2
        part[...] = term
        send_one[...] = low(term[half:])
        send_two[...] = low(term[:half])


def attn_forward(where, head_in, weights, bias, width, first):
    rows, model = head_in[0].shape
    low_shape = lambda *shape: jax.ShapeDtypeStruct(shape, jnp.bfloat16)
    wide_shape = lambda *shape: jax.ShapeDtypeStruct(shape, jnp.float32)
    shapes = [low_shape(3 * width, rows), low_shape(width, rows), wide_shape(width // HEAD_DIM, rows), wide_shape(rows, model)]
    shapes = [low_shape(rows, model), low_shape(model, rows)] + shapes if first else shapes + [low_shape(rows // 2, model)] * 2
    operands = [where] + list(head_in) + [weights, bias]
    return pl.pallas_call(
        lambda *refs: attn_forward_body(first, width, *refs),
        in_specs=[pl.BlockSpec(memory_space=pltpu.SMEM)] + vmem(len(operands) - 1),
        out_specs=vmem(len(shapes)),
        out_shape=shapes,
        scratch_shapes=[pltpu.VMEM((rows, 1), jnp.float32)],
        compiler_params=pltpu.CompilerParams(vmem_limit_bytes=VMEM_LIMIT),
        cost_estimate=tiny_cost(),
        name="attn_forward",
    )(*operands)


def attn_backward_body(first, width, size, *refs):
    where, gb, weights, joined, totals = refs[:5]
    if first:
        mixed, part, acts, gmt, djoined, mask = refs[5:]
    else:
        late, outs, scratch = refs[5:11], refs[11:-9], refs[-9:]
        gmt, mask, *buffers, sems = scratch
        djoined, grads = outs[0], outs[1]
        copies = [pltpu.make_async_copy(item, buffer, sems.at[k]) for k, (item, buffer) in enumerate(zip(late, buffers))]
        for item in copies:
            item.start()
        gbt, sib_gbt, n1t, sib_n1t, mixed, sib_acts = buffers
    scale = HEAD_DIM ** (-0.5)
    fill_mask(where, mask)
    gmt[...] = low(mm(gb[...], weights[:, 3 * width :])).T

    def one(head, carry):
        begin, query, keys, values, scores = attn_head(joined, head, width, mask)
        probs = jnp.exp(scores - totals[pl.ds(head, 1), :])
        gm = gmt[pl.ds(begin, HEAD_DIM), :]
        grad_probs = dot_t(values, gm)
        delta = jnp.sum(grad_probs * probs, axis=0, keepdims=True)
        grad_scores = low(probs * (grad_probs - delta))
        djoined[pl.ds(begin, HEAD_DIM), :] = low(mm(keys, grad_scores) * scale)
        djoined[pl.ds(pl.multiple_of(width + begin, 16), HEAD_DIM), :] = low(mm_right(query, grad_scores) * scale)
        djoined[pl.ds(pl.multiple_of(2 * width + begin, 16), HEAD_DIM), :] = low(mm_right(gm, low(probs)))
        return carry

    lax.fori_loop(0, width // HEAD_DIM, one, 0, unroll=True)
    if first:
        acts[: 3 * width] = djoined[...]
        acts[3 * width :] = mixed[...]
        part[...] = mm_right(djoined[...].T, weights[:, : 3 * width])
        return
    for item in copies:
        item.wait()
    copies = []
    ones = jnp.ones((8, gb.shape[0]), jnp.bfloat16)
    outs[2][...] = mm_right(ones, djoined[...]) + mm_right(ones, sib_acts[: 3 * width])
    grad_qkv = low(mm_right(n1t[...], djoined[...]) + mm_right(sib_n1t[...], sib_acts[: 3 * width]))
    grad_out = low(mm_right(gbt[...], mixed[...]) + mm_right(sib_gbt[...], sib_acts[3 * width :]))
    if size:
        grads[:, :, : 3 * width] = grad_qkv.reshape(size, -1, 3 * width)
        grads[:, :, 3 * width :] = grad_out.reshape(size, -1, width)
        masks = scatter_masks(size)
        for side in range(2):
            mask = masks[side][0]
            rest = sorted(set(masks[side]) - {mask})
            for number in range(size // 2):
                block = ((where[2] ^ mask) & mask) | spread(number, rest)
                source = grads.at[block, :, pl.ds(side * 2 * width, 2 * width)]
                copies.append(pltpu.make_async_copy(source, outs[3 + side].at[number], sems.at[6 + len(copies)]))
                copies[-1].start()
    else:
        grads[:, : 3 * width] = grad_qkv
        grads[:, 3 * width :] = grad_out
    for item in copies:
        item.wait()


def attn_backward(where, gb, weights, saved, width, late=(), size=0):
    rows, model = gb.shape
    first = not late
    joined, mixed, totals = saved
    operands = [where, gb, weights, joined, totals]
    specs = [pl.BlockSpec(memory_space=pltpu.SMEM)] + vmem(4)
    low_shape = lambda *shape: jax.ShapeDtypeStruct(shape, jnp.bfloat16)
    full = jax.ShapeDtypeStruct((rows, model), jnp.float32)
    scratch = [
        pltpu.VMEM((width, rows), jnp.bfloat16),
        pltpu.VMEM((3 * width, rows), jnp.bfloat16),
        pltpu.VMEM((rows, 1), jnp.float32),
    ]
    if first:
        operands.append(mixed)
        specs += vmem(1)
        shapes = [full, low_shape(4 * width, rows)]
        out_specs = vmem(2)
    else:
        gbt, sib_gbt, n1t, sib_n1t, sib_acts = late
        late = [gbt, sib_gbt, n1t, sib_n1t, mixed, sib_acts]
        operands += late
        specs += [pl.BlockSpec(memory_space=pl.ANY)] * len(late)
        del scratch[1]
        scratch += [pltpu.VMEM(item.shape, item.dtype) for item in late] + [pltpu.SemaphoreType.DMA((len(late) + size,))]
        grads = low_shape(size, model // size, 4 * width) if size else low_shape(model, 4 * width)
        shapes = [low_shape(3 * width, rows), grads, jax.ShapeDtypeStruct((8, 3 * width), jnp.float32)]
        out_specs = vmem(3)
        if size:
            shapes += [low_shape(size // 2, model // size, 2 * width)] * 2
            out_specs += [pl.BlockSpec(memory_space=pl.ANY)] * 2
    return pl.pallas_call(
        lambda *refs: attn_backward_body(first, width, size, *refs),
        in_specs=specs,
        out_specs=out_specs,
        out_shape=shapes,
        scratch_shapes=scratch,
        compiler_params=pltpu.CompilerParams(vmem_limit_bytes=VMEM_LIMIT),
        cost_estimate=tiny_cost(),
        name="attn_backward",
    )(*operands)


def input_grad_body(width, half, previous, acts, weights, keep, send):
    term = previous[...] + mm_right(acts[...].T, weights[:, : 3 * width])
    keep[...] = term
    send[...] = low(term[half:])


def input_grad(previous, acts, weights, width):
    rows, model = previous.shape
    return pl.pallas_call(
        lambda *refs: input_grad_body(width, rows // 2, *refs),
        in_specs=vmem(3),
        out_specs=vmem(2),
        out_shape=[jax.ShapeDtypeStruct((rows, model), jnp.float32), jax.ShapeDtypeStruct((rows // 2, model), jnp.bfloat16)],
        compiler_params=pltpu.CompilerParams(vmem_limit_bytes=VMEM_LIMIT),
        cost_estimate=tiny_cost(),
        name="input_grad",
    )(previous, acts, weights)


def middle_body(x, part, got_one, got_two, vectors, inner, n2, n2t, stats):
    got = jnp.where(pl.program_id(0) < 2, wide(got_one[...]), wide(got_two[...]))
    value = wide(x[...]) + (part[...] + got + vectors[2:3])
    inner[...] = value
    mean = jnp.mean(value, axis=-1, keepdims=True)
    center = value - mean
    inverse = lax.rsqrt(jnp.mean(center * center, axis=-1, keepdims=True) + norm_eps)
    n2[...] = low(center * inverse * vectors[3:4] + vectors[4:5])
    stats[:, 0:1] = mean
    stats[:, 1:2] = inverse
    n2t[...] = n2[...].T


def row_spec(block, model):
    return pl.BlockSpec((block, model), lambda i: (i, 0))


def middle(x, part, got_one, got_two, vectors):
    rows, model = x.shape
    block = rows // 4
    shapes = [
        jax.ShapeDtypeStruct((rows, model), jnp.float32),
        jax.ShapeDtypeStruct((rows, model), jnp.bfloat16),
        jax.ShapeDtypeStruct((model, rows), jnp.bfloat16),
        jax.ShapeDtypeStruct((rows, 2), jnp.float32),
    ]
    return pl.pallas_call(
        middle_body,
        grid=(4,),
        in_specs=[row_spec(block, model)] * 2
        + [pl.BlockSpec((block, model), lambda i: (jnp.minimum(i, 1), 0)), pl.BlockSpec((block, model), lambda i: (jnp.maximum(i - 2, 0), 0))]
        + [pl.BlockSpec(vectors.shape, lambda i: (0, 0))],
        out_specs=[row_spec(block, model)] * 2 + [pl.BlockSpec((model, block), lambda i: (0, i)), row_spec(block, 2)],
        out_shape=shapes,
        compiler_params=pltpu.CompilerParams(vmem_limit_bytes=VMEM_LIMIT),
        cost_estimate=tiny_cost(),
        name="middle",
    )(x, part, got_one, got_two, vectors)


def turn_body(inner, stats, grad, got, cot, vectors, keep, gb, gbt, sums):
    step = pl.program_id(0)
    value = grad[...] + wide(got[...])
    inverse = stats[:, 1:2]
    xhat = (inner[...] - stats[:, 0:1]) * inverse
    top = wide(cot[...])
    total = top + norm_back(value, xhat, inverse, vectors[3:4])
    gb[...] = low(total)
    gbt[...] = gb[...].T

    @pl.when(step < 2)
    def _():
        keep[...] = total
        parts = [jnp.sum(item, axis=0, keepdims=True) for item in (wide(low(total)), value * xhat, value, top)]
        joined = jnp.concatenate(parts, axis=0)
        sums[...] = jnp.where(step == 0, joined, sums[...] + joined)


def turn(inner, stats, grad, got, cot, vectors):
    rows, model = inner.shape
    block = rows // 4
    shapes = [
        jax.ShapeDtypeStruct((rows // 2, model), jnp.float32),
        jax.ShapeDtypeStruct((rows, model), jnp.bfloat16),
        jax.ShapeDtypeStruct((model, rows), jnp.bfloat16),
        jax.ShapeDtypeStruct((4, model), jnp.float32),
    ]
    return pl.pallas_call(
        turn_body,
        grid=(4,),
        in_specs=[row_spec(block, model), row_spec(block, 2)] + [row_spec(block, model)] * 3 + [pl.BlockSpec(vectors.shape, lambda i: (0, 0))],
        out_specs=[
            pl.BlockSpec((block, model), lambda i: (jnp.minimum(i, 1), 0)),
            row_spec(block, model),
            pl.BlockSpec((model, block), lambda i: (0, i)),
            pl.BlockSpec((4, model), lambda i: (0, 0)),
        ],
        out_shape=shapes,
        compiler_params=pltpu.CompilerParams(vmem_limit_bytes=VMEM_LIMIT),
        cost_estimate=tiny_cost(),
        name="turn",
    )(inner, stats, grad, got, cot, vectors)


def pick(pair, index):
    return lax.dynamic_index_in_dim(pair, index, axis=0, keepdims=False)


def order_pair(mine, other, core):
    return jnp.where(core == 0, jnp.stack([mine, other]), jnp.stack([other, mine]))


def shards(
    clips,
    lengths,
    norm1_gain,
    norm1_bias,
    w_query,
    bias_query,
    w_key,
    w_value,
    bias_value,
    w_out,
    bias_out,
    norm2_gain,
    norm2_bias,
    w_up,
    bias_up,
    w_down,
    bias_down,
    cotangent,
):
    rows = clips.shape[1]
    model = clips.shape[2]
    depth, width = w_query.shape
    hidden_width = w_up.shape[1]
    data_size = lax.axis_size("dp")
    place = lax.axis_index("tensor")
    core = place % 2
    masks = masks_of(data_size)

    vectors = (norm1_gain, norm1_bias, bias_out, norm2_gain, norm2_bias, bias_down)
    attn = Gather(prepare(vectors, (w_query, w_key, w_value, w_out.T)))
    attn.early()
    pair, cot_pair = after((clips, cotangent), attn.held)
    sent = jnp.concatenate([pick(pair, 1 - core), pick(cot_pair, 1 - core)], axis=0)
    got = tensor_swap(sent, 1)
    half_clip = jnp.concatenate([pick(pair, core), got[:rows]], axis=0)
    half_cot = jnp.concatenate([pick(cot_pair, core), got[rows:]], axis=0)
    other_clip = tensor_swap(half_clip, 2)
    local_bias = jnp.concatenate([bias_up, bias_query, bias_value])
    sib_bias = tensor_swap(local_bias.reshape(1, -1), 1)[0]
    cut = FIRST_TILES * TILE
    down_t = w_down.T
    ff_one = Gather(jnp.concatenate([w_up[:, :cut], down_t[:, :cut]], axis=1))
    ff_two = Gather(jnp.concatenate([w_up[:, cut:], down_t[:, cut:]], axis=1))
    where = jnp.stack([place, pick(lengths, core), lax.axis_index("dp")]).astype(jnp.int32)
    other_clip, half_cot, sib_bias, where = settle(attn, ff_one, ff_two, other_clip, half_cot, sib_bias, where)

    attn.second()
    other_cot = tensor_swap(half_cot, 2)
    biases = (local_bias.reshape(1, -1), sib_bias.reshape(1, -1))
    joined_biases = []
    for item in biases:
        item = wide(item[:, hidden_width:])
        joined_biases.append(jnp.concatenate([item[:, :width], jnp.zeros((1, width), jnp.float32), item[:, width:]], axis=1))
    joined_biases, other_clip = settle(attn, ff_one, joined_biases, other_clip)

    attn.third()
    ff_one.early()
    low_rows, cot, cott = assemble(jnp.concatenate([half_clip, half_cot], axis=0), other_clip, other_cot)
    low_rows, cot, cott = settle(attn, ff_one, ff_two, low_rows, cot, cott)

    attn_all, vector_all = place_blocks(attn, depth, VEC_ROWS)
    attn_own = attn_all.reshape(model, model)
    attn_sib = tensor_swap(attn_own, 1)
    attn_w = (attn_own, attn_sib)
    ff_one.second()
    ff_two.early()
    sib_cott = tensor_swap(cott, 1)
    vectors_full = wide(vector_all[:, :6, :depth].transpose(1, 0, 2).reshape(6, model))
    outs = attn_forward(where, (low_rows, vectors_full), attn_own, joined_biases[0], width, True)
    normed_one, n1t = outs[:2]
    saved = [outs[2:5]]
    outs = attn_forward(where, (normed_one, outs[5]), attn_sib, joined_biases[1], width, False)
    saved.append(outs[:3])
    part_keep, *part_send = outs[3:]

    def ff_weights(gathered):
        own_w = place_blocks(gathered, depth)[0].reshape(model, -1)
        return own_w, tensor_swap(own_w, 1)

    part_send, sib_cott, n1t = settle(ff_one, ff_two, part_send, sib_cott, n1t)
    got_one = tensor_swap(part_send[0], 2)
    ff_one.third()
    got_one, part_two, n1t = settle(ff_one, got_one, part_send[1], n1t)
    got_two = tensor_swap(part_two, 2)
    ff_two.second()
    one_own, one_sib = ff_weights(ff_one)
    sib_n1t = tensor_swap(n1t, 1)
    got_one, got_two, one_own = settle(ff_two, got_one, got_two, one_own)
    ff_two.third()
    inner, normed_two, n2t, stats = middle(low_rows, part_keep, got_one, got_two, vectors_full)
    bias_rows = [[item[:, :cut], item[:, cut:hidden_width]] for item in biases]
    outs = feed_forward(normed_two, cot, one_own, one_sib, bias_rows[0][0], bias_rows[1][0], TILE)
    sums_so_far, own_acts, other_acts = outs[:2], outs[2], outs[3]
    sums_so_far, other_acts, n2t, sib_n1t = settle(ff_two, sums_so_far, other_acts, n2t, sib_n1t)
    sib_n2t = tensor_swap(n2t, 1)
    sib_acts = tensor_swap(other_acts, 1)
    two_own = place_blocks(ff_two, depth)[0].reshape(model, -1)
    sib_acts, sib_n2t, two_own = settle(sib_acts, sib_n2t, two_own)
    two_sib = tensor_swap(two_own, 1)
    left = (n2t, sib_n2t, cott, sib_cott)
    direct = data_size if depth % 16 == 0 and FIRST_TILES == 2 else 0
    one_grad, one_sums, *first_sends = weight_grads(left, own_acts, sib_acts, TILE, direct)
    scatter_one = Scatter(one_grad, first_sends or None)
    scatter_one.advance()
    sums_so_far, two_sib = after((sums_so_far, two_sib), scatter_one.sends)
    outs = feed_forward(normed_two, cot, two_own, two_sib, bias_rows[0][1], bias_rows[1][1], TILE, sums_so_far)
    out_keep, out_send, grad_keep, grad_send, own_acts, other_acts = settle_scatters([scatter_one], *outs)

    grad_got = tensor_swap(grad_send, 2)
    sib_acts = tensor_swap(other_acts, 1)
    scatter_one.advance()
    two_grad, two_sums = weight_grads(left, own_acts, sib_acts, TILE)
    out_send, two_grad = settle_scatters([scatter_one], out_send, two_grad)
    scatter_two = Scatter(two_grad)
    scatter_two.advance()
    grad_got = after(grad_got, scatter_two.sends)
    inner_keep, grad_branch, gbt, vectors_two = turn(inner, stats, grad_keep, grad_got, cot, vectors_full)
    grad_branch, gbt, out_send = settle_scatters([scatter_two], grad_branch, gbt, out_send)
    sib_gbt = tensor_swap(gbt, 1)
    out_got = tensor_swap(out_send, 2)
    advance_both(scatter_one, scatter_two)
    scatter_one.rest()
    grad_branch = after(grad_branch, scatter_one.sends, scatter_two.sends)
    part, other_acts = attn_backward(where, grad_branch, attn_w[1], saved[1], width)
    part, other_acts, sib_gbt = settle(part, other_acts, sib_gbt)
    sib_acts = tensor_swap(other_acts, 1)
    late = (gbt, sib_gbt, n1t, sib_n1t, sib_acts)
    direct = data_size if depth % 16 == 0 else 0
    own_acts, own_grad, own_sums, *first_sends = attn_backward(where, grad_branch, attn_w[0], saved[0], width, late, direct)
    scatter_attn = Scatter(own_grad.reshape(model, -1), first_sends or None)
    (scatter_attn.sends,) = settle_scatters([scatter_one, scatter_two], scatter_attn.sends)
    scatter_attn.advance()
    scatter_two.gots = after(scatter_two.gots, scatter_attn.sends)
    scatter_two.rest()
    one_keep, one_send = input_grad(after(part, scatter_attn.sends, scatter_two.sends), own_acts, attn_w[0], width)

    rest = (one_keep, out_got, one_sums, two_sums, own_sums, low_rows, vectors_full)
    one_keep, out_got, one_sums, two_sums, own_sums, low_rows, vectors_full = after(rest, scatter_attn.sends)
    gain_one, down_bias = vectors_full[0:1], vectors_full[5:6]
    xhat_one, inverse_one = norm_parts(wide(low_rows))
    v_gain_one = jnp.sum(one_keep * xhat_one, axis=0, keepdims=True)
    v_shift_one = jnp.sum(one_keep, axis=0, keepdims=True)
    small = jnp.concatenate([v_gain_one, v_shift_one, vectors_two], axis=0)
    first_row = jnp.pad(jnp.concatenate((one_sums, two_sums), axis=1), ((0, 0), (0, model - hidden_width)))
    spare = jnp.zeros((1, model - 2 * width), jnp.float32)
    second_row = jnp.concatenate([own_sums[:1, :width], own_sums[:1, 2 * width :], spare], axis=1)
    small = small + tensor_swap(small, 1)
    from_y = tensor_swap(small, 2)
    small = jnp.concatenate([small + from_y, first_row, second_row], axis=0)
    out_half = inner[: 2 * rows] + (out_keep + wide(out_got) + down_bias)
    out_low = low(out_half)
    scatter_one.gots = after(scatter_one.gots, scatter_attn.sends)
    one_parts = scatter_one.finish()
    out_low, small, one_parts, one_send = settle_scatters([scatter_two, scatter_attn], out_low, small, one_parts, one_send)
    one_got = tensor_swap(one_send, 2)

    scatter_attn.advance()
    out_low, small = after((out_low, small), scatter_attn.sends)
    out_other = tensor_swap(out_low[rows:], 1)
    for mask_bit in masks[:-1]:
        small = small + data_swap(small, mask_bit)
    one_got, out_other, small = settle_scatters([scatter_attn], one_got, out_other, small)
    scatter_attn.rest()
    last = (one_got, out_other, small, scatter_two.gots)
    one_got, out_other, small, scatter_two.gots = after(last, scatter_attn.sends)
    small = small + data_swap(small, masks[-1])
    own = slice(0, 2 * rows)
    grad_normed_one = one_keep[own] + wide(one_got)
    clip_half = inner_keep + norm_back(grad_normed_one, xhat_one[own], inverse_one[own], gain_one)
    clip_other = tensor_swap(clip_half[rows:], 1)
    ff_parts = one_parts + scatter_two.finish()
    output = order_pair(out_low[:rows], out_other, core)
    clip_grad = order_pair(clip_half[:rows], clip_other, core)
    vector_own = lax.dynamic_slice_in_dim(small[:6], lax.axis_index("dp") * depth, depth, axis=1)
    joined = jnp.concatenate(ff_parts, axis=1)
    ups = [joined[:, 2 * i : 2 * i + TILE] for i in range(0, hidden_width, TILE)]
    downs = [joined[:, 2 * i + TILE : 2 * i + 2 * TILE] for i in range(0, hidden_width, TILE)]
    up_grad = jnp.concatenate(ups, axis=1)
    down_grad = jnp.concatenate(downs, axis=1).T
    scatter_attn.gots, others = pin((scatter_attn.gots, (output, clip_grad, up_grad, down_grad, small, vector_own)))
    output, clip_grad, up_grad, down_grad, small, vector_own = others
    q_grad, k_grad, v_grad, out_grad = scatter_attn.total(True, False, True)
    return (
        output,
        clip_grad,
        vector_own[0],
        vector_own[1],
        q_grad,
        small[7, :width],
        k_grad,
        v_grad,
        small[7, width : 2 * width],
        out_grad.T,
        vector_own[2],
        vector_own[3],
        vector_own[4],
        up_grad,
        small[6, :hidden_width],
        down_grad,
        vector_own[5],
    )


def solution(mesh):
    rows_spec = P("dp", "tensor", None)
    data, tensor = P("dp"), P("tensor")
    wide_spec, tall_spec = P("dp", "tensor"), P("tensor", "dp")
    placed = (
        rows_spec,
        data,
        data,
        data,
        wide_spec,
        tensor,
        wide_spec,
        wide_spec,
        tensor,
        tall_spec,
        data,
        data,
        data,
        wide_spec,
        tensor,
        tall_spec,
        data,
        rows_spec,
    )
    outs = (
        rows_spec,
        rows_spec,
        data,
        data,
        wide_spec,
        tensor,
        wide_spec,
        wide_spec,
        tensor,
        tall_spec,
        data,
        data,
        data,
        wide_spec,
        tensor,
        tall_spec,
        data,
    )
    return jax.shard_map(shards, mesh=mesh, in_specs=placed, out_specs=outs, check_vma=False)
```
